32 devices in a mesh: reg: 16 (over z, y, x), col: 2 (over core).
Axes of the slice: x: 2, y: 2, z: 4, core: 2. Of those that a mesh axis runs over, the one named last changes fastest.
Arguments:
- innovation: float32 [64, 131072], P(None, ('reg', 'col')), may hold values from -6 to 6
- obs_along: float32 [131072], P(('reg', 'col')), may hold values from 0 to 2
- obs_across: float32 [131072], P(('reg', 'col')), may hold values from 0 to 32
- obs_scale: float32 [131072], P(('reg', 'col')), may hold values from 0.5 to 2
- obs_error: float32 [131072], P(('reg', 'col')), may hold values from 0.1 to 1
- obs_gain: float32 [131072], P(('reg', 'col')), may hold values from 0.3 to 3
- pair_live: int32 [128, 2], P(('reg', 'col')), may hold values 0 or 1
- obs_count: int32 [128], P(('reg', 'col')), may hold values from 256 to 1024, as said below
- col_owner: int32 [131072], P(('reg', 'col')), may hold values from 0 to 32767, as said below
Outputs:
- weights: float32 [64, 131072], P(None, ('reg', 'col'))
- increments: float32 [64, 32768], P(None, ('reg', 'col'))
The draws below stay inside these ranges and needn't reach their ends.
Inputs may be any that keep to these rules, and one draw needn't show every extreme that they name: `obs_count`: slots of a region block at or after its count are empty. Some region holds 1024 observations and some holds 256. `col_owner`: observation slot o lies in device block k = o // 4096, and its column is one of k * 1024 to k * 1024 + 2 * 1024 - 1, taken modulo 32768; column block k belongs to the same position k in the order of devices.
All inputs are finite; a program needn't handle non-finite values. No bound on the sum of `pair_live` on one device may be relied on, other than what follows from the above.
Results may differ from the reference program's by a relative error of at most 0.0003.
Values sent between devices are 32-bit elements; how exact they have to be, the bound alone decides.
A program may use at most 64 MiB of HBM per device.

```python
import math
import jax
import jax.numpy as jnp
from jax import lax

ENS = 64
ROWS = 1024
REACH = 2
ITERS = 2
REG_DEV = 4
COLS_DEV = 1024
NREG = 128
NOBS = 131072
NCOL = 32768


def draw_obs_count(key, part):
    counts = jax.random.randint(jax.random.fold_in(key, 11), (NREG,), ROWS // 4, ROWS + 1)
    full_region = jax.random.randint(jax.random.fold_in(key, 12), (), 0, NREG)
    shift_draw = jax.random.randint(jax.random.fold_in(key, 13), (), 1, NREG)
    least_region = (full_region + shift_draw) % NREG
    region_ids = jnp.arange(NREG, dtype=jnp.int32)
    counts = jnp.where(region_ids == full_region, ROWS, counts)
    counts = jnp.where(region_ids == least_region, ROWS // 4, counts)
    return counts.astype(jnp.int32)


def draw_col_owner(key, part):
    owner_block = jnp.arange(NOBS, dtype=jnp.int32) // (REG_DEV * ROWS)
    offset_draw = jax.random.randint(jax.random.fold_in(key, 21), (NOBS,), 0, 2 * COLS_DEV)
    return ((owner_block * COLS_DEV + offset_draw) % NCOL).astype(jnp.int32)


def set_ends(values, rng, smallest, largest):
    place = [jax.random.randint(jax.random.fold_in(rng, axis), (), 0, length) for axis, length in enumerate(values.shape)]
    main_axis = values.shape.index(max(values.shape))
    neighbour = place[:main_axis] + [(place[main_axis] + 1) % values.shape[main_axis]] + place[main_axis + 1:]
    return values.at[tuple(place)].set(smallest).at[tuple(neighbour)].set(largest)


def shard_levels(rng, shape, shards, least, top_value):
    factor_of = 1.0
    for dim, blocks in shards:
        heights = jax.random.uniform(jax.random.fold_in(jax.random.fold_in(rng, 6), dim), (blocks,), jnp.float32, least / len(shards), top_value / len(shards))
        factor_of = factor_of * jnp.repeat(jnp.exp(heights), shape[dim] // blocks).reshape((-1,) + (1,) * (len(shape) - 1 - dim))
    return factor_of


def gaussian(rng, dims, scale, bound, shards=(), held_as=jnp.bfloat16):
    result = scale * jax.random.normal(rng, dims, jnp.float32)
    if shards:
        result = result * shard_levels(rng, dims, shards, -0.22, 0.18)
    return jnp.clip(result, -bound, bound).astype(held_as)


def setup_inputs(seed: int = 0) -> dict:
    streams_of = jax.random.split(jax.random.key(seed), 10)
    return {
        "innovation": gaussian(streams_of[0], (ENS, NOBS), 1.0, 6.0, ((1, 32),), jnp.float32),
        "obs_along": jnp.clip(2.0 * jax.random.uniform(streams_of[1], (NOBS,), jnp.float32) ** shard_levels(streams_of[1], (NOBS,), ((0, 32),), -0.2, 0.2), 0.0, 2.0),
        "obs_across": jnp.clip(32.0 * jax.random.uniform(streams_of[2], (NOBS,), jnp.float32) ** shard_levels(streams_of[2], (NOBS,), ((0, 32),), -0.2, 0.2), 0.0, 32.0),
        "obs_scale": jnp.clip(jnp.exp(math.log(2.0) - 1.3862944 * jax.random.uniform(streams_of[3], (NOBS,), jnp.float32) ** shard_levels(streams_of[3], (NOBS,), ((0, 32),), -0.2, 0.2)), 0.5, 2.0),
        "obs_error": jnp.clip(jnp.exp(math.log(1.0) - 2.3025851 * jax.random.uniform(streams_of[4], (NOBS,), jnp.float32) ** shard_levels(streams_of[4], (NOBS,), ((0, 32),), -0.2, 0.2)), 0.1, 1.0),
        "obs_gain": jnp.clip(jnp.exp(math.log(3.0) - 2.3025851 * jax.random.uniform(streams_of[5], (NOBS,), jnp.float32) ** shard_levels(streams_of[5], (NOBS,), ((0, 32),), -0.2, 0.2)), 0.3, 3.0),
        "pair_live": set_ends((jax.random.randint(streams_of[6], (NREG, REACH), 0, 4) < 3).astype(jnp.int32), jax.random.fold_in(streams_of[6], 1), 0, 1),
        "obs_count": draw_obs_count(jax.random.fold_in(streams_of[9], 71), 0),
        "col_owner": draw_col_owner(jax.random.fold_in(streams_of[9], 71), 0),
    }


support_radius = 1.0
norm_scale = 16.0
highest = lax.Precision.HIGHEST

def support_shape(row_along, row_across, col_along, col_across, offset):
    delta_along = offset + col_along[None, :] - row_along[:, None]
    delta_across = col_across[None, :] - row_across[:, None]
    scaled_dist = jnp.minimum(jnp.sqrt(delta_along * delta_along + delta_across * delta_across) / support_radius, 1.0)
    return (1.0 - scaled_dist) ** 4 * (4.0 * scaled_dist + 1.0)

def cov_block(row_meta, col_meta, offset, factor):
    shape_part = support_shape(row_meta[0], row_meta[1], col_meta[0], col_meta[1], offset)
    return row_meta[2][:, None] * col_meta[2][None, :] * (shape_part * (factor / norm_scale))

def gram_matrix(lhs_rows, rhs_rows):
    return lax.dot_general(lhs_rows.astype(jnp.float32), rhs_rows.astype(jnp.float32), (((1,), (1,)), ((), ())), precision=highest, preferred_element_type=jnp.float32)

def combine_rows(coefficients, blocks):
    return lax.dot_general(coefficients.astype(jnp.float32), blocks.astype(jnp.float32), (((0,), (0,)), ((), ())), precision=highest, preferred_element_type=jnp.float32)

def symmetric(matrix):
    return 0.5 * (matrix + matrix.T)

def spd_solve(matrix, right_side):
    lower_factor = jnp.linalg.cholesky(matrix)
    return jax.scipy.linalg.cho_solve((lower_factor, True), right_side)

def operate(vectors, obs_along, obs_across, weight, factors, obs_error):
    blocks = vectors.reshape(ENS, NREG, ROWS)
    along_blocks = obs_along.reshape(NREG, ROWS)
    across_blocks = obs_across.reshape(NREG, ROWS)
    weight_blocks = weight.reshape(NREG, ROWS)
    summed = (obs_error[None, :] * vectors).reshape(ENS, NREG, ROWS)
    for offset in range(REACH + 1):

        def one_pair(region, offset=offset):
            partner = (region + offset) % NREG
            row_meta = (along_blocks[region], across_blocks[region], weight_blocks[region])
            col_meta = (along_blocks[partner], across_blocks[partner], weight_blocks[partner])
            factor = 1.0 if offset == 0 else factors[region, offset - 1]
            cov_tile = cov_block(row_meta, col_meta, offset, factor)
            to_self = gram_matrix(blocks[:, partner], cov_tile)
            if offset == 0:
                return (to_self, to_self)
            to_partner = jnp.dot(blocks[:, region].astype(jnp.float32), cov_tile.astype(jnp.float32), precision=highest, preferred_element_type=jnp.float32)
            return (to_self, to_partner)
        to_self, to_partner = lax.map(one_pair, jnp.arange(NREG, dtype=jnp.int32))
        summed = summed + jnp.transpose(to_self, (1, 0, 2))
        if offset > 0:
            summed = summed + jnp.transpose(jnp.roll(to_partner, offset, axis=0), (1, 0, 2))
    return summed.reshape(ENS, NOBS)

def reference(innovation, obs_along, obs_across, obs_scale, obs_error, obs_gain, pair_live, obs_count, col_owner):
    live_mask = (jnp.arange(ROWS, dtype=jnp.int32)[None, :] < obs_count[:, None]).astype(jnp.float32).reshape(NOBS)
    weight = obs_scale * live_mask
    factors = pair_live.astype(jnp.float32)
    residual = innovation * live_mask[None, :]
    solution = jnp.zeros_like(residual)
    direction = residual
    norm_now = symmetric(gram_matrix(residual, residual))
    for iteration in range(ITERS):
        images = operate(direction, obs_along, obs_across, weight, factors, obs_error)
        curvature = symmetric(gram_matrix(direction, images))
        step_size = spd_solve(curvature, norm_now)
        solution = solution + combine_rows(step_size, direction)
        residual = residual - combine_rows(step_size, images)
        if iteration + 1 < ITERS:
            norm_next = symmetric(gram_matrix(residual, residual))
            conjugate = spd_solve(norm_now, norm_next)
            direction = residual + combine_rows(conjugate, direction)
            norm_now = norm_next
    scaled = solution * obs_gain[None, :]
    increments = jax.ops.segment_sum(scaled.T, col_owner, num_segments=NCOL).T
    return (solution, increments)
```

```python
import functools

import jax
import jax.numpy as jnp
from jax import lax
from jax.experimental import pallas as pl
from jax.experimental.pallas import tpu as pltpu
from jax.sharding import PartitionSpec as P

ROWS = 1024
REACH = 2
COLS_DEV = 1024
META = 16
TILE = 32
STEP = 16
PAIR = 4
EMPTY = ROWS // STEP
DEAD = 1e9
FAR = 1e6
VMEM_LIMIT = 60 * 1024 * 1024

highest = lax.Precision.HIGHEST
f32 = jnp.float32
bf16 = jnp.bfloat16
NT = (((1,), (1,)), ((), ()))
NN = (((1,), (0,)), ((), ()))
TN = (((0,), (0,)), ((), ()))
vmem = pl.BlockSpec(memory_space=pltpu.VMEM)
smem = pl.BlockSpec(memory_space=pltpu.SMEM)


def shift(block, distance):
    axis = ("reg", "col")
    n = lax.axis_size(axis)
    return lax.ppermute(block, axis, [((i - distance) % n, i) for i in range(n)])


def dot(a, b, dims=NN):
    return lax.dot_general(a, b, dims, preferred_element_type=f32)


def two(x):
    hi = x.astype(bf16)
    return hi, (x - hi.astype(f32)).astype(bf16)


def three(x):
    hi = x.astype(bf16)
    rest = x - hi.astype(f32)
    mid = rest.astype(bf16)
    return hi, mid, (rest - mid.astype(f32)).astype(bf16)


def combine(coef_t, blocks):
    chi, clo = two(coef_t)
    bhi, blo = two(blocks)
    return dot(
        jnp.concatenate([chi, chi, clo], axis=1), jnp.concatenate([bhi, blo, bhi], axis=0)
    )


def params():
    return pltpu.CompilerParams(vmem_limit_bytes=VMEM_LIMIT)


def sort_kernel(innov_ref, meta_ref, first_ref, last_ref, rank_ref):
    regions = innov_ref.shape[1] // ROWS
    kept = first_ref.shape[0]
    sub = lax.broadcasted_iota(jnp.int32, (ROWS, 128), 0)
    lane = lax.broadcasted_iota(jnp.int32, (ROWS, 128), 1)
    for g in range(regions):
        cols = pl.ds(g * ROWS, ROWS)
        meta = meta_ref[:, cols]
        key = meta[6:7]
        live = (key < 0.5 * DEAD).astype(f32)
        key_col = jnp.broadcast_to(key, (128, ROWS)).T
        ranks = []
        for b in range(ROWS // 128):
            mine = key[:, b * 128 : (b + 1) * 128]
            before = (key_col < mine) | ((key_col == mine) & (sub < lane + b * 128))
            ranks.append(jnp.sum(before.astype(f32), axis=0, keepdims=True))
        rank = jnp.concatenate(ranks, axis=1)
        rank_ref[:, cols] = jnp.broadcast_to(rank, (8, ROWS))
        stack = jnp.concatenate([innov_ref[:, cols] * live, meta], axis=0)
        lhs = jnp.concatenate(three(stack), axis=0)
        n = stack.shape[0]
        rank_i = rank.astype(jnp.int32)
        out_ref = first_ref if g < regions // 2 else last_ref
        for c in range(ROWS // 256):
            slot = lax.broadcasted_iota(jnp.int32, (256, ROWS), 0) + c * 256
            place = (slot == rank_i).astype(f32).astype(bf16)
            got = dot(lhs, place, NT)
            start = (g % (regions // 2)) * ROWS + c * 256
            got = (got[:n] + got[n : 2 * n] + got[2 * n :])[:kept]
            out_ref[:, start : start + 256] = got


def sort_call(innov, meta):
    ens, n = innov.shape
    half = jax.ShapeDtypeStruct((ens + 8, n // 2), f32)
    return pl.pallas_call(
        sort_kernel,
        out_shape=(half, half, jax.ShapeDtypeStruct((8, n), f32)),
        in_specs=[vmem, vmem],
        out_specs=(vmem,) * 3,
        compiler_params=params(),
        name="sort_slots",
    )(innov, meta)


def lay_grid(chunks, row_ref, grid_ref):
    width = chunks[0].shape[1]
    per = width // ROWS
    blocks = ROWS // 128
    grid_ref[...] = jnp.full(grid_ref.shape, FAR, f32)
    for c, ref in enumerate(chunks):
        row_ref[:, c * width : (c + 1) * width] = ref[ref.shape[0] - 8 :, :]
        for r in range(per):
            h = c * per + r
            at = slice(h * ROWS, (h + 1) * ROWS)
            row_ref[0:1, at] = row_ref[0:1, at] + float(h)
            for q, source in enumerate((0, 1, 6)):
                for b in range(blocks):
                    line = h * (blocks + 1) + b
                    begin = h * ROWS + b * 128
                    grid_ref[q, line : line + 1, :] = row_ref[source : source + 1, begin : begin + 128]


def lay_tables(grid_ref, table_refs, spread_refs):
    own = spread_refs[0].shape[0]
    blocks = ROWS // 128
    count = (own // ROWS + 2 * REACH) * (blocks + 1)
    ways = 128 // STEP
    lane = lax.broadcasted_iota(jnp.int32, (count, 128), 1)
    for q in range(2):
        here = grid_ref[q, :count, :]
        later = grid_ref[q, 1 : count + 1, :]
        table_refs[q][pl.ds(0, count, stride=ways), :] = here
        for k in range(1, ways):
            joined = jnp.where(lane < k * STEP, later, here)
            table_refs[q][pl.ds(k, count, stride=ways), :] = pltpu.roll(joined, 128 - k * STEP, 1)
        turned = jnp.concatenate([here, jnp.zeros((128 - count, 128), f32)], axis=0).T
        for g in range(own // ROWS):
            for b in range(blocks):
                line = (g + REACH) * (blocks + 1) + b
                begin = g * ROWS + b * 128
                spread_refs[q][begin : begin + 128, :] = jnp.broadcast_to(
                    turned[:, line : line + 1], (128, 128)
                )


def plan_windows(row_ref, grid_ref, span_ref, item_ref):
    blocks = ROWS // 128
    regions = row_ref.shape[1] // ROWS - 2 * REACH
    per = ROWS // TILE
    tiles = regions * per
    ways = 128 // STEP
    offsets = 2 * REACH + 1
    keys = [
        grid_ref[2, h * (blocks + 1) : h * (blocks + 1) + blocks, :] for h in range(regions + 2 * REACH)
    ]
    mine = jnp.concatenate(keys[REACH : REACH + regions], axis=0)
    top = jnp.where(mine < 0.5 * DEAD, mine, -DEAD)
    size = 1
    while size < TILE:
        top = jnp.maximum(top, pltpu.roll(top, 128 - size, 1))
        size *= 2
    parts = 128 // TILE
    lines = regions * blocks
    tile = lax.broadcasted_iota(jnp.int32, (lines, tiles), 1)
    line = lax.broadcasted_iota(jnp.int32, (lines, tiles), 0)
    first = jnp.zeros((1, tiles), f32)
    last = jnp.zeros((1, tiles), f32)
    for p in range(parts):
        here = tile == line * parts + p
        lane = slice(p * TILE, p * TILE + 1)
        first = first + jnp.sum(
            jnp.where(here, jnp.broadcast_to(mine[:, lane], (lines, tiles)), 0.0), axis=0, keepdims=True
        )
        last = last + jnp.sum(
            jnp.where(here, jnp.broadcast_to(top[:, lane], (lines, tiles)), 0.0), axis=0, keepdims=True
        )
    under, over = first - 1.001, last + 1.001
    begins, ends = [], []
    for key in keys:
        begin = jnp.zeros((blocks, tiles), f32)
        end = jnp.zeros((blocks, tiles), f32)
        for k in range(ways):
            low = jnp.broadcast_to(key[:, k * STEP : k * STEP + 1], (blocks, tiles))
            high = jnp.broadcast_to(key[:, (k + 1) * STEP - 1 : (k + 1) * STEP], (blocks, tiles))
            begin = begin + jnp.where(high < under, 1.0, 0.0)
            end = end + jnp.where(low <= over, 1.0, 0.0)
        begins.append(jnp.sum(begin, axis=0, keepdims=True))
        ends.append(jnp.sum(end, axis=0, keepdims=True))
    group = lax.broadcasted_iota(jnp.int32, (1, tiles), 1) // per
    alive = first < 0.5 * DEAD
    starts, stops = [], []
    needs = jnp.zeros((1, tiles), f32)
    for dh in range(offsets):
        d = dh - REACH
        start = jnp.zeros((1, tiles), f32)
        stop = jnp.zeros((1, tiles), f32)
        for g in range(regions):
            h = g + dh
            base = float(h * (ROWS + 128) // STEP)
            begin, end = begins[h] + base, ends[h] + base
            if d:
                source = 3 + abs(d)
                owner = (g + REACH if d > 0 else h) * ROWS
                flag = row_ref[source : source + 1, owner : owner + 128]
                end = jnp.where(flag[:, :tiles] > 0.5, end, begin)
            start = jnp.where(group == g, begin, start)
            stop = jnp.where(group == g, end, stop)
        stop = jnp.where(alive, jnp.maximum(stop, start), start)
        needs = jnp.maximum(needs, jnp.floor((stop - start + (ways - 1.0)) * (1.0 / ways)))
        starts.append(start)
        stops.append(stop)
    blank = jnp.full((8 - offsets, tiles), float(EMPTY), f32)
    for m in range(blocks + 1):
        lines_m = [
            jnp.where(start + float(ways * m) < stop, start + float(ways * m), float(EMPTY))
            for start, stop in zip(starts, stops)
        ]
        span_ref[8 * m : 8 * m + 8, :] = jnp.concatenate(lines_m + [blank], axis=0).astype(jnp.int32)
    row = lax.broadcasted_iota(jnp.int32, (tiles, tiles), 0)
    col = lax.broadcasted_iota(jnp.int32, (tiles, tiles), 1)
    many = jnp.broadcast_to(needs, (tiles, tiles)).astype(bf16)
    done = dot((col <= row).astype(f32).astype(bf16), many, NT)
    each = dot((col == row).astype(f32).astype(bf16), many, NT)
    total = jnp.max(done, axis=0, keepdims=True)
    for k in range(item_ref.shape[1]):
        slot = lax.broadcasted_iota(jnp.int32, (1, tiles), 1).astype(f32) + float(k * tiles)
        past = done <= slot
        at = jnp.sum(jnp.where(past, 1.0, 0.0), axis=0, keepdims=True)
        began = jnp.sum(jnp.where(past, each, 0.0), axis=0, keepdims=True)
        spare = slot >= total
        item_ref[0, k : k + 1, :] = jnp.where(spare, 0.0, at).astype(jnp.int32)
        item_ref[1, k : k + 1, :] = jnp.where(spare, float(blocks), slot - began).astype(jnp.int32)
        item_ref[2, k : k + 1, :] = total.astype(jnp.int32)


def turn_vectors(v_ref, row_ref, turn_ref):
    ens, wide = v_ref.shape
    padded = ROWS + 128
    row = lax.broadcasted_iota(jnp.int32, (256, 256), 0)
    eye = (row == lax.broadcasted_iota(jnp.int32, (256, 256), 1)).astype(f32).astype(bf16)
    for h in range(wide // ROWS):
        for b in range(ROWS // 256):
            at = slice(h * ROWS + b * 256, h * ROWS + (b + 1) * 256)
            stack = jnp.concatenate(two(v_ref[:, at] * row_ref[2:3, at]), axis=0)
            begin = h * padded + b * 256
            turn_ref[begin : begin + 256, :] = dot(eye, stack, NT).astype(bf16)
        turn_ref[h * padded + ROWS : (h + 1) * padded, :] = jnp.zeros((128, 2 * ens), bf16)


def apply_cov(
    span_ref, item_ref, row_ref, table_refs, spread_refs, v_ref, img_ref, turn_ref, sum_ref, s_ref
):
    ens, wide = v_ref.shape
    own = img_ref.shape[1]
    lead = REACH * ROWS
    s_ref[...] = jnp.zeros_like(s_ref)
    sum_ref[...] = jnp.zeros_like(sum_ref)

    def windows(n):
        line, lane = lax.shift_right_logical(n, jnp.int32(7)), lax.bitwise_and(n, jnp.int32(127))
        tile = item_ref[0, line, lane]
        level = item_ref[1, line, lane] * 8
        return [tile] + [span_ref[level + dh, tile] for dh in range(2 * REACH + 1)]

    def step(k, carry):
        for p in range(PAIR):
            tile, *found = carry[p]
            rhs = jnp.concatenate(
                [turn_ref[pl.ds(pl.multiple_of(w * STEP, STEP), 128), :] for w in found], axis=0
            )
            got = dot(s_ref[p], rhs)
            at = pl.ds(pl.multiple_of(tile * TILE, TILE), TILE)
            sum_ref[at, :] += got[:TILE] + got[TILE:]
        now = [windows(k * PAIR + p) for p in range(PAIR)]
        for p in range(PAIR):
            tile, *found = now[p]
            at = pl.ds(pl.multiple_of(tile * TILE, TILE), TILE)
            a_i = spread_refs[0][at, :]
            b_i = spread_refs[1][at, :]
            for d, w in enumerate(found):
                da = table_refs[0][pl.ds(w, 1), :] - a_i
                db = table_refs[1][pl.ds(w, 1), :] - b_i
                r2 = da * da + db * db
                r = r2 * lax.rsqrt(jnp.maximum(r2, 1e-30))
                u = jnp.maximum(1.0 - r, 0.0)
                u2 = u * u
                hi, lo = two((u2 * u2) * (r + 0.25))
                s_ref[p, 0:TILE, d * 128 : (d + 1) * 128] = hi
                s_ref[p, TILE : 2 * TILE, d * 128 : (d + 1) * 128] = lo
        return now

    trips = lax.shift_right_logical(item_ref[2, 0, 0] + (PAIR - 1), jnp.int32(PAIR.bit_length() - 1))
    lax.fori_loop(0, trips + 1, step, [windows(p) for p in range(PAIR)])
    for c in range(own // 128):
        at = slice(c * 128, (c + 1) * 128)
        e_at = slice(lead + c * 128, lead + (c + 1) * 128)
        turned = sum_ref[at, :].T
        img_ref[:, at] = (
            (turned[:ens] + turned[ens:]) * (row_ref[2:3, e_at] * 0.25) + row_ref[3:4, e_at] * v_ref[:, e_at]
        )


def gram(a, b):
    ahi, alo = two(a)
    bhi, blo = two(b)
    return dot(
        jnp.concatenate([ahi, ahi, alo], axis=1), jnp.concatenate([bhi, blo, bhi], axis=1), NT
    )


def first_kernel(
    c0,
    c1,
    c2,
    c3,
    imga_ref,
    imgb_ref,
    gram_ref,
    span_out,
    item_out,
    span_ref,
    item_ref,
    plan_sem,
    row_ref,
    grid_ref,
    along_ref,
    across_ref,
    along_i_ref,
    across_i_ref,
    v_ref,
    img_ref,
    turn_ref,
    sum_ref,
    s_ref,
):
    ens, own = img_ref.shape
    lead = REACH * ROWS
    chunks = [c0, c1, c2, c3]
    tables = (along_ref, across_ref)
    spreads = (along_i_ref, across_i_ref)
    lay_grid(chunks, row_ref, grid_ref)
    plan_windows(row_ref, grid_ref, span_out, item_out)
    span_copy = pltpu.make_async_copy(span_out, span_ref, plan_sem.at[0])
    item_copy = pltpu.make_async_copy(item_out, item_ref, plan_sem.at[1])
    span_copy.start()
    item_copy.start()
    lay_tables(grid_ref, tables, spreads)
    for c, ref in enumerate(chunks):
        v_ref[:, c * lead : (c + 1) * lead] = ref[:ens, :]
    turn_vectors(v_ref, row_ref, turn_ref)
    span_copy.wait()
    item_copy.wait()
    apply_cov(
        span_ref, item_ref, row_ref, tables, spreads, v_ref, img_ref, turn_ref, sum_ref, s_ref
    )
    imga_ref[...] = img_ref[:, :lead]
    imgb_ref[...] = img_ref[:, lead:]
    r = v_ref[:, lead : lead + own]
    gram_ref[...] = gram(r, jnp.concatenate([r, img_ref[...]], axis=0))


def second_kernel(
    span_in,
    item_in,
    step_ref,
    c0,
    c1,
    c2,
    c3,
    i0,
    i1,
    i2,
    i3,
    gram_ref,
    span_ref,
    item_ref,
    plan_sem,
    row_ref,
    grid_ref,
    along_ref,
    across_ref,
    along_i_ref,
    across_i_ref,
    v_ref,
    img_ref,
    turn_ref,
    sum_ref,
    s_ref,
):
    ens, own = img_ref.shape
    lead = REACH * ROWS
    chunks = [c0, c1, c2, c3]
    tables = (along_ref, across_ref)
    spreads = (along_i_ref, across_i_ref)
    span_copy = pltpu.make_async_copy(span_in, span_ref, plan_sem.at[0])
    item_copy = pltpu.make_async_copy(item_in, item_ref, plan_sem.at[1])
    span_copy.start()
    item_copy.start()
    lay_grid(chunks, row_ref, grid_ref)
    lay_tables(grid_ref, tables, spreads)
    step_t = step_ref[...].T
    for c, (ref, image) in enumerate(zip(chunks, [i0, i1, i2, i3])):
        v_ref[:, c * lead : (c + 1) * lead] = ref[:ens, :] - combine(step_t, image[...])
    turn_vectors(v_ref, row_ref, turn_ref)
    span_copy.wait()
    item_copy.wait()
    apply_cov(
        span_ref, item_ref, row_ref, tables, spreads, v_ref, img_ref, turn_ref, sum_ref, s_ref
    )
    r = v_ref[:, lead : lead + own]
    gram_ref[:ens] = gram(r, jnp.concatenate([r, img_ref[...]], axis=0))
    mixed = gram(r, jnp.concatenate([i1[...], i2[...]], axis=1))
    gram_ref[ens:] = jnp.concatenate([mixed, mixed], axis=1)


def plan_shapes(own):
    tiles = own // TILE
    most = tiles * (ROWS // 128)
    return (8 * (ROWS // 128 + 1), tiles), (3, most // 128 + 1, 128)


def scratch(ens, own):
    regions = own // ROWS + 2 * REACH
    wide = regions * ROWS
    lines = -(-(regions * (ROWS // 128 + 1) + 1) // 8) * 8
    table = pltpu.VMEM((128 // STEP * lines, 128), f32)
    spread = pltpu.VMEM((own, 128), f32)
    spans, items = plan_shapes(own)
    return [
        pltpu.SMEM(spans, jnp.int32),
        pltpu.SMEM(items, jnp.int32),
        pltpu.SemaphoreType.DMA((2,)),
        pltpu.VMEM((8, wide), f32),
        pltpu.VMEM((3, lines, 128), f32),
        table,
        table,
        spread,
        spread,
        pltpu.VMEM((ens, wide), f32),
        pltpu.VMEM((ens, own), f32),
        pltpu.VMEM((regions * (ROWS + 128) + 128, 2 * ens), bf16),
        pltpu.VMEM((own, 128), f32),
        pltpu.VMEM((PAIR, 2 * TILE, (2 * REACH + 1) * 128), bf16),
    ]


def first_call(chunks, ens, own):
    half = jax.ShapeDtypeStruct((ens, own // 2), f32)
    spans, items = plan_shapes(own)
    return pl.pallas_call(
        first_kernel,
        out_shape=(
            half,
            half,
            jax.ShapeDtypeStruct((ens, 2 * ens), f32),
            jax.ShapeDtypeStruct(spans, jnp.int32),
            jax.ShapeDtypeStruct(items, jnp.int32),
        ),
        in_specs=[vmem] * 4,
        out_specs=(vmem,) * 5,
        scratch_shapes=scratch(ens, own),
        compiler_params=params(),
        name="operate_first",
    )(*chunks)


def second_call(plan, step, chunks, images, ens, own):
    return pl.pallas_call(
        second_kernel,
        out_shape=jax.ShapeDtypeStruct((2 * ens, 2 * ens), f32),
        in_specs=[vmem] * 11,
        out_specs=vmem,
        scratch_shapes=scratch(ens, own),
        compiler_params=params(),
        name="operate_second",
    )(*plan, step, *chunks, *images)


def flip(me, size):
    return size * (1 - 2 * ((me // size) % 2))


def exchange_steps(total):
    bits = total.bit_length() - 1
    steps = [[1]] if bits % 2 else []
    for k in range(bits % 2, bits, 2):
        steps.append([2**k, 2 ** (k + 1)])
    return steps


def reduce_kernel(steps, n_col, x_ref, out_ref, send, recv, send_sem, recv_sem):
    me = lax.axis_index("reg") * n_col + lax.axis_index("col")
    partners = []
    for sizes in steps:
        others = [me + flip(me, size) for size in sizes]
        if len(sizes) == 2:
            others.append(others[0] + flip(me, sizes[1]))
        partners.append([(other // n_col, other % n_col) for other in others])
    barrier = pltpu.get_barrier_semaphore()
    for group in partners:
        for other in group:
            pl.semaphore_signal(
                barrier, inc=1, device_id=other, device_id_type=pl.DeviceIdType.MESH
            )
    pl.semaphore_wait(barrier, sum(len(group) for group in partners))
    total = x_ref[...]
    slot = 0
    for k, group in enumerate(partners):
        if k:
            send[k] = total
        copies = []
        for p, other in enumerate(group):
            copies.append(
                pltpu.make_async_remote_copy(
                    src_ref=send.at[k] if k else x_ref,
                    dst_ref=recv.at[slot + p],
                    send_sem=send_sem.at[slot + p],
                    recv_sem=recv_sem.at[slot + p],
                    device_id=other,
                    device_id_type=pl.DeviceIdType.MESH,
                )
            )
        for copy in copies:
            copy.start()
        for copy in copies:
            copy.wait()
        total = total + recv[slot]
        if len(group) == 3:
            total = total + (recv[slot + 1] + recv[slot + 2])
        slot += len(group)
    out_ref[...] = total


def sum_all(x, which):
    n_col = lax.axis_size("col")
    steps = exchange_steps(lax.axis_size("reg") * n_col)
    slots = sum(2 ** len(sizes) - 1 for sizes in steps)
    return pl.pallas_call(
        functools.partial(reduce_kernel, steps, n_col),
        out_shape=jax.ShapeDtypeStruct(x.shape, f32),
        in_specs=[vmem],
        out_specs=vmem,
        scratch_shapes=[
            pltpu.VMEM((len(steps),) + x.shape, f32),
            pltpu.VMEM((slots,) + x.shape, f32),
            pltpu.SemaphoreType.DMA((slots,)),
            pltpu.SemaphoreType.DMA((slots,)),
        ],
        compiler_params=pltpu.CompilerParams(collective_id=which, has_side_effects=True),
        name="sum_all",
    )(x)


def symmetric(matrix):
    return 0.5 * (matrix + matrix.T)


def mm(a, b, dims=NN):
    return lax.dot_general(a, b, dims, precision=highest, preferred_element_type=f32)


def eliminate(chains):
    ens, both = chains[0].shape
    rows = lax.broadcasted_iota(jnp.int32, (ens, both), 0)
    for k in range(ens):
        done = []
        for m in chains:
            col = jnp.broadcast_to(m[:, k : k + 1], (ens, both))
            pivot = m[k : k + 1] / col[k : k + 1]
            done.append(jnp.where(rows == k, pivot, m - col * pivot))
        chains = done
    return [m[:, ens:] for m in chains]


def solve_first_kernel(gram_ref, step_ref, inv_ref, curv_ref):
    ens = gram_ref.shape[0]
    norm = symmetric(gram_ref[:, :ens])
    curv = symmetric(gram_ref[:, ens:])
    rows = lax.broadcasted_iota(jnp.int32, (ens, ens), 0)
    eye = (rows == lax.broadcasted_iota(jnp.int32, (ens, ens), 1)).astype(f32)
    step, inv = eliminate(
        [jnp.concatenate([curv, norm], axis=1), jnp.concatenate([norm, eye], axis=1)]
    )
    step_ref[...] = step
    inv_ref[...] = inv
    curv_ref[...] = curv


def solve_second_kernel(gram_ref, step_ref, inv_ref, curv_ref, coef_ref):
    ens = step_ref.shape[0]
    norm = symmetric(gram_ref[:ens, :ens])
    cross = gram_ref[:ens, ens:]
    mixed = gram_ref[ens:, :ens]
    conj = mm(inv_ref[...], norm)
    coupled = mm(mixed, conj)
    quad = mm(conj, mm(curv_ref[...], conj), TN)
    curv = symmetric(cross + coupled + coupled.T + quad)
    (step,) = eliminate([jnp.concatenate([curv, norm], axis=1)])
    step0 = step_ref[...]
    keep = step0 + step + mm(conj, step)
    coef_ref[...] = jnp.concatenate([keep.T, -mm(step0, step).T], axis=1)


def solve_first(grams):
    ens = grams.shape[0]
    small = jax.ShapeDtypeStruct((ens, ens), f32)
    return pl.pallas_call(
        solve_first_kernel,
        out_shape=(small, small, small),
        in_specs=[vmem],
        out_specs=(vmem, vmem, vmem),
        name="solve_first",
    )(grams)


def solve_second(grams, step0, inv0, curv0):
    ens = step0.shape[0]
    return pl.pallas_call(
        solve_second_kernel,
        out_shape=jax.ShapeDtypeStruct((ens, 2 * ens), f32),
        in_specs=[vmem] * 4,
        out_specs=vmem,
        name="solve_second",
    )(grams, step0, inv0, curv0)


def add_columns(stack, owner, cols_ref):
    ens = cols_ref.shape[0]
    for c in range(2 * COLS_DEV // 256):
        slot = lax.broadcasted_iota(jnp.int32, (256, ROWS), 0) + c * 256
        hot = (slot == owner).astype(f32).astype(bf16)
        got = dot(stack, hot, NT)
        part = slice(c * 256, (c + 1) * 256)
        cols_ref[:, part] += got[:ens] + got[ens:]


def innov_columns_kernel(innov_ref, info_ref, cols_ref):
    cols_ref[...] = jnp.zeros_like(cols_ref)

    def one(g, carry):
        at = pl.ds(pl.multiple_of(g * ROWS, ROWS), ROWS)
        scale = info_ref[0:1, at] * info_ref[1:2, at]
        owner = info_ref[2:3, at].astype(jnp.int32)
        add_columns(jnp.concatenate(two(innov_ref[:, at] * scale), axis=0), owner, cols_ref)
        return carry

    lax.fori_loop(0, innov_ref.shape[1] // ROWS, one, 0)


def columns_kernel(info_ref, rank_ref, imga_ref, imgb_ref, back_ref, cols_ref):
    ens, own = back_ref.shape
    half = own // 2
    cols_ref[...] = jnp.zeros_like(cols_ref)
    for g in range(own // ROWS):
        at = slice(g * ROWS, (g + 1) * ROWS)
        rank = rank_ref[0:1, at].astype(jnp.int32)
        img_ref = imga_ref if g * ROWS < half else imgb_ref
        begin = (g * ROWS) % half
        lhs = jnp.concatenate(two(img_ref[:, begin : begin + ROWS]), axis=0)
        total = jnp.zeros((2 * ens, ROWS), f32)
        for c in range(ROWS // 256):
            slot = lax.broadcasted_iota(jnp.int32, (256, ROWS), 0) + c * 256
            place = (slot == rank).astype(f32).astype(bf16)
            total = total + dot(lhs[:, c * 256 : (c + 1) * 256], place)
        image = total[:ens] + total[ens:]
        back_ref[:, at] = image
        owner = info_ref[2:3, at].astype(jnp.int32)
        add_columns(jnp.concatenate(two(image * info_ref[0:1, at]), axis=0), owner, cols_ref)


def innov_columns_call(innov, info):
    ens, own = innov.shape
    return pl.pallas_call(
        innov_columns_kernel,
        out_shape=jax.ShapeDtypeStruct((ens, 2 * COLS_DEV), f32),
        in_specs=[vmem] * 2,
        out_specs=vmem,
        compiler_params=params(),
        cost_estimate=pl.CostEstimate(
            flops=2 * 256 * own * 2048, bytes_accessed=4 << 20, transcendentals=0
        ),
        name="innov_columns",
    )(innov, info)


def columns_call(info, rank, imga, imgb):
    ens, half = imga.shape
    return pl.pallas_call(
        columns_kernel,
        out_shape=(
            jax.ShapeDtypeStruct((ens, 2 * half), f32),
            jax.ShapeDtypeStruct((ens, 2 * COLS_DEV), f32),
        ),
        in_specs=[vmem] * 4,
        out_specs=(vmem, vmem),
        compiler_params=params(),
        cost_estimate=pl.CostEstimate(
            flops=2 * 256 * 2 * half * 3072, bytes_accessed=4 << 20, transcendentals=0
        ),
        name="columns",
    )(info, rank, imga, imgb)


def final_kernel(coef_ref, innov_ref, info_ref, back_ref, rc_ref, rin_ref, ic_ref, iin_ref, w_ref, inc_ref):
    coef = coef_ref[...]
    ens = coef.shape[0]
    own = innov_ref.shape[1]
    chunk = 1024
    first, second = coef[:, :ens], coef[:, ens:]
    for c in range(own // chunk):
        at = pl.ds(c * chunk, chunk)
        live = info_ref[1:2, at]
        w_ref[:, at] = combine(first, innov_ref[:, at] * live) + combine(second, back_ref[:, at])
    inc_ref[...] = combine(first, rc_ref[:, :COLS_DEV] + rin_ref[...]) + combine(
        second, ic_ref[:, :COLS_DEV] + iin_ref[...]
    )


def final_call(coef, innov, info, back, *cols):
    ens, own = innov.shape
    return pl.pallas_call(
        final_kernel,
        out_shape=(
            jax.ShapeDtypeStruct((ens, own), f32),
            jax.ShapeDtypeStruct((ens, COLS_DEV), f32),
        ),
        in_specs=[vmem] * 8,
        out_specs=(vmem, vmem),
        compiler_params=params(),
        name="final",
    )(coef, innov, info, back, *cols)


def on_device(
    innovation,
    obs_along,
    obs_across,
    obs_scale,
    obs_error,
    obs_gain,
    pair_live,
    obs_count,
    col_owner,
):
    axes = ("reg", "col")
    ens, own = innovation.shape
    live = (
        (jnp.arange(ROWS, dtype=jnp.int32)[None, :] < obs_count[:, None])
        .astype(f32)
        .reshape(own)
    )
    flags = jnp.repeat(pair_live.astype(f32).T, ROWS, axis=1)
    zero = jnp.zeros((own,), f32)
    meta = jnp.stack(
        [obs_along, obs_across, obs_scale * live, obs_error, flags[0], flags[1]]
        + [jnp.where(live > 0.5, obs_across, DEAD)]
        + [zero] * (META - 7)
    )
    total_cols = COLS_DEV * lax.axis_size(axes)
    local_col = (col_owner - lax.axis_index(axes) * COLS_DEV) % total_cols
    info = jnp.stack([obs_gain, live, local_col.astype(f32)] + [zero] * 5)

    first, last, rank = sort_call(innovation, meta)
    after = shift(first, -1)
    before = shift(last, 1)
    chunks = [before, first, last, after]
    innov_cols = innov_columns_call(innovation, info)
    innov_came = shift(innov_cols[:, COLS_DEV:], 1)
    imga, imgb, grams, *plan = first_call(chunks, ens, own)
    img_after = shift(imga, -1)
    img_before = shift(imgb, 1)
    step0, inv0, curv0 = solve_first(sum_all(grams, 0))
    back, img_cols = columns_call(info, rank, imga, imgb)
    img_came = shift(img_cols[:, COLS_DEV:], 1)
    grams = second_call(plan, step0, chunks, [img_before, imga, imgb, img_after], ens, own)
    coef = solve_second(sum_all(grams, 1), step0, inv0, curv0)
    return tuple(
        final_call(coef, innovation, info, back, innov_cols, innov_came, img_cols, img_came)
    )


def solution(mesh):
    one = P(("reg", "col"))
    in_specs = (P(None, ("reg", "col")), one, one, one, one, one, P(("reg", "col"), None), one, one)
    out_specs = (P(None, ("reg", "col")), P(None, ("reg", "col")))
    return jax.shard_map(
        on_device, mesh=mesh, in_specs=in_specs, out_specs=out_specs, check_vma=False
    )
```

```python
import functools

import jax
import jax.numpy as jnp
from jax import lax
from jax.experimental import pallas as pl
from jax.experimental.pallas import tpu as pltpu
from jax.sharding import PartitionSpec as P

ROWS = 1024
REACH = 2
COLS_DEV = 1024
META = 16
TILE = 32
STEP = 16
PAIR = 4
PANEL = 8
EMPTY = ROWS // STEP
DEAD = 1e9
FAR = 1e6
VMEM_LIMIT = 60 * 1024 * 1024

highest = lax.Precision.HIGHEST
f32 = jnp.float32
bf16 = jnp.bfloat16
NT = (((1,), (1,)), ((), ()))
NN = (((1,), (0,)), ((), ()))
TN = (((0,), (0,)), ((), ()))
vmem = pl.BlockSpec(memory_space=pltpu.VMEM)
smem = pl.BlockSpec(memory_space=pltpu.SMEM)


def shift(block, distance):
    axis = ("reg", "col")
    n = lax.axis_size(axis)
    return lax.ppermute(block, axis, [((i - distance) % n, i) for i in range(n)])


def dot(a, b, dims=NN):
    return lax.dot_general(a, b, dims, preferred_element_type=f32)


def two(x):
    hi = x.astype(bf16)
    return hi, (x - hi.astype(f32)).astype(bf16)


def three(x):
    hi = x.astype(bf16)
    rest = x - hi.astype(f32)
    mid = rest.astype(bf16)
    return hi, mid, (rest - mid.astype(f32)).astype(bf16)


def combine(coef_t, blocks):
    chi, clo = two(coef_t)
    bhi, blo = two(blocks)
    return dot(
        jnp.concatenate([chi, chi, clo], axis=1), jnp.concatenate([bhi, blo, bhi], axis=0)
    )


def params():
    return pltpu.CompilerParams(vmem_limit_bytes=VMEM_LIMIT)


def sort_kernel(innov_ref, meta_ref, first_ref, last_ref, rank_ref):
    regions = innov_ref.shape[1] // ROWS
    kept = first_ref.shape[0]
    sub = lax.broadcasted_iota(jnp.int32, (128, 128), 0)
    lane = lax.broadcasted_iota(jnp.int32, (128, 128), 1)
    for g in range(regions):
        cols = pl.ds(g * ROWS, ROWS)
        meta = meta_ref[:, cols]
        key = meta[6:7]
        live = (key < 0.5 * DEAD).astype(f32)
        key_col = jnp.broadcast_to(key, (128, ROWS)).T
        ranks = []
        for b in range(ROWS // 128):
            begin, end = b * 128, (b + 1) * 128
            mine = key[:, begin:end]
            other = key_col[begin:end]
            before = (other < mine) | ((other == mine) & (sub < lane))
            total = jnp.sum(jnp.where(before, 1.0, 0.0), axis=0, keepdims=True)
            if b:
                before = jnp.where(key_col[:begin] <= mine, 1.0, 0.0)
                total = total + jnp.sum(before, axis=0, keepdims=True)
            if end < ROWS:
                before = jnp.where(key_col[end:] < mine, 1.0, 0.0)
                total = total + jnp.sum(before, axis=0, keepdims=True)
            ranks.append(total)
        rank = jnp.concatenate(ranks, axis=1)
        rank_ref[:, cols] = jnp.broadcast_to(rank, (8, ROWS))
        stack = jnp.concatenate([innov_ref[:, cols] * live, meta], axis=0)
        lhs = jnp.concatenate(three(stack), axis=0)
        n = stack.shape[0]
        rank_i = rank.astype(jnp.int32)
        out_ref = first_ref if g < regions // 2 else last_ref
        for c in range(ROWS // 256):
            slot = lax.broadcasted_iota(jnp.int32, (256, ROWS), 0) + c * 256
            place = (slot == rank_i).astype(f32).astype(bf16)
            got = dot(lhs, place, NT)
            start = (g % (regions // 2)) * ROWS + c * 256
            got = (got[:n] + got[n : 2 * n] + got[2 * n :])[:kept]
            out_ref[:, start : start + 256] = got


def sort_call(innov, meta):
    ens, n = innov.shape
    half = jax.ShapeDtypeStruct((ens + 8, n // 2), f32)
    return pl.pallas_call(
        sort_kernel,
        out_shape=(half, half, jax.ShapeDtypeStruct((8, n), f32)),
        in_specs=[vmem, vmem],
        out_specs=(vmem,) * 3,
        compiler_params=params(),
        name="sort_slots",
    )(innov, meta)


def lay_grid(chunks, row_ref, grid_ref):
    width = chunks[0].shape[1]
    per = width // ROWS
    blocks = ROWS // 128
    grid_ref[...] = jnp.full(grid_ref.shape, FAR, f32)
    for c, ref in enumerate(chunks):
        row_ref[:, c * width : (c + 1) * width] = ref[ref.shape[0] - 8 :, :]
        for r in range(per):
            h = c * per + r
            at = slice(h * ROWS, (h + 1) * ROWS)
            row_ref[0:1, at] = row_ref[0:1, at] + float(h)
            for q, source in enumerate((0, 1, 6)):
                for b in range(blocks):
                    line = h * (blocks + 1) + b
                    begin = h * ROWS + b * 128
                    grid_ref[q, line : line + 1, :] = row_ref[source : source + 1, begin : begin + 128]


def lay_tables(grid_ref, table_refs, spread_refs):
    own = spread_refs[0].shape[0]
    blocks = ROWS // 128
    count = (own // ROWS + 2 * REACH) * (blocks + 1)
    ways = 128 // STEP
    lane = lax.broadcasted_iota(jnp.int32, (count, 128), 1)
    for q in range(2):
        here = grid_ref[q, :count, :]
        later = grid_ref[q, 1 : count + 1, :]
        table_refs[q][pl.ds(0, count, stride=ways), :] = here
        for k in range(1, ways):
            joined = jnp.where(lane < k * STEP, later, here)
            table_refs[q][pl.ds(k, count, stride=ways), :] = pltpu.roll(joined, 128 - k * STEP, 1)
        turned = jnp.concatenate([here, jnp.zeros((128 - count, 128), f32)], axis=0).T
        for g in range(own // ROWS):
            for b in range(blocks):
                line = (g + REACH) * (blocks + 1) + b
                begin = g * ROWS + b * 128
                spread_refs[q][begin : begin + 128, :] = jnp.broadcast_to(
                    turned[:, line : line + 1], (128, 128)
                )


def plan_windows(row_ref, grid_ref, span_ref, item_ref):
    blocks = ROWS // 128
    regions = row_ref.shape[1] // ROWS - 2 * REACH
    per = ROWS // TILE
    tiles = regions * per
    ways = 128 // STEP
    offsets = 2 * REACH + 1
    keys = [
        grid_ref[2, h * (blocks + 1) : h * (blocks + 1) + blocks, :] for h in range(regions + 2 * REACH)
    ]
    mine = jnp.concatenate(keys[REACH : REACH + regions], axis=0)
    top = jnp.where(mine < 0.5 * DEAD, mine, -DEAD)
    size = 1
    while size < TILE:
        top = jnp.maximum(top, pltpu.roll(top, 128 - size, 1))
        size *= 2
    parts = 128 // TILE
    lines = regions * blocks
    tile = lax.broadcasted_iota(jnp.int32, (lines, tiles), 1)
    line = lax.broadcasted_iota(jnp.int32, (lines, tiles), 0)
    first = jnp.zeros((1, tiles), f32)
    last = jnp.zeros((1, tiles), f32)
    for p in range(parts):
        here = tile == line * parts + p
        lane = slice(p * TILE, p * TILE + 1)
        first = first + jnp.sum(
            jnp.where(here, jnp.broadcast_to(mine[:, lane], (lines, tiles)), 0.0), axis=0, keepdims=True
        )
        last = last + jnp.sum(
            jnp.where(here, jnp.broadcast_to(top[:, lane], (lines, tiles)), 0.0), axis=0, keepdims=True
        )
    under, over = first - 1.001, last + 1.001
    begins, ends = [], []
    for key in keys:
        begin = jnp.zeros((blocks, tiles), f32)
        end = jnp.zeros((blocks, tiles), f32)
        for k in range(ways):
            low = jnp.broadcast_to(key[:, k * STEP : k * STEP + 1], (blocks, tiles))
            high = jnp.broadcast_to(key[:, (k + 1) * STEP - 1 : (k + 1) * STEP], (blocks, tiles))
            begin = begin + jnp.where(high < under, 1.0, 0.0)
            end = end + jnp.where(low <= over, 1.0, 0.0)
        begins.append(jnp.sum(begin, axis=0, keepdims=True))
        ends.append(jnp.sum(end, axis=0, keepdims=True))
    group = lax.broadcasted_iota(jnp.int32, (1, tiles), 1) // per
    alive = first < 0.5 * DEAD
    starts, stops = [], []
    needs = jnp.zeros((1, tiles), f32)
    for dh in range(offsets):
        d = dh - REACH
        start = jnp.zeros((1, tiles), f32)
        stop = jnp.zeros((1, tiles), f32)
        for g in range(regions):
            h = g + dh
            base = float(h * (ROWS + 128) // STEP)
            begin, end = begins[h] + base, ends[h] + base
            if d:
                source = 3 + abs(d)
                owner = (g + REACH if d > 0 else h) * ROWS
                flag = row_ref[source : source + 1, owner : owner + 128]
                end = jnp.where(flag[:, :tiles] > 0.5, end, begin)
            start = jnp.where(group == g, begin, start)
            stop = jnp.where(group == g, end, stop)
        stop = jnp.where(alive, jnp.maximum(stop, start), start)
        needs = jnp.maximum(needs, jnp.floor((stop - start + (ways - 1.0)) * (1.0 / ways)))
        starts.append(start)
        stops.append(stop)
    blank = jnp.full((8 - offsets, tiles), float(EMPTY), f32)
    for m in range(blocks + 1):
        lines_m = [
            jnp.where(start + float(ways * m) < stop, start + float(ways * m), float(EMPTY))
            for start, stop in zip(starts, stops)
        ]
        span_ref[8 * m : 8 * m + 8, :] = jnp.concatenate(lines_m + [blank], axis=0).astype(jnp.int32)
    row = lax.broadcasted_iota(jnp.int32, (tiles, tiles), 0)
    col = lax.broadcasted_iota(jnp.int32, (tiles, tiles), 1)
    many = jnp.broadcast_to(needs, (tiles, tiles)).astype(bf16)
    done = dot((col <= row).astype(f32).astype(bf16), many, NT)
    each = dot((col == row).astype(f32).astype(bf16), many, NT)
    total = jnp.max(done, axis=0, keepdims=True)
    for k in range(item_ref.shape[1]):
        slot = lax.broadcasted_iota(jnp.int32, (1, tiles), 1).astype(f32) + float(k * tiles)
        past = done <= slot
        at = jnp.sum(jnp.where(past, 1.0, 0.0), axis=0, keepdims=True)
        began = jnp.sum(jnp.where(past, each, 0.0), axis=0, keepdims=True)
        spare = slot >= total
        item_ref[0, k : k + 1, :] = jnp.where(spare, 0.0, at).astype(jnp.int32)
        item_ref[1, k : k + 1, :] = jnp.where(spare, float(blocks), slot - began).astype(jnp.int32)
        item_ref[2, k : k + 1, :] = total.astype(jnp.int32)


def turn_vectors(v_ref, row_ref, turn_ref):
    ens, wide = v_ref.shape
    padded = ROWS + 128
    row = lax.broadcasted_iota(jnp.int32, (256, 256), 0)
    eye = (row == lax.broadcasted_iota(jnp.int32, (256, 256), 1)).astype(f32).astype(bf16)
    for h in range(wide // ROWS):
        for b in range(ROWS // 256):
            at = slice(h * ROWS + b * 256, h * ROWS + (b + 1) * 256)
            stack = jnp.concatenate(two(v_ref[:, at] * row_ref[2:3, at]), axis=0)
            begin = h * padded + b * 256
            turn_ref[begin : begin + 256, :] = dot(eye, stack, NT).astype(bf16)
        turn_ref[h * padded + ROWS : (h + 1) * padded, :] = jnp.zeros((128, 2 * ens), bf16)


def apply_cov(
    span_ref, item_ref, row_ref, table_refs, spread_refs, v_ref, img_ref, turn_ref, sum_ref, s_ref
):
    ens, wide = v_ref.shape
    own = img_ref.shape[1]
    lead = REACH * ROWS
    s_ref[...] = jnp.zeros_like(s_ref)
    sum_ref[...] = jnp.zeros_like(sum_ref)

    def windows(n):
        line, lane = lax.shift_right_logical(n, jnp.int32(7)), lax.bitwise_and(n, jnp.int32(127))
        tile = item_ref[0, line, lane]
        level = item_ref[1, line, lane] * 8
        return [tile] + [span_ref[level + dh, tile] for dh in range(2 * REACH + 1)]

    def step(k, carry):
        for p in range(PAIR):
            tile, *found = carry[p]
            rhs = jnp.concatenate(
                [turn_ref[pl.ds(pl.multiple_of(w * STEP, STEP), 128), :] for w in found], axis=0
            )
            got = dot(s_ref[p], rhs)
            at = pl.ds(pl.multiple_of(tile * TILE, TILE), TILE)
            sum_ref[at, :] += got[:TILE] + got[TILE:]
        now = [windows(k * PAIR + p) for p in range(PAIR)]
        for p in range(PAIR):
            tile, *found = now[p]
            at = pl.ds(pl.multiple_of(tile * TILE, TILE), TILE)
            a_i = spread_refs[0][at, :]
            b_i = spread_refs[1][at, :]
            for d, w in enumerate(found):
                da = table_refs[0][pl.ds(w, 1), :] - a_i
                db = table_refs[1][pl.ds(w, 1), :] - b_i
                r2 = da * da + db * db
                r = r2 * lax.rsqrt(jnp.maximum(r2, 1e-30))
                u = jnp.maximum(1.0 - r, 0.0)
                u2 = u * u
                hi, lo = two((u2 * u2) * (r + 0.25))
                s_ref[p, 0:TILE, d * 128 : (d + 1) * 128] = hi
                s_ref[p, TILE : 2 * TILE, d * 128 : (d + 1) * 128] = lo
        return now

    trips = lax.shift_right_logical(item_ref[2, 0, 0] + (PAIR - 1), jnp.int32(PAIR.bit_length() - 1))
    lax.fori_loop(0, trips + 1, step, [windows(p) for p in range(PAIR)])
    for c in range(own // 128):
        at = slice(c * 128, (c + 1) * 128)
        e_at = slice(lead + c * 128, lead + (c + 1) * 128)
        turned = sum_ref[at, :].T
        img_ref[:, at] = (
            (turned[:ens] + turned[ens:]) * (row_ref[2:3, e_at] * 0.25) + row_ref[3:4, e_at] * v_ref[:, e_at]
        )


def gram(a, b):
    ahi, alo = two(a)
    bhi, blo = two(b)
    return dot(
        jnp.concatenate([ahi, ahi, alo], axis=1), jnp.concatenate([bhi, blo, bhi], axis=1), NT
    )


def square(n):
    return lax.broadcasted_iota(jnp.int32, (n, n), 0), lax.broadcasted_iota(jnp.int32, (n, n), 1)


def pack_pair(upper, lower):
    n = upper.shape[0]
    row, col = square(n)
    upper, lower = symmetric(upper), symmetric(lower)
    spare = jnp.sum(jnp.where(row == col, lower, 0.0), axis=0, keepdims=True)
    return jnp.where(col >= row, upper, lower), jnp.broadcast_to(spare, (8, n))


def unpack_pair(packed, spare):
    n = packed.shape[0]
    row, col = square(n)
    other = packed.T
    lower = jnp.where(row == col, jnp.broadcast_to(spare, (n, n)), jnp.where(col > row, other, packed))
    return jnp.where(col >= row, packed, other), lower


def first_kernel(
    c0,
    c1,
    c2,
    c3,
    imga_ref,
    imgb_ref,
    gram_ref,
    span_out,
    item_out,
    span_ref,
    item_ref,
    plan_sem,
    row_ref,
    grid_ref,
    along_ref,
    across_ref,
    along_i_ref,
    across_i_ref,
    v_ref,
    img_ref,
    turn_ref,
    sum_ref,
    s_ref,
):
    ens, own = img_ref.shape
    lead = REACH * ROWS
    chunks = [c0, c1, c2, c3]
    tables = (along_ref, across_ref)
    spreads = (along_i_ref, across_i_ref)
    lay_grid(chunks, row_ref, grid_ref)
    plan_windows(row_ref, grid_ref, span_out, item_out)
    span_copy = pltpu.make_async_copy(span_out, span_ref, plan_sem.at[0])
    item_copy = pltpu.make_async_copy(item_out, item_ref, plan_sem.at[1])
    span_copy.start()
    item_copy.start()
    lay_tables(grid_ref, tables, spreads)
    for c, ref in enumerate(chunks):
        v_ref[:, c * lead : (c + 1) * lead] = ref[:ens, :]
    turn_vectors(v_ref, row_ref, turn_ref)
    span_copy.wait()
    item_copy.wait()
    apply_cov(
        span_ref, item_ref, row_ref, tables, spreads, v_ref, img_ref, turn_ref, sum_ref, s_ref
    )
    imga_ref[...] = img_ref[:, :lead]
    imgb_ref[...] = img_ref[:, lead:]
    r = v_ref[:, lead : lead + own]
    both = gram(r, jnp.concatenate([r, img_ref[...]], axis=0))
    packed, spare = pack_pair(both[:, :ens], both[:, ens:])
    half = ens // 2
    gram_ref[0:half, :] = jnp.concatenate([packed[:half], packed[half:]], axis=1)
    gram_ref[half : half + 8, :] = jnp.concatenate([spare, spare], axis=1)


def second_kernel(
    span_in,
    item_in,
    step_ref,
    c0,
    c1,
    c2,
    c3,
    i0,
    i1,
    i2,
    i3,
    gram_ref,
    span_ref,
    item_ref,
    plan_sem,
    row_ref,
    grid_ref,
    along_ref,
    across_ref,
    along_i_ref,
    across_i_ref,
    v_ref,
    img_ref,
    turn_ref,
    sum_ref,
    s_ref,
):
    ens, own = img_ref.shape
    lead = REACH * ROWS
    chunks = [c0, c1, c2, c3]
    tables = (along_ref, across_ref)
    spreads = (along_i_ref, across_i_ref)
    span_copy = pltpu.make_async_copy(span_in, span_ref, plan_sem.at[0])
    item_copy = pltpu.make_async_copy(item_in, item_ref, plan_sem.at[1])
    span_copy.start()
    item_copy.start()
    lay_grid(chunks, row_ref, grid_ref)
    lay_tables(grid_ref, tables, spreads)
    step_t = step_ref[...].T
    for c, (ref, image) in enumerate(zip(chunks, [i0, i1, i2, i3])):
        v_ref[:, c * lead : (c + 1) * lead] = ref[:ens, :] - combine(step_t, image[...])
    turn_vectors(v_ref, row_ref, turn_ref)
    span_copy.wait()
    item_copy.wait()
    apply_cov(
        span_ref, item_ref, row_ref, tables, spreads, v_ref, img_ref, turn_ref, sum_ref, s_ref
    )
    r = v_ref[:, lead : lead + own]
    both = gram(r, jnp.concatenate([r, img_ref[...]], axis=0))
    mixed = gram(r, jnp.concatenate([i1[...], i2[...]], axis=1))
    packed, spare = pack_pair(both[:, :ens], both[:, ens:])
    gram_ref[0:ens, :] = jnp.concatenate([packed, mixed], axis=1)
    gram_ref[ens : ens + 8, :] = jnp.concatenate([spare, spare], axis=1)


def plan_shapes(own):
    tiles = own // TILE
    most = tiles * (ROWS // 128)
    return (8 * (ROWS // 128 + 1), tiles), (3, most // 128 + 1, 128)


def scratch(ens, own):
    regions = own // ROWS + 2 * REACH
    wide = regions * ROWS
    lines = -(-(regions * (ROWS // 128 + 1) + 1) // 8) * 8
    table = pltpu.VMEM((128 // STEP * lines, 128), f32)
    spread = pltpu.VMEM((own, 128), f32)
    spans, items = plan_shapes(own)
    return [
        pltpu.SMEM(spans, jnp.int32),
        pltpu.SMEM(items, jnp.int32),
        pltpu.SemaphoreType.DMA((2,)),
        pltpu.VMEM((8, wide), f32),
        pltpu.VMEM((3, lines, 128), f32),
        table,
        table,
        spread,
        spread,
        pltpu.VMEM((ens, wide), f32),
        pltpu.VMEM((ens, own), f32),
        pltpu.VMEM((regions * (ROWS + 128) + 128, 2 * ens), bf16),
        pltpu.VMEM((own, 128), f32),
        pltpu.VMEM((PAIR, 2 * TILE, (2 * REACH + 1) * 128), bf16),
    ]


def first_call(chunks, ens, own):
    half = jax.ShapeDtypeStruct((ens, own // 2), f32)
    spans, items = plan_shapes(own)
    return pl.pallas_call(
        first_kernel,
        out_shape=(
            half,
            half,
            jax.ShapeDtypeStruct((ens // 2 + 8, 2 * ens), f32),
            jax.ShapeDtypeStruct(spans, jnp.int32),
            jax.ShapeDtypeStruct(items, jnp.int32),
        ),
        in_specs=[vmem] * 4,
        out_specs=(vmem,) * 5,
        scratch_shapes=scratch(ens, own),
        compiler_params=params(),
        name="operate_first",
    )(*chunks)


def second_call(plan, step, chunks, images, ens, own):
    return pl.pallas_call(
        second_kernel,
        out_shape=jax.ShapeDtypeStruct((ens + 8, 2 * ens), f32),
        in_specs=[vmem] * 11,
        out_specs=vmem,
        scratch_shapes=scratch(ens, own),
        compiler_params=params(),
        name="operate_second",
    )(*plan, step, *chunks, *images)


def flip(me, size):
    return size * (1 - 2 * ((me // size) % 2))


def exchange_steps(total):
    bits = total.bit_length() - 1
    steps = [[1]] if bits % 2 else []
    for k in range(bits % 2, bits, 2):
        steps.append([2**k, 2 ** (k + 1)])
    return steps


def reduce_kernel(steps, n_col, x_ref, out_ref, send, recv, send_sem, recv_sem):
    me = lax.axis_index("reg") * n_col + lax.axis_index("col")
    partners = []
    for sizes in steps:
        others = [me + flip(me, size) for size in sizes]
        if len(sizes) == 2:
            others.append(others[0] + flip(me, sizes[1]))
        partners.append([(other // n_col, other % n_col) for other in others])
    barrier = pltpu.get_barrier_semaphore()
    for group in partners:
        for other in group:
            pl.semaphore_signal(
                barrier, inc=1, device_id=other, device_id_type=pl.DeviceIdType.MESH
            )
    pl.semaphore_wait(barrier, sum(len(group) for group in partners))
    total = x_ref[...]
    slot = 0
    for k, group in enumerate(partners):
        if k:
            send[k] = total
        copies = []
        for p, other in enumerate(group):
            copies.append(
                pltpu.make_async_remote_copy(
                    src_ref=send.at[k] if k else x_ref,
                    dst_ref=recv.at[slot + p],
                    send_sem=send_sem.at[slot + p],
                    recv_sem=recv_sem.at[slot + p],
                    device_id=other,
                    device_id_type=pl.DeviceIdType.MESH,
                )
            )
        for copy in copies:
            copy.start()
        for copy in copies:
            copy.wait()
        total = total + recv[slot]
        if len(group) == 3:
            total = total + (recv[slot + 1] + recv[slot + 2])
        slot += len(group)
    out_ref[...] = total


def sum_all(x, which):
    n_col = lax.axis_size("col")
    steps = exchange_steps(lax.axis_size("reg") * n_col)
    slots = sum(2 ** len(sizes) - 1 for sizes in steps)
    return pl.pallas_call(
        functools.partial(reduce_kernel, steps, n_col),
        out_shape=jax.ShapeDtypeStruct(x.shape, f32),
        in_specs=[vmem],
        out_specs=vmem,
        scratch_shapes=[
            pltpu.VMEM((len(steps),) + x.shape, f32),
            pltpu.VMEM((slots,) + x.shape, f32),
            pltpu.SemaphoreType.DMA((slots,)),
            pltpu.SemaphoreType.DMA((slots,)),
        ],
        compiler_params=pltpu.CompilerParams(collective_id=which, has_side_effects=True),
        name="sum_all",
    )(x)


def symmetric(matrix):
    return 0.5 * (matrix + matrix.T)


def mm(a, b, dims=NN):
    return lax.dot_general(a, b, dims, precision=highest, preferred_element_type=f32)


def eliminate(chains):
    ens, both = chains[0].shape
    parts = range(ens // 8)
    rows = lax.broadcasted_iota(jnp.int32, (8, both), 0)
    chains = [[m[8 * i : 8 * i + 8] for i in parts] for m in chains]

    def clear(parts_of, col, pivot, at):
        done = [x - c * pivot for x, c in zip(parts_of, col)]
        done[at // 8] = jnp.where(rows == at % 8, pivot, done[at // 8])
        return done

    for k in range(0, ens, PANEL):
        columns = [
            [[jnp.broadcast_to(x[:, k + j : k + j + 1], (8, both)) for x in m] for j in range(PANEL)]
            for m in chains
        ]
        for p in range(PANEL):
            at = k + p
            one = slice(at % 8, at % 8 + 1)
            done = []
            for m, cols in zip(chains, columns):
                col = cols[p]
                scale = 1.0 / col[at // 8][one]
                for j in range(p + 1, PANEL):
                    cols[j] = clear(cols[j], col, cols[j][at // 8][one] * scale, at)
                done.append(clear(m, col, m[at // 8][one] * scale, at))
            chains = done
    return [jnp.concatenate(m, axis=0)[:, ens:] for m in chains]


def solve_first_kernel(gram_ref, step_ref, inv_ref, curv_ref):
    ens = step_ref.shape[0]
    half = ens // 2
    packed = jnp.concatenate([gram_ref[0:half, :ens], gram_ref[0:half, ens:]], axis=0)
    norm, curv = unpack_pair(packed, gram_ref[half : half + 1, :ens])
    row, col = square(ens)
    eye = (row == col).astype(f32)
    step, inv = eliminate(
        [jnp.concatenate([curv, norm], axis=1), jnp.concatenate([norm, eye], axis=1)]
    )
    step_ref[...] = step
    inv_ref[...] = inv
    curv_ref[...] = curv


def solve_second_kernel(gram_ref, step_ref, inv_ref, curv_ref, coef_ref):
    ens = step_ref.shape[0]
    norm, cross = unpack_pair(gram_ref[0:ens, :ens], gram_ref[ens : ens + 1, :ens])
    mixed = gram_ref[0:ens, ens:]
    conj = mm(inv_ref[...], norm)
    coupled = mm(mixed, conj)
    quad = mm(conj, mm(curv_ref[...], conj), TN)
    curv = symmetric(cross + coupled + coupled.T + quad)
    (step,) = eliminate([jnp.concatenate([curv, norm], axis=1)])
    step0 = step_ref[...]
    keep = step0 + step + mm(conj, step)
    coef_ref[...] = jnp.concatenate([keep.T, -mm(step0, step).T], axis=1)


def solve_first(grams):
    ens = grams.shape[1] // 2
    small = jax.ShapeDtypeStruct((ens, ens), f32)
    return pl.pallas_call(
        solve_first_kernel,
        out_shape=(small, small, small),
        in_specs=[vmem],
        out_specs=(vmem, vmem, vmem),
        name="solve_first",
    )(grams)


def solve_second(grams, step0, inv0, curv0):
    ens = step0.shape[0]
    return pl.pallas_call(
        solve_second_kernel,
        out_shape=jax.ShapeDtypeStruct((ens, 2 * ens), f32),
        in_specs=[vmem] * 4,
        out_specs=vmem,
        name="solve_second",
    )(grams, step0, inv0, curv0)


def add_columns(stack, owner, cols_ref):
    ens = cols_ref.shape[0]
    for c in range(2 * COLS_DEV // 256):
        slot = lax.broadcasted_iota(jnp.int32, (256, ROWS), 0) + c * 256
        hot = (slot == owner).astype(f32).astype(bf16)
        got = dot(stack, hot, NT)
        part = slice(c * 256, (c + 1) * 256)
        cols_ref[:, part] += got[:ens] + got[ens:]


def innov_columns_kernel(innov_ref, info_ref, cols_ref):
    cols_ref[...] = jnp.zeros_like(cols_ref)

    def one(g, carry):
        at = pl.ds(pl.multiple_of(g * ROWS, ROWS), ROWS)
        scale = info_ref[0:1, at] * info_ref[1:2, at]
        owner = info_ref[2:3, at].astype(jnp.int32)
        add_columns(jnp.concatenate(two(innov_ref[:, at] * scale), axis=0), owner, cols_ref)
        return carry

    lax.fori_loop(0, innov_ref.shape[1] // ROWS, one, 0)


def columns_kernel(info_ref, rank_ref, imga_ref, imgb_ref, back_ref, cols_ref):
    ens, own = back_ref.shape
    half = own // 2
    cols_ref[...] = jnp.zeros_like(cols_ref)
    for g in range(own // ROWS):
        at = slice(g * ROWS, (g + 1) * ROWS)
        rank = rank_ref[0:1, at].astype(jnp.int32)
        img_ref = imga_ref if g * ROWS < half else imgb_ref
        begin = (g * ROWS) % half
        lhs = jnp.concatenate(two(img_ref[:, begin : begin + ROWS]), axis=0)
        total = jnp.zeros((2 * ens, ROWS), f32)
        for c in range(ROWS // 256):
            slot = lax.broadcasted_iota(jnp.int32, (256, ROWS), 0) + c * 256
            place = (slot == rank).astype(f32).astype(bf16)
            total = total + dot(lhs[:, c * 256 : (c + 1) * 256], place)
        image = total[:ens] + total[ens:]
        back_ref[:, at] = image
        owner = info_ref[2:3, at].astype(jnp.int32)
        add_columns(jnp.concatenate(two(image * info_ref[0:1, at]), axis=0), owner, cols_ref)


def innov_columns_call(innov, info):
    ens, own = innov.shape
    return pl.pallas_call(
        innov_columns_kernel,
        out_shape=jax.ShapeDtypeStruct((ens, 2 * COLS_DEV), f32),
        in_specs=[vmem] * 2,
        out_specs=vmem,
        compiler_params=params(),
        cost_estimate=pl.CostEstimate(
            flops=2 * 256 * own * 2048, bytes_accessed=4 << 20, transcendentals=0
        ),
        name="innov_columns",
    )(innov, info)


def columns_call(info, rank, imga, imgb):
    ens, half = imga.shape
    return pl.pallas_call(
        columns_kernel,
        out_shape=(
            jax.ShapeDtypeStruct((ens, 2 * half), f32),
            jax.ShapeDtypeStruct((ens, 2 * COLS_DEV), f32),
        ),
        in_specs=[vmem] * 4,
        out_specs=(vmem, vmem),
        compiler_params=params(),
        cost_estimate=pl.CostEstimate(
            flops=2 * 256 * 2 * half * 3072, bytes_accessed=4 << 20, transcendentals=0
        ),
        name="columns",
    )(info, rank, imga, imgb)


def final_kernel(coef_ref, innov_ref, info_ref, back_ref, rc_ref, rin_ref, ic_ref, iin_ref, w_ref, inc_ref):
    coef = coef_ref[...]
    ens = coef.shape[0]
    own = innov_ref.shape[1]
    chunk = 1024
    first, second = coef[:, :ens], coef[:, ens:]
    for c in range(own // chunk):
        at = pl.ds(c * chunk, chunk)
        live = info_ref[1:2, at]
        w_ref[:, at] = combine(first, innov_ref[:, at] * live) + combine(second, back_ref[:, at])
    inc_ref[...] = combine(first, rc_ref[:, :COLS_DEV] + rin_ref[...]) + combine(
        second, ic_ref[:, :COLS_DEV] + iin_ref[...]
    )


def final_call(coef, innov, info, back, *cols):
    ens, own = innov.shape
    return pl.pallas_call(
        final_kernel,
        out_shape=(
            jax.ShapeDtypeStruct((ens, own), f32),
            jax.ShapeDtypeStruct((ens, COLS_DEV), f32),
        ),
        in_specs=[vmem] * 8,
        out_specs=(vmem, vmem),
        compiler_params=params(),
        name="final",
    )(coef, innov, info, back, *cols)


def on_device(
    innovation,
    obs_along,
    obs_across,
    obs_scale,
    obs_error,
    obs_gain,
    pair_live,
    obs_count,
    col_owner,
):
    axes = ("reg", "col")
    ens, own = innovation.shape
    live = (
        (jnp.arange(ROWS, dtype=jnp.int32)[None, :] < obs_count[:, None])
        .astype(f32)
        .reshape(own)
    )
    flags = jnp.repeat(pair_live.astype(f32).T, ROWS, axis=1)
    zero = jnp.zeros((own,), f32)
    meta = jnp.stack(
        [obs_along, obs_across, obs_scale * live, obs_error, flags[0], flags[1]]
        + [jnp.where(live > 0.5, obs_across, DEAD)]
        + [zero] * (META - 7)
    )
    total_cols = COLS_DEV * lax.axis_size(axes)
    local_col = (col_owner - lax.axis_index(axes) * COLS_DEV) % total_cols
    info = jnp.stack([obs_gain, live, local_col.astype(f32)] + [zero] * 5)

    first, last, rank = sort_call(innovation, meta)
    after = shift(first, -1)
    before = shift(last, 1)
    chunks = [before, first, last, after]
    innov_cols = innov_columns_call(innovation, info)
    innov_came = shift(innov_cols[:, COLS_DEV:], 1)
    imga, imgb, grams, *plan = first_call(chunks, ens, own)
    img_after = shift(imga, -1)
    img_before = shift(imgb, 1)
    step0, inv0, curv0 = solve_first(sum_all(grams, 0))
    back, img_cols = columns_call(info, rank, imga, imgb)
    img_came = shift(img_cols[:, COLS_DEV:], 1)
    grams = second_call(plan, step0, chunks, [img_before, imga, imgb, img_after], ens, own)
    coef = solve_second(sum_all(grams, 1), step0, inv0, curv0)
    return tuple(
        final_call(coef, innovation, info, back, innov_cols, innov_came, img_cols, img_came)
    )


def solution(mesh):
    one = P(("reg", "col"))
    in_specs = (P(None, ("reg", "col")), one, one, one, one, one, P(("reg", "col"), None), one, one)
    out_specs = (P(None, ("reg", "col")), P(None, ("reg", "col")))
    return jax.shard_map(
        on_device, mesh=mesh, in_specs=in_specs, out_specs=out_specs, check_vma=False
    )
```

```python
import functools

import jax
import jax.numpy as jnp
from jax import lax
from jax.experimental import pallas as pl
from jax.experimental.pallas import tpu as pltpu
from jax.sharding import PartitionSpec as P

ROWS = 1024
REACH = 2
COLS_DEV = 1024
TILE = 32
STEP = 16
PAIR = 4
PANEL = 8
EMPTY = ROWS // STEP
DEAD = 1e9
FAR = 1e6
VMEM_LIMIT = 60 * 1024 * 1024

highest = lax.Precision.HIGHEST
f32 = jnp.float32
bf16 = jnp.bfloat16
NT = (((1,), (1,)), ((), ()))
NN = (((1,), (0,)), ((), ()))
TN = (((0,), (0,)), ((), ()))
vmem = pl.BlockSpec(memory_space=pltpu.VMEM)
smem = pl.BlockSpec(memory_space=pltpu.SMEM)
anywhere = pl.BlockSpec(memory_space=pl.ANY)


def dot(a, b, dims=NN):
    return lax.dot_general(a, b, dims, preferred_element_type=f32)


def two(x):
    hi = x.astype(bf16)
    return hi, (x - hi.astype(f32)).astype(bf16)


def three(x):
    hi = x.astype(bf16)
    rest = x - hi.astype(f32)
    mid = rest.astype(bf16)
    return hi, mid, (rest - mid.astype(f32)).astype(bf16)


def combine(coef_t, blocks):
    chi, clo = two(coef_t)
    bhi, blo = two(blocks)
    return dot(
        jnp.concatenate([chi, chi, clo], axis=1), jnp.concatenate([bhi, blo, bhi], axis=0)
    )


def params():
    return pltpu.CompilerParams(vmem_limit_bytes=VMEM_LIMIT)


def ring(total, n_col):
    me = lax.axis_index("reg") * n_col + lax.axis_index("col")
    left, right = (me + total - 1) % total, (me + 1) % total
    return me, (left // n_col, left % n_col), (right // n_col, right % n_col)


def send_to(src, dst, sems, k, device):
    return pltpu.make_async_remote_copy(
        src_ref=src,
        dst_ref=dst,
        send_sem=sems[0].at[k],
        recv_sem=sems[1].at[k],
        device_id=device,
        device_id_type=pl.DeviceIdType.MESH,
    )


def greet(devices):
    barrier = pltpu.get_barrier_semaphore()
    for device in devices:
        pl.semaphore_signal(barrier, inc=1, device_id=device, device_id_type=pl.DeviceIdType.MESH)


def live_row(count_ref, g):
    slot = lax.broadcasted_iota(jnp.int32, (1, ROWS), 1)
    return (slot < count_ref[g]).astype(f32)


def sort_kernel(
    total,
    n_col,
    count_ref,
    pair_ref,
    innov_ref,
    along_ref,
    across_ref,
    scale_ref,
    error_ref,
    first_ref,
    last_ref,
    before_ref,
    after_ref,
    rank_ref,
    send_sem,
    recv_sem,
):
    regions = innov_ref.shape[1] // ROWS
    sub = lax.broadcasted_iota(jnp.int32, (128, 128), 0)
    lane = lax.broadcasted_iota(jnp.int32, (128, 128), 1)
    _, left, right = ring(total, n_col)
    greet([left, right])

    def sort_region(out_ref, shift_by, r, carry):
        g = shift_by + r
        cols = pl.ds(pl.multiple_of(g * ROWS, ROWS), ROWS)
        live = live_row(count_ref, g)
        across = across_ref[:, cols]
        key = jnp.where(live > 0.5, across, DEAD)
        flags = [jnp.full((1, ROWS), pair_ref[g, d], jnp.int32).astype(f32) for d in range(REACH)]
        meta = [along_ref[:, cols], across, scale_ref[:, cols] * live, error_ref[:, cols]]
        stack = jnp.concatenate(
            [innov_ref[:, cols] * live] + meta + flags + [key, jnp.zeros((1, ROWS), f32)], axis=0
        )
        key_col = jnp.broadcast_to(key, (128, ROWS)).T
        ranks = []
        for b in range(ROWS // 128):
            begin, end = b * 128, (b + 1) * 128
            mine = key[:, begin:end]
            other = key_col[begin:end]
            ahead = (other < mine) | ((other == mine) & (sub < lane))
            rank = jnp.sum(jnp.where(ahead, 1.0, 0.0), axis=0, keepdims=True)
            if b:
                ahead = jnp.where(key_col[:begin] <= mine, 1.0, 0.0)
                rank = rank + jnp.sum(ahead, axis=0, keepdims=True)
            if end < ROWS:
                ahead = jnp.where(key_col[end:] < mine, 1.0, 0.0)
                rank = rank + jnp.sum(ahead, axis=0, keepdims=True)
            ranks.append(rank)
        rank = jnp.concatenate(ranks, axis=1)
        rank_ref[:, cols] = jnp.broadcast_to(rank, (8, ROWS))
        lhs = jnp.concatenate(three(stack), axis=0)
        n = stack.shape[0]
        rank_i = rank.astype(jnp.int32)
        for c in range(ROWS // 256):
            slot = lax.broadcasted_iota(jnp.int32, (256, ROWS), 0) + c * 256
            place = (slot == rank_i).astype(f32).astype(bf16)
            got = dot(lhs, place, NT)
            at = pl.ds(pl.multiple_of(r * ROWS + c * 256, 256), 256)
            out_ref[:, at] = got[:n] + got[n : 2 * n] + got[2 * n :]
        return carry

    half = regions // 2
    lax.fori_loop(0, half, functools.partial(sort_region, first_ref, 0), 0)
    pl.semaphore_wait(pltpu.get_barrier_semaphore(), 2)
    sems = (send_sem, recv_sem)
    back = send_to(first_ref, after_ref, sems, 0, left)
    back.start()
    lax.fori_loop(0, half, functools.partial(sort_region, last_ref, half), 0)
    ahead = send_to(last_ref, before_ref, sems, 1, right)
    ahead.start()
    back.wait()
    ahead.wait()


def sizes():
    n_col = lax.axis_size("col")
    return lax.axis_size("reg") * n_col, n_col


def comm_params(which):
    return pltpu.CompilerParams(
        collective_id=which, has_side_effects=True, vmem_limit_bytes=VMEM_LIMIT
    )


def sort_call(count, pair, innov, *rows):
    ens, n = innov.shape
    half = jax.ShapeDtypeStruct((ens + 8, n // 2), f32)
    return pl.pallas_call(
        functools.partial(sort_kernel, *sizes()),
        out_shape=(half,) * 4 + (jax.ShapeDtypeStruct((8, n), f32),),
        in_specs=[smem] * 2 + [vmem] * 5,
        out_specs=(vmem, vmem, anywhere, anywhere, vmem),
        scratch_shapes=[pltpu.SemaphoreType.DMA((2,)), pltpu.SemaphoreType.DMA((2,))],
        compiler_params=comm_params(0),
        name="sort_slots",
    )(count, pair, innov, *rows)


def lay_grid(chunks, row_ref, grid_ref):
    width = chunks[0].shape[1]
    per = width // ROWS
    blocks = ROWS // 128
    grid_ref[...] = jnp.full(grid_ref.shape, FAR, f32)
    for c, ref in enumerate(chunks):
        row_ref[:, c * width : (c + 1) * width] = ref[ref.shape[0] - 8 :, :]
        for r in range(per):
            h = c * per + r
            at = slice(h * ROWS, (h + 1) * ROWS)
            row_ref[0:1, at] = row_ref[0:1, at] + float(h)
            for q, source in enumerate((0, 1, 6)):
                for b in range(blocks):
                    line = h * (blocks + 1) + b
                    begin = h * ROWS + b * 128
                    grid_ref[q, line : line + 1, :] = row_ref[source : source + 1, begin : begin + 128]


def lay_tables(grid_ref, table_refs, spread_refs):
    own = spread_refs[0].shape[0]
    blocks = ROWS // 128
    count = (own // ROWS + 2 * REACH) * (blocks + 1)
    ways = 128 // STEP
    lane = lax.broadcasted_iota(jnp.int32, (count, 128), 1)
    for q in range(2):
        here = grid_ref[q, :count, :]
        later = grid_ref[q, 1 : count + 1, :]
        table_refs[q][pl.ds(0, count, stride=ways), :] = here
        for k in range(1, ways):
            joined = jnp.where(lane < k * STEP, later, here)
            table_refs[q][pl.ds(k, count, stride=ways), :] = pltpu.roll(joined, 128 - k * STEP, 1)
        turned = jnp.concatenate([here, jnp.zeros((128 - count, 128), f32)], axis=0).T
        for g in range(own // ROWS):
            for b in range(blocks):
                line = (g + REACH) * (blocks + 1) + b
                begin = g * ROWS + b * 128
                spread_refs[q][begin : begin + 128, :] = jnp.broadcast_to(
                    turned[:, line : line + 1], (128, 128)
                )


def plan_windows(row_ref, grid_ref, span_ref, item_ref):
    blocks = ROWS // 128
    regions = row_ref.shape[1] // ROWS - 2 * REACH
    per = ROWS // TILE
    tiles = regions * per
    ways = 128 // STEP
    offsets = 2 * REACH + 1
    keys = [
        grid_ref[2, h * (blocks + 1) : h * (blocks + 1) + blocks, :] for h in range(regions + 2 * REACH)
    ]
    mine = jnp.concatenate(keys[REACH : REACH + regions], axis=0)
    top = jnp.where(mine < 0.5 * DEAD, mine, -DEAD)
    size = 1
    while size < TILE:
        top = jnp.maximum(top, pltpu.roll(top, 128 - size, 1))
        size *= 2
    parts = 128 // TILE
    lines = regions * blocks
    tile = lax.broadcasted_iota(jnp.int32, (lines, tiles), 1)
    line = lax.broadcasted_iota(jnp.int32, (lines, tiles), 0)
    first = jnp.zeros((1, tiles), f32)
    last = jnp.zeros((1, tiles), f32)
    for p in range(parts):
        here = tile == line * parts + p
        lane = slice(p * TILE, p * TILE + 1)
        first = first + jnp.sum(
            jnp.where(here, jnp.broadcast_to(mine[:, lane], (lines, tiles)), 0.0), axis=0, keepdims=True
        )
        last = last + jnp.sum(
            jnp.where(here, jnp.broadcast_to(top[:, lane], (lines, tiles)), 0.0), axis=0, keepdims=True
        )
    under, over = first - 1.001, last + 1.001
    begins, ends = [], []
    for key in keys:
        begin = jnp.zeros((blocks, tiles), f32)
        end = jnp.zeros((blocks, tiles), f32)
        for k in range(ways):
            low = jnp.broadcast_to(key[:, k * STEP : k * STEP + 1], (blocks, tiles))
            high = jnp.broadcast_to(key[:, (k + 1) * STEP - 1 : (k + 1) * STEP], (blocks, tiles))
            begin = begin + jnp.where(high < under, 1.0, 0.0)
            end = end + jnp.where(low <= over, 1.0, 0.0)
        begins.append(jnp.sum(begin, axis=0, keepdims=True))
        ends.append(jnp.sum(end, axis=0, keepdims=True))
    group = lax.broadcasted_iota(jnp.int32, (1, tiles), 1) // per
    alive = first < 0.5 * DEAD
    starts, stops = [], []
    needs = jnp.zeros((1, tiles), f32)
    for dh in range(offsets):
        d = dh - REACH
        start = jnp.zeros((1, tiles), f32)
        stop = jnp.zeros((1, tiles), f32)
        for g in range(regions):
            h = g + dh
            base = float(h * (ROWS + 128) // STEP)
            begin, end = begins[h] + base, ends[h] + base
            if d:
                source = 3 + abs(d)
                owner = (g + REACH if d > 0 else h) * ROWS
                flag = row_ref[source : source + 1, owner : owner + 128]
                end = jnp.where(flag[:, :tiles] > 0.5, end, begin)
            start = jnp.where(group == g, begin, start)
            stop = jnp.where(group == g, end, stop)
        stop = jnp.where(alive, jnp.maximum(stop, start), start)
        needs = jnp.maximum(needs, jnp.floor((stop - start + (ways - 1.0)) * (1.0 / ways)))
        starts.append(start)
        stops.append(stop)
    blank = jnp.full((8 - offsets, tiles), float(EMPTY), f32)
    for m in range(blocks + 1):
        lines_m = [
            jnp.where(start + float(ways * m) < stop, start + float(ways * m), float(EMPTY))
            for start, stop in zip(starts, stops)
        ]
        span_ref[8 * m : 8 * m + 8, :] = jnp.concatenate(lines_m + [blank], axis=0).astype(jnp.int32)
    row = lax.broadcasted_iota(jnp.int32, (tiles, tiles), 0)
    col = lax.broadcasted_iota(jnp.int32, (tiles, tiles), 1)
    many = jnp.broadcast_to(needs, (tiles, tiles)).astype(bf16)
    done = dot((col <= row).astype(f32).astype(bf16), many, NT)
    each = dot((col == row).astype(f32).astype(bf16), many, NT)
    total = jnp.max(done, axis=0, keepdims=True)
    for k in range(item_ref.shape[1]):
        slot = lax.broadcasted_iota(jnp.int32, (1, tiles), 1).astype(f32) + float(k * tiles)
        past = done <= slot
        at = jnp.sum(jnp.where(past, 1.0, 0.0), axis=0, keepdims=True)
        began = jnp.sum(jnp.where(past, each, 0.0), axis=0, keepdims=True)
        spare = slot >= total
        item_ref[0, k : k + 1, :] = jnp.where(spare, 0.0, at).astype(jnp.int32)
        item_ref[1, k : k + 1, :] = jnp.where(spare, float(blocks), slot - began).astype(jnp.int32)
        item_ref[2, k : k + 1, :] = total.astype(jnp.int32)


def turn_vectors(v_ref, row_ref, turn_ref):
    ens, wide = v_ref.shape
    padded = ROWS + 128
    row = lax.broadcasted_iota(jnp.int32, (256, 256), 0)
    eye = (row == lax.broadcasted_iota(jnp.int32, (256, 256), 1)).astype(f32).astype(bf16)
    for h in range(wide // ROWS):
        for b in range(ROWS // 256):
            at = slice(h * ROWS + b * 256, h * ROWS + (b + 1) * 256)
            stack = jnp.concatenate(two(v_ref[:, at] * row_ref[2:3, at]), axis=0)
            begin = h * padded + b * 256
            turn_ref[begin : begin + 256, :] = dot(eye, stack, NT).astype(bf16)
        turn_ref[h * padded + ROWS : (h + 1) * padded, :] = jnp.zeros((128, 2 * ens), bf16)


def apply_cov(
    span_ref, item_ref, row_ref, table_refs, spread_refs, v_ref, img_ref, turn_ref, sum_ref, s_ref
):
    ens, wide = v_ref.shape
    own = img_ref.shape[1]
    lead = REACH * ROWS
    s_ref[...] = jnp.zeros_like(s_ref)
    sum_ref[...] = jnp.zeros_like(sum_ref)

    def windows(n):
        line, lane = lax.shift_right_logical(n, jnp.int32(7)), lax.bitwise_and(n, jnp.int32(127))
        tile = item_ref[0, line, lane]
        level = item_ref[1, line, lane] * 8
        return [tile] + [span_ref[level + dh, tile] for dh in range(2 * REACH + 1)]

    def step(k, carry):
        for p in range(PAIR):
            tile, *found = carry[p]
            rhs = jnp.concatenate(
                [turn_ref[pl.ds(pl.multiple_of(w * STEP, STEP), 128), :] for w in found], axis=0
            )
            got = dot(s_ref[p], rhs)
            at = pl.ds(pl.multiple_of(tile * TILE, TILE), TILE)
            sum_ref[at, :] += got[:TILE] + got[TILE:]
        now = [windows(k * PAIR + p) for p in range(PAIR)]
        for p in range(PAIR):
            tile, *found = now[p]
            at = pl.ds(pl.multiple_of(tile * TILE, TILE), TILE)
            a_i = spread_refs[0][at, :]
            b_i = spread_refs[1][at, :]
            for d, w in enumerate(found):
                da = table_refs[0][pl.ds(w, 1), :] - a_i
                db = table_refs[1][pl.ds(w, 1), :] - b_i
                r2 = da * da + db * db
                r = r2 * lax.rsqrt(jnp.maximum(r2, 1e-30))
                u = jnp.maximum(1.0 - r, 0.0)
                u2 = u * u
                hi, lo = two((u2 * u2) * (r + 0.25))
                s_ref[p, 0:TILE, d * 128 : (d + 1) * 128] = hi
                s_ref[p, TILE : 2 * TILE, d * 128 : (d + 1) * 128] = lo
        return now

    trips = lax.shift_right_logical(item_ref[2, 0, 0] + (PAIR - 1), jnp.int32(PAIR.bit_length() - 1))
    lax.fori_loop(0, trips + 1, step, [windows(p) for p in range(PAIR)])
    for c in range(own // 128):
        at = slice(c * 128, (c + 1) * 128)
        e_at = slice(lead + c * 128, lead + (c + 1) * 128)
        turned = sum_ref[at, :].T
        img_ref[:, at] = (
            (turned[:ens] + turned[ens:]) * (row_ref[2:3, e_at] * 0.25) + row_ref[3:4, e_at] * v_ref[:, e_at]
        )


def gram(a, b):
    ahi, alo = two(a)
    bhi, blo = two(b)
    return dot(
        jnp.concatenate([ahi, ahi, alo], axis=1), jnp.concatenate([bhi, blo, bhi], axis=1), NT
    )


def square(n):
    return lax.broadcasted_iota(jnp.int32, (n, n), 0), lax.broadcasted_iota(jnp.int32, (n, n), 1)


def pack_pair(upper, lower):
    n = upper.shape[0]
    row, col = square(n)
    upper, lower = symmetric(upper), symmetric(lower)
    spare = jnp.sum(jnp.where(row == col, lower, 0.0), axis=0, keepdims=True)
    return jnp.where(col >= row, upper, lower), jnp.broadcast_to(spare, (8, n))


def unpack_pair(packed, spare):
    n = packed.shape[0]
    row, col = square(n)
    other = packed.T
    lower = jnp.where(row == col, jnp.broadcast_to(spare, (n, n)), jnp.where(col > row, other, packed))
    return jnp.where(col >= row, packed, other), lower


def first_kernel(
    c0,
    c1,
    c2,
    c3,
    imga_ref,
    imgb_ref,
    gram_ref,
    span_out,
    item_out,
    span_ref,
    item_ref,
    plan_sem,
    row_ref,
    grid_ref,
    along_ref,
    across_ref,
    along_i_ref,
    across_i_ref,
    v_ref,
    img_ref,
    turn_ref,
    sum_ref,
    s_ref,
):
    ens, own = img_ref.shape
    lead = REACH * ROWS
    chunks = [c0, c1, c2, c3]
    tables = (along_ref, across_ref)
    spreads = (along_i_ref, across_i_ref)
    lay_grid(chunks, row_ref, grid_ref)
    plan_windows(row_ref, grid_ref, span_out, item_out)
    span_copy = pltpu.make_async_copy(span_out, span_ref, plan_sem.at[0])
    item_copy = pltpu.make_async_copy(item_out, item_ref, plan_sem.at[1])
    span_copy.start()
    item_copy.start()
    lay_tables(grid_ref, tables, spreads)
    for c, ref in enumerate(chunks):
        v_ref[:, c * lead : (c + 1) * lead] = ref[:ens, :]
    turn_vectors(v_ref, row_ref, turn_ref)
    span_copy.wait()
    item_copy.wait()
    apply_cov(
        span_ref, item_ref, row_ref, tables, spreads, v_ref, img_ref, turn_ref, sum_ref, s_ref
    )
    imga_ref[...] = img_ref[:, :lead]
    imgb_ref[...] = img_ref[:, lead:]
    r = v_ref[:, lead : lead + own]
    both = gram(r, jnp.concatenate([r, img_ref[...]], axis=0))
    packed, spare = pack_pair(both[:, :ens], both[:, ens:])
    half = ens // 2
    gram_ref[0:half, :] = jnp.concatenate([packed[:half], packed[half:]], axis=1)
    gram_ref[half : half + 8, :] = jnp.concatenate([spare, spare], axis=1)


def second_kernel(
    span_in,
    item_in,
    step_ref,
    c0,
    c1,
    c2,
    c3,
    i0,
    i1,
    i2,
    i3,
    gram_ref,
    span_ref,
    item_ref,
    plan_sem,
    row_ref,
    grid_ref,
    along_ref,
    across_ref,
    along_i_ref,
    across_i_ref,
    v_ref,
    img_ref,
    turn_ref,
    sum_ref,
    s_ref,
):
    ens, own = img_ref.shape
    lead = REACH * ROWS
    chunks = [c0, c1, c2, c3]
    tables = (along_ref, across_ref)
    spreads = (along_i_ref, across_i_ref)
    span_copy = pltpu.make_async_copy(span_in, span_ref, plan_sem.at[0])
    item_copy = pltpu.make_async_copy(item_in, item_ref, plan_sem.at[1])
    span_copy.start()
    item_copy.start()
    lay_grid(chunks, row_ref, grid_ref)
    lay_tables(grid_ref, tables, spreads)
    step_t = step_ref[...].T
    for c, (ref, image) in enumerate(zip(chunks, [i0, i1, i2, i3])):
        v_ref[:, c * lead : (c + 1) * lead] = ref[:ens, :] - combine(step_t, image[...])
    turn_vectors(v_ref, row_ref, turn_ref)
    span_copy.wait()
    item_copy.wait()
    apply_cov(
        span_ref, item_ref, row_ref, tables, spreads, v_ref, img_ref, turn_ref, sum_ref, s_ref
    )
    r = v_ref[:, lead : lead + own]
    both = gram(r, jnp.concatenate([r, img_ref[...]], axis=0))
    mixed = gram(r, jnp.concatenate([i1[...], i2[...]], axis=1))
    packed, spare = pack_pair(both[:, :ens], both[:, ens:])
    gram_ref[0:ens, :] = jnp.concatenate([packed, mixed], axis=1)
    gram_ref[ens : ens + 8, :] = jnp.concatenate([spare, spare], axis=1)


def plan_shapes(own):
    tiles = own // TILE
    most = tiles * (ROWS // 128)
    return (8 * (ROWS // 128 + 1), tiles), (3, most // 128 + 1, 128)


def scratch(ens, own):
    regions = own // ROWS + 2 * REACH
    wide = regions * ROWS
    lines = -(-(regions * (ROWS // 128 + 1) + 1) // 8) * 8
    table = pltpu.VMEM((128 // STEP * lines, 128), f32)
    spread = pltpu.VMEM((own, 128), f32)
    spans, items = plan_shapes(own)
    return [
        pltpu.SMEM(spans, jnp.int32),
        pltpu.SMEM(items, jnp.int32),
        pltpu.SemaphoreType.DMA((2,)),
        pltpu.VMEM((8, wide), f32),
        pltpu.VMEM((3, lines, 128), f32),
        table,
        table,
        spread,
        spread,
        pltpu.VMEM((ens, wide), f32),
        pltpu.VMEM((ens, own), f32),
        pltpu.VMEM((regions * (ROWS + 128) + 128, 2 * ens), bf16),
        pltpu.VMEM((own, 128), f32),
        pltpu.VMEM((PAIR, 2 * TILE, (2 * REACH + 1) * 128), bf16),
    ]


def first_call(chunks, ens, own):
    half = jax.ShapeDtypeStruct((ens, own // 2), f32)
    spans, items = plan_shapes(own)
    return pl.pallas_call(
        first_kernel,
        out_shape=(
            half,
            half,
            jax.ShapeDtypeStruct((ens // 2 + 8, 2 * ens), f32),
            jax.ShapeDtypeStruct(spans, jnp.int32),
            jax.ShapeDtypeStruct(items, jnp.int32),
        ),
        in_specs=[vmem] * 4,
        out_specs=(vmem,) * 5,
        scratch_shapes=scratch(ens, own),
        compiler_params=params(),
        name="operate_first",
    )(*chunks)


def second_call(plan, step, chunks, images, ens, own):
    return pl.pallas_call(
        second_kernel,
        out_shape=jax.ShapeDtypeStruct((ens + 8, 2 * ens), f32),
        in_specs=[vmem] * 11,
        out_specs=vmem,
        scratch_shapes=scratch(ens, own),
        compiler_params=params(),
        name="operate_second",
    )(*plan, step, *chunks, *images)


def flip(me, size):
    return size * (1 - 2 * ((me // size) % 2))


def exchange_steps(total):
    bits = total.bit_length() - 1
    steps = [[1]] if bits % 2 else []
    for k in range(bits % 2, bits, 2):
        steps.append([2**k, 2 ** (k + 1)])
    return steps


def partners_of(steps, n_col, me):
    found = []
    for amounts in steps:
        others = [me + flip(me, size) for size in amounts]
        if len(amounts) == 2:
            others.append(others[0] + flip(me, amounts[1]))
        found.append([(other // n_col, other % n_col) for other in others])
    return found


def sum_all(partners, x_ref, send, recv, sems, work):
    total = x_ref[...]
    slot = 0
    for k, group in enumerate(partners):
        if k:
            send[k] = total
        source = send.at[k] if k else x_ref
        copies = [
            send_to(source, recv.at[slot + p], sems, slot + p, other) for p, other in enumerate(group)
        ]
        for copy in copies:
            copy.start()
        if k < len(work):
            work[k]()
        for copy in copies:
            copy.wait()
        total = total + recv[slot]
        if len(group) == 3:
            total = total + (recv[slot + 1] + recv[slot + 2])
        slot += len(group)
    for piece in work[len(partners) :]:
        piece()
    return total


def local_column(owner, me, total):
    local = owner - me * COLS_DEV
    return jnp.where(local < 0, local + total * COLS_DEV, local)


def add_columns(scaled_ref, owner_ref, me, total, base, target_ref):
    own = owner_ref.shape[1]

    def one(c, carry):
        got = jnp.zeros((scaled_ref.shape[0], 256), f32)
        for g in range(own // ROWS):
            at = slice(g * ROWS, (g + 1) * ROWS)
            slot = lax.broadcasted_iota(jnp.int32, (256, ROWS), 0) + (base + c * 256)
            owner = local_column(owner_ref[:, at], me, total)
            hot = (slot == owner).astype(f32).astype(bf16)
            got = got + dot(scaled_ref[:, at], hot, NT)
        ens = target_ref.shape[0]
        target_ref[:, pl.ds(pl.multiple_of(c * 256, 256), 256)] = got[:ens] + got[ens:]
        return carry

    lax.fori_loop(0, COLS_DEV // 256, one, 0)


def join_first_kernel(
    steps,
    total,
    n_col,
    x_ref,
    imga_ref,
    imgb_ref,
    rank_ref,
    gain_ref,
    owner_ref,
    out_ref,
    before_ref,
    after_ref,
    back_ref,
    cols_ref,
    came_ref,
    scaled_ref,
    edge_ref,
    send,
    recv,
    send_sem,
    recv_sem,
    bulk_send_sem,
    bulk_recv_sem,
):
    ens, half = imga_ref.shape
    me, left, right = ring(total, n_col)
    partners = partners_of(steps, n_col, me)
    everyone = [other for group in partners for other in group] + [left, right]
    greet(everyone)
    pl.semaphore_wait(pltpu.get_barrier_semaphore(), len(everyone))
    bulk = (bulk_send_sem, bulk_recv_sem)
    copies = [send_to(imga_ref, after_ref, bulk, 0, left), send_to(imgb_ref, before_ref, bulk, 1, right)]
    edge = send_to(edge_ref, came_ref, bulk, 2, right)

    def unsort():
        for copy in copies:
            copy.start()
        for k, img_ref in enumerate((imga_ref, imgb_ref)):

            def one(r, carry, k=k, img_ref=img_ref):
                at = pl.ds(pl.multiple_of(k * half + r * ROWS, ROWS), ROWS)
                rank = rank_ref[0:1, at].astype(jnp.int32)
                mine = img_ref[:, pl.ds(pl.multiple_of(r * ROWS, ROWS), ROWS)]
                lhs = jnp.concatenate(two(mine), axis=0)
                got = jnp.zeros((2 * ens, ROWS), f32)
                for c in range(ROWS // 256):
                    slot = lax.broadcasted_iota(jnp.int32, (256, ROWS), 0) + c * 256
                    place = (slot == rank).astype(f32).astype(bf16)
                    got = got + dot(lhs[:, c * 256 : (c + 1) * 256], place)
                image = got[:ens] + got[ens:]
                back_ref[:, at] = image
                scaled_ref[:, at] = jnp.concatenate(two(image * gain_ref[:, at]), axis=0)
                return carry

            lax.fori_loop(0, half // ROWS, one, 0)

    def outer():
        add_columns(scaled_ref, owner_ref, me, total, COLS_DEV, edge_ref)
        edge.start()

    def inner():
        add_columns(scaled_ref, owner_ref, me, total, 0, cols_ref)

    out_ref[...] = sum_all(partners, x_ref, send, recv, (send_sem, recv_sem), [unsort, outer, inner])
    for copy in copies + [edge]:
        copy.wait()


def join_second_kernel(
    steps,
    total,
    n_col,
    count_ref,
    x_ref,
    innov_ref,
    gain_ref,
    owner_ref,
    out_ref,
    cols_ref,
    came_ref,
    scaled_ref,
    edge_ref,
    send,
    recv,
    send_sem,
    recv_sem,
    bulk_send_sem,
    bulk_recv_sem,
):
    own = innov_ref.shape[1]
    me, left, right = ring(total, n_col)
    partners = partners_of(steps, n_col, me)
    everyone = [other for group in partners for other in group] + [left, right]
    greet(everyone)
    pl.semaphore_wait(pltpu.get_barrier_semaphore(), len(everyone))
    edge = send_to(edge_ref, came_ref, (bulk_send_sem, bulk_recv_sem), 0, right)

    def scale():
        def one(g, carry):
            at = pl.ds(pl.multiple_of(g * ROWS, ROWS), ROWS)
            factor = gain_ref[:, at] * live_row(count_ref, g)
            scaled_ref[:, at] = jnp.concatenate(two(innov_ref[:, at] * factor), axis=0)
            return carry

        lax.fori_loop(0, own // ROWS, one, 0)

    def outer():
        add_columns(scaled_ref, owner_ref, me, total, COLS_DEV, edge_ref)
        edge.start()

    def inner():
        add_columns(scaled_ref, owner_ref, me, total, 0, cols_ref)

    out_ref[...] = sum_all(partners, x_ref, send, recv, (send_sem, recv_sem), [scale, outer, inner])
    edge.wait()


def join_scratch(steps, shape, ens, own, bulk):
    slots = sum(2 ** len(amounts) - 1 for amounts in steps)
    return [
        pltpu.VMEM((2 * ens, own), bf16),
        pltpu.VMEM((ens, COLS_DEV), f32),
        pltpu.VMEM((len(steps),) + shape, f32),
        pltpu.VMEM((slots,) + shape, f32),
        pltpu.SemaphoreType.DMA((slots,)),
        pltpu.SemaphoreType.DMA((slots,)),
        pltpu.SemaphoreType.DMA((bulk,)),
        pltpu.SemaphoreType.DMA((bulk,)),
    ]


def join_first(x, imga, imgb, rank, gain, owner):
    ens, half = imga.shape
    total, n_col = sizes()
    steps = exchange_steps(total)
    halo = jax.ShapeDtypeStruct((ens, half), f32)
    cols = jax.ShapeDtypeStruct((ens, COLS_DEV), f32)
    return pl.pallas_call(
        functools.partial(join_first_kernel, steps, total, n_col),
        out_shape=(
            jax.ShapeDtypeStruct(x.shape, f32),
            halo,
            halo,
            jax.ShapeDtypeStruct((ens, 2 * half), f32),
            cols,
            cols,
        ),
        in_specs=[vmem] * 6,
        out_specs=(vmem, anywhere, anywhere, vmem, vmem, anywhere),
        scratch_shapes=join_scratch(steps, x.shape, ens, 2 * half, 3),
        compiler_params=comm_params(1),
        name="join_first",
    )(x, imga, imgb, rank, gain, owner)


def join_second(count, x, innov, gain, owner):
    ens, own = innov.shape
    total, n_col = sizes()
    steps = exchange_steps(total)
    cols = jax.ShapeDtypeStruct((ens, COLS_DEV), f32)
    return pl.pallas_call(
        functools.partial(join_second_kernel, steps, total, n_col),
        out_shape=(jax.ShapeDtypeStruct(x.shape, f32), cols, cols),
        in_specs=[smem] + [vmem] * 4,
        out_specs=(vmem, vmem, anywhere),
        scratch_shapes=join_scratch(steps, x.shape, ens, own, 1),
        compiler_params=comm_params(2),
        name="join_second",
    )(count, x, innov, gain, owner)


def symmetric(matrix):
    return 0.5 * (matrix + matrix.T)


def mm(a, b, dims=NN):
    return lax.dot_general(a, b, dims, precision=highest, preferred_element_type=f32)


def eliminate(chains):
    ens, both = chains[0].shape
    parts = range(ens // 8)
    rows = lax.broadcasted_iota(jnp.int32, (8, both), 0)
    chains = [[m[8 * i : 8 * i + 8] for i in parts] for m in chains]

    def clear(parts_of, col, pivot, at):
        done = [x - c * pivot for x, c in zip(parts_of, col)]
        done[at // 8] = jnp.where(rows == at % 8, pivot, done[at // 8])
        return done

    for k in range(0, ens, PANEL):
        columns = [
            [[jnp.broadcast_to(x[:, k + j : k + j + 1], (8, both)) for x in m] for j in range(PANEL)]
            for m in chains
        ]
        for p in range(PANEL):
            at = k + p
            one = slice(at % 8, at % 8 + 1)
            done = []
            for m, cols in zip(chains, columns):
                col = cols[p]
                scale = 1.0 / col[at // 8][one]
                for j in range(p + 1, PANEL):
                    cols[j] = clear(cols[j], col, cols[j][at // 8][one] * scale, at)
                done.append(clear(m, col, m[at // 8][one] * scale, at))
            chains = done
    return [jnp.concatenate(m, axis=0)[:, ens:] for m in chains]


def solve_first_kernel(gram_ref, step_ref, inv_ref, curv_ref):
    ens = step_ref.shape[0]
    half = ens // 2
    packed = jnp.concatenate([gram_ref[0:half, :ens], gram_ref[0:half, ens:]], axis=0)
    norm, curv = unpack_pair(packed, gram_ref[half : half + 1, :ens])
    row, col = square(ens)
    eye = (row == col).astype(f32)
    step, inv = eliminate(
        [jnp.concatenate([curv, norm], axis=1), jnp.concatenate([norm, eye], axis=1)]
    )
    step_ref[...] = step
    inv_ref[...] = inv
    curv_ref[...] = curv


def solve_second_kernel(gram_ref, step_ref, inv_ref, curv_ref, coef_ref):
    ens = step_ref.shape[0]
    norm, cross = unpack_pair(gram_ref[0:ens, :ens], gram_ref[ens : ens + 1, :ens])
    mixed = gram_ref[0:ens, ens:]
    conj = mm(inv_ref[...], norm)
    coupled = mm(mixed, conj)
    quad = mm(conj, mm(curv_ref[...], conj), TN)
    curv = symmetric(cross + coupled + coupled.T + quad)
    (step,) = eliminate([jnp.concatenate([curv, norm], axis=1)])
    step0 = step_ref[...]
    keep = step0 + step + mm(conj, step)
    coef_ref[...] = jnp.concatenate([keep.T, -mm(step0, step).T], axis=1)


def solve_first(grams):
    ens = grams.shape[1] // 2
    small = jax.ShapeDtypeStruct((ens, ens), f32)
    return pl.pallas_call(
        solve_first_kernel,
        out_shape=(small, small, small),
        in_specs=[vmem],
        out_specs=(vmem, vmem, vmem),
        name="solve_first",
    )(grams)


def solve_second(grams, step0, inv0, curv0):
    ens = step0.shape[0]
    return pl.pallas_call(
        solve_second_kernel,
        out_shape=jax.ShapeDtypeStruct((ens, 2 * ens), f32),
        in_specs=[vmem] * 4,
        out_specs=vmem,
        name="solve_second",
    )(grams, step0, inv0, curv0)


def final_kernel(count_ref, coef_ref, innov_ref, back_ref, rc_ref, rin_ref, ic_ref, iin_ref, w_ref, inc_ref):
    coef = coef_ref[...]
    ens = coef.shape[0]
    first, second = coef[:, :ens], coef[:, ens:]
    for g in range(innov_ref.shape[1] // ROWS):
        at = pl.ds(g * ROWS, ROWS)
        live = live_row(count_ref, g)
        w_ref[:, at] = combine(first, innov_ref[:, at] * live) + combine(second, back_ref[:, at])
    inc_ref[...] = combine(first, rc_ref[...] + rin_ref[...]) + combine(
        second, ic_ref[...] + iin_ref[...]
    )


def final_call(count, coef, innov, back, *cols):
    ens, own = innov.shape
    return pl.pallas_call(
        final_kernel,
        out_shape=(
            jax.ShapeDtypeStruct((ens, own), f32),
            jax.ShapeDtypeStruct((ens, COLS_DEV), f32),
        ),
        in_specs=[smem] + [vmem] * 7,
        out_specs=(vmem, vmem),
        compiler_params=params(),
        name="final",
    )(count, coef, innov, back, *cols)


def on_device(
    innovation,
    obs_along,
    obs_across,
    obs_scale,
    obs_error,
    obs_gain,
    pair_live,
    obs_count,
    col_owner,
):
    ens, own = innovation.shape
    rows = [x.reshape(1, own) for x in (obs_along, obs_across, obs_scale, obs_error)]
    gain, owner = obs_gain.reshape(1, own), col_owner.reshape(1, own)
    first, last, before, after, rank = sort_call(obs_count, pair_live, innovation, *rows)
    chunks = [before, first, last, after]
    imga, imgb, grams, *plan = first_call(chunks, ens, own)
    grams, img_before, img_after, back, ic, iin = join_first(grams, imga, imgb, rank, gain, owner)
    step0, inv0, curv0 = solve_first(grams)
    grams = second_call(plan, step0, chunks, [img_before, imga, imgb, img_after], ens, own)
    grams, rc, rin = join_second(obs_count, grams, innovation, gain, owner)
    coef = solve_second(grams, step0, inv0, curv0)
    return tuple(final_call(obs_count, coef, innovation, back, rc, rin, ic, iin))


def solution(mesh):
    one = P(("reg", "col"))
    in_specs = (P(None, ("reg", "col")), one, one, one, one, one, P(("reg", "col"), None), one, one)
    out_specs = (P(None, ("reg", "col")), P(None, ("reg", "col")))
    return jax.shard_map(
        on_device, mesh=mesh, in_specs=in_specs, out_specs=out_specs, check_vma=False
    )
```

```python
import functools

import jax
import jax.numpy as jnp
from jax import lax
from jax.experimental import pallas as pl
from jax.experimental.pallas import tpu as pltpu
from jax.sharding import PartitionSpec as P

ROWS = 1024
REACH = 2
COLS_DEV = 1024
TILE = 32
STEP = 16
PAIR = 4
PANEL = 8
EMPTY = ROWS // STEP
DEAD = 1e9
FAR = 1e6
VMEM_LIMIT = 24 * 1024 * 1024
SORT_LIMIT = 60 * 1024 * 1024
KEEP = 128

highest = lax.Precision.HIGHEST
f32 = jnp.float32
bf16 = jnp.bfloat16
NT = (((1,), (1,)), ((), ()))
NN = (((1,), (0,)), ((), ()))
TN = (((0,), (0,)), ((), ()))
vmem = pl.BlockSpec(memory_space=pltpu.VMEM)
smem = pl.BlockSpec(memory_space=pltpu.SMEM)
anywhere = pl.BlockSpec(memory_space=pl.ANY)


def shift(block, distance):
    axis = ("reg", "col")
    n = lax.axis_size(axis)
    return lax.ppermute(block, axis, [((i - distance) % n, i) for i in range(n)])


def dot(a, b, dims=NN):
    return lax.dot_general(a, b, dims, preferred_element_type=f32)


def two(x):
    hi = x.astype(bf16)
    return hi, (x - hi.astype(f32)).astype(bf16)


def three(x):
    hi = x.astype(bf16)
    rest = x - hi.astype(f32)
    mid = rest.astype(bf16)
    return hi, mid, (rest - mid.astype(f32)).astype(bf16)


def combine(coef_t, blocks):
    chi, clo = two(coef_t)
    bhi, blo = two(blocks)
    return dot(
        jnp.concatenate([chi, chi, clo], axis=1), jnp.concatenate([bhi, blo, bhi], axis=0)
    )


def params():
    return pltpu.CompilerParams(vmem_limit_bytes=VMEM_LIMIT)


def ring(total, n_col):
    me = lax.axis_index("reg") * n_col + lax.axis_index("col")
    left, right = (me + total - 1) % total, (me + 1) % total
    return me, (left // n_col, left % n_col), (right // n_col, right % n_col)


def send_to(src, dst, sems, k, device):
    return pltpu.make_async_remote_copy(
        src_ref=src,
        dst_ref=dst,
        send_sem=sems[0].at[k],
        recv_sem=sems[1].at[k],
        device_id=device,
        device_id_type=pl.DeviceIdType.MESH,
    )


def greet(devices):
    barrier = pltpu.get_barrier_semaphore()
    for device in devices:
        pl.semaphore_signal(barrier, inc=1, device_id=device, device_id_type=pl.DeviceIdType.MESH)


def live_row(count_ref, g):
    slot = lax.broadcasted_iota(jnp.int32, (1, ROWS), 1)
    return (slot < count_ref[g]).astype(f32)


def sort_kernel(
    count_ref,
    pair_ref,
    innov_ref,
    along_ref,
    across_ref,
    scale_ref,
    error_ref,
    first_ref,
    last_ref,
    rank_ref,
):
    regions = innov_ref.shape[1] // ROWS
    sub = lax.broadcasted_iota(jnp.int32, (128, 128), 0)
    lane = lax.broadcasted_iota(jnp.int32, (128, 128), 1)

    def sort_region(out_ref, shift_by, r, carry):
        g = shift_by + r
        cols = pl.ds(pl.multiple_of(g * ROWS, ROWS), ROWS)
        live = live_row(count_ref, g)
        across = across_ref[:, cols]
        key = jnp.where(live > 0.5, across, DEAD)
        flags = [jnp.full((1, ROWS), pair_ref[d, g], jnp.int32).astype(f32) for d in range(REACH)]
        meta = [along_ref[:, cols], across, scale_ref[:, cols] * live, error_ref[:, cols]]
        stack = jnp.concatenate(
            [innov_ref[:, cols] * live] + meta + flags + [key, jnp.zeros((1, ROWS), f32)], axis=0
        )
        key_col = jnp.broadcast_to(key, (128, ROWS)).T
        ranks = []
        for b in range(ROWS // 128):
            begin, end = b * 128, (b + 1) * 128
            mine = key[:, begin:end]
            other = key_col[begin:end]
            ahead = (other < mine) | ((other == mine) & (sub < lane))
            rank = jnp.sum(jnp.where(ahead, 1.0, 0.0), axis=0, keepdims=True)
            if b:
                ahead = jnp.where(key_col[:begin] <= mine, 1.0, 0.0)
                rank = rank + jnp.sum(ahead, axis=0, keepdims=True)
            if end < ROWS:
                ahead = jnp.where(key_col[end:] < mine, 1.0, 0.0)
                rank = rank + jnp.sum(ahead, axis=0, keepdims=True)
            ranks.append(rank)
        rank = jnp.concatenate(ranks, axis=1)
        rank_ref[:, cols] = jnp.broadcast_to(rank, (8, ROWS))
        lhs = jnp.concatenate(three(stack), axis=0)
        n = stack.shape[0]
        rank_i = rank.astype(jnp.int32)
        for c in range(ROWS // 256):
            slot = lax.broadcasted_iota(jnp.int32, (256, ROWS), 0) + c * 256
            place = (slot == rank_i).astype(f32).astype(bf16)
            got = dot(lhs, place, NT)
            at = pl.ds(pl.multiple_of(r * ROWS + c * 256, 256), 256)
            out_ref[:, at] = got[:n] + got[n : 2 * n] + got[2 * n :]
        return carry

    half = regions // 2
    lax.fori_loop(0, half, functools.partial(sort_region, first_ref, 0), 0)
    lax.fori_loop(0, half, functools.partial(sort_region, last_ref, half), 0)


def sizes():
    n_col = lax.axis_size("col")
    return lax.axis_size("reg") * n_col, n_col


def comm_params(which):
    return pltpu.CompilerParams(
        collective_id=which, has_side_effects=True, vmem_limit_bytes=VMEM_LIMIT
    )


def sort_call(count, pair, innov, *rows):
    ens, n = innov.shape
    half = jax.ShapeDtypeStruct((ens + 8, n // 2), f32)
    return pl.pallas_call(
        sort_kernel,
        out_shape=(half, half, jax.ShapeDtypeStruct((8, n), f32)),
        in_specs=[smem] * 2 + [vmem] * 5,
        out_specs=(vmem,) * 3,
        compiler_params=pltpu.CompilerParams(vmem_limit_bytes=SORT_LIMIT),
        name="sort_slots",
    )(count, pair, innov, *rows)


def lay_grid(chunks, offsets, row_ref, grid_ref):
    width = chunks[0].shape[1]
    per = width // ROWS
    blocks = ROWS // 128
    grid_ref[...] = jnp.full(grid_ref.shape, FAR, f32)
    for c, ref in enumerate(chunks):
        row_ref[:, c * width : (c + 1) * width] = ref[ref.shape[0] - 8 :, :]
        for r in range(per):
            h = c * per + r
            at = slice(h * ROWS, (h + 1) * ROWS)
            row_ref[0:1, at] = row_ref[0:1, at] + float(offsets[h])
            for q, source in enumerate((0, 1, 6)):
                for b in range(blocks):
                    line = h * (blocks + 1) + b
                    begin = h * ROWS + b * 128
                    grid_ref[q, line : line + 1, :] = row_ref[source : source + 1, begin : begin + 128]


def lay_tables(grid_ref, regions, table_refs):
    count = regions * (ROWS // 128 + 1)
    ways = 128 // STEP
    lane = lax.broadcasted_iota(jnp.int32, (count, 128), 1)
    for q in range(2):
        here = grid_ref[q, :count, :]
        later = grid_ref[q, 1 : count + 1, :]
        table_refs[q][pl.ds(0, count, stride=ways), :] = here
        for k in range(1, ways):
            joined = jnp.where(lane < k * STEP, later, here)
            table_refs[q][pl.ds(k, count, stride=ways), :] = pltpu.roll(joined, 128 - k * STEP, 1)


def spread_rows(grid_ref, spread_refs):
    blocks = ROWS // 128
    regions = spread_refs[0].shape[0] // ROWS
    count = regions * (blocks + 1)
    for q in range(2):
        turned = jnp.concatenate(
            [grid_ref[q, :count, :], jnp.zeros((128 - count, 128), f32)], axis=0
        ).T
        for g in range(regions):
            for b in range(blocks):
                line = g * (blocks + 1) + b
                begin = g * ROWS + b * 128
                spread_refs[q][begin : begin + 128, :] = jnp.broadcast_to(
                    turned[:, line : line + 1], (128, 128)
                )


def own_pairs(regions):
    near = range(-REACH, REACH + 1)
    return [[(g + d, d) for d in near if 0 <= g + d < regions] for g in range(regions)]


def halo_pairs(regions):
    found = []
    for g in range(regions):
        mine = [(g + d + REACH, d) for d in range(-REACH, 0) if g + d < 0]
        mine += [(g + d - regions + REACH, d) for d in range(1, REACH + 1) if g + d >= regions]
        found.append(mine)
    return found


def widest(pairs):
    return max(len(mine) for mine in pairs)


def plan_windows(pairs, row_ref, grid_ref, row_i_ref, grid_i_ref, span_ref, item_ref):
    blocks = ROWS // 128
    regions = len(pairs)
    per = ROWS // TILE
    tiles = regions * per
    ways = 128 // STEP
    slots = widest(pairs)

    def keys_of(ref, count):
        return [ref[2, h * (blocks + 1) : h * (blocks + 1) + blocks, :] for h in range(count)]

    mine = jnp.concatenate(keys_of(grid_i_ref, regions), axis=0)
    top = jnp.where(mine < 0.5 * DEAD, mine, -DEAD)
    size = 1
    while size < TILE:
        top = jnp.maximum(top, pltpu.roll(top, 128 - size, 1))
        size *= 2
    parts = 128 // TILE
    lines = regions * blocks
    tile = lax.broadcasted_iota(jnp.int32, (lines, tiles), 1)
    line = lax.broadcasted_iota(jnp.int32, (lines, tiles), 0)
    first = jnp.zeros((1, tiles), f32)
    last = jnp.zeros((1, tiles), f32)
    for p in range(parts):
        here = tile == line * parts + p
        lane = slice(p * TILE, p * TILE + 1)
        first = first + jnp.sum(
            jnp.where(here, jnp.broadcast_to(mine[:, lane], (lines, tiles)), 0.0), axis=0, keepdims=True
        )
        last = last + jnp.sum(
            jnp.where(here, jnp.broadcast_to(top[:, lane], (lines, tiles)), 0.0), axis=0, keepdims=True
        )
    under, over = first - 1.001, last + 1.001
    begins, ends = [], []
    for key in keys_of(grid_ref, row_ref.shape[1] // ROWS):
        begin = jnp.zeros((blocks, tiles), f32)
        end = jnp.zeros((blocks, tiles), f32)
        for k in range(ways):
            low = jnp.broadcast_to(key[:, k * STEP : k * STEP + 1], (blocks, tiles))
            high = jnp.broadcast_to(key[:, (k + 1) * STEP - 1 : (k + 1) * STEP], (blocks, tiles))
            begin = begin + jnp.where(high < under, 1.0, 0.0)
            end = end + jnp.where(low <= over, 1.0, 0.0)
        begins.append(jnp.sum(begin, axis=0, keepdims=True))
        ends.append(jnp.sum(end, axis=0, keepdims=True))
    group = lax.broadcasted_iota(jnp.int32, (1, tiles), 1) // per
    alive = first < 0.5 * DEAD
    starts, stops = [], []
    needs = jnp.zeros((1, tiles), f32)
    for slot in range(slots):
        start = jnp.zeros((1, tiles), f32)
        stop = jnp.zeros((1, tiles), f32)
        for g, mine in enumerate(pairs):
            if slot >= len(mine):
                continue
            j, d = mine[slot]
            base = float(j * (ROWS + 128) // STEP)
            begin, end = begins[j] + base, ends[j] + base
            if d:
                source = 3 + abs(d)
                owner, holder = (g, row_i_ref) if d > 0 else (j, row_ref)
                flag = holder[source : source + 1, owner * ROWS : owner * ROWS + 128]
                end = jnp.where(flag[:, :tiles] > 0.5, end, begin)
            start = jnp.where(group == g, begin, start)
            stop = jnp.where(group == g, end, stop)
        stop = jnp.where(alive, jnp.maximum(stop, start), start)
        needs = jnp.maximum(needs, jnp.floor((stop - start + (ways - 1.0)) * (1.0 / ways)))
        starts.append(start)
        stops.append(stop)
    blank = jnp.full((8 - slots, tiles), float(EMPTY), f32)
    for m in range(blocks + 1):
        lines_m = [
            jnp.where(start + float(ways * m) < stop, start + float(ways * m), float(EMPTY))
            for start, stop in zip(starts, stops)
        ]
        span_ref[8 * m : 8 * m + 8, :] = jnp.concatenate(lines_m + [blank], axis=0).astype(jnp.int32)
    row = lax.broadcasted_iota(jnp.int32, (tiles, tiles), 0)
    col = lax.broadcasted_iota(jnp.int32, (tiles, tiles), 1)
    many = jnp.broadcast_to(needs, (tiles, tiles)).astype(bf16)
    done = dot((col <= row).astype(f32).astype(bf16), many, NT)
    each = dot((col == row).astype(f32).astype(bf16), many, NT)
    total = jnp.max(done, axis=0, keepdims=True)
    for k in range(item_ref.shape[1]):
        slot = lax.broadcasted_iota(jnp.int32, (1, tiles), 1).astype(f32) + float(k * tiles)
        past = done <= slot
        at = jnp.sum(jnp.where(past, 1.0, 0.0), axis=0, keepdims=True)
        began = jnp.sum(jnp.where(past, each, 0.0), axis=0, keepdims=True)
        spare = slot >= total
        item_ref[0, k : k + 1, :] = jnp.where(spare, 0.0, at).astype(jnp.int32)
        item_ref[1, k : k + 1, :] = jnp.where(spare, float(blocks), slot - began).astype(jnp.int32)
        item_ref[2, k : k + 1, :] = total.astype(jnp.int32)


def turn_vectors(v_ref, row_ref, turn_ref):
    ens, wide = v_ref.shape
    padded = ROWS + 128
    row = lax.broadcasted_iota(jnp.int32, (256, 256), 0)
    eye = (row == lax.broadcasted_iota(jnp.int32, (256, 256), 1)).astype(f32).astype(bf16)
    for h in range(wide // ROWS):
        for b in range(ROWS // 256):
            at = slice(h * ROWS + b * 256, h * ROWS + (b + 1) * 256)
            stack = jnp.concatenate(two(v_ref[:, at] * row_ref[2:3, at]), axis=0)
            begin = h * padded + b * 256
            turn_ref[begin : begin + 256, :] = dot(eye, stack, NT).astype(bf16)
        turn_ref[h * padded + ROWS : (h + 1) * padded, :] = jnp.zeros((128, 2 * ens), bf16)


def windows(work, n, slots):
    line, lane = lax.shift_right_logical(n, jnp.int32(7)), lax.bitwise_and(n, jnp.int32(127))
    tile = work["item"][0, line, lane]
    level = work["item"][1, line, lane] * 8
    return [tile] + [work["span"][level + slot, tile] for slot in range(slots)]


def gather(work, cov, where_to):
    tile, *found = where_to
    turn_ref = work["turn"]
    rhs = jnp.concatenate(
        [turn_ref[pl.ds(pl.multiple_of(w * STEP, STEP), 128), :] for w in found], axis=0
    )
    got = dot(cov, rhs)
    at = pl.ds(pl.multiple_of(tile * TILE, TILE), TILE)
    work["sum"][at, :] += got[:TILE] + got[TILE:]


def count_trips(work):
    return lax.shift_right_logical(
        work["item"][2, 0, 0] + (PAIR - 1), jnp.int32(PAIR.bit_length() - 1)
    )


def apply_cov(work, s_ref, keep, begin):
    slots = s_ref.shape[2] // 128
    s_ref[keep : keep + PAIR] = jnp.zeros((PAIR,) + s_ref.shape[1:], bf16)

    def place(k):
        return jnp.where(k < keep // PAIR, k * PAIR, keep)

    def step(k, carry):
        before = jnp.where(k == begin, keep, place(k - 1))
        for p in range(PAIR):
            gather(work, s_ref[before + p], carry[p])
        now = [windows(work, k * PAIR + p, slots) for p in range(PAIR)]
        after = place(k)
        for p in range(PAIR):
            tile, *found = now[p]
            at = pl.ds(pl.multiple_of(tile * TILE, TILE), TILE)
            a_i = work["along_i"][at, :]
            b_i = work["across_i"][at, :]
            for d, w in enumerate(found):
                da = work["along"][pl.ds(w, 1), :] - a_i
                db = work["across"][pl.ds(w, 1), :] - b_i
                r2 = da * da + db * db
                r = r2 * lax.rsqrt(jnp.maximum(r2, 1e-30))
                u = jnp.maximum(1.0 - r, 0.0)
                u2 = u * u
                hi, lo = two((u2 * u2) * (r + 0.25))
                s_ref[after + p, 0:TILE, d * 128 : (d + 1) * 128] = hi
                s_ref[after + p, TILE : 2 * TILE, d * 128 : (d + 1) * 128] = lo
        return now

    trips = count_trips(work)
    end = jnp.where(trips > begin, trips + 1, begin)
    lax.fori_loop(begin, end, step, [windows(work, p, slots) for p in range(PAIR)])


def apply_kept(work, kept_ref, ring_ref):
    slots = kept_ref.shape[2] // 128
    most = KEEP // PAIR

    def step(k, carry):
        for p in range(PAIR):
            gather(work, kept_ref[k * PAIR + p], windows(work, k * PAIR + p, slots))
        return carry

    lax.fori_loop(0, jnp.minimum(count_trips(work), most), step, 0)
    apply_cov(work, ring_ref, 0, most)


def finish(sum_ref, base_ref, row_ref, v_ref, img_ref):
    ens, own = img_ref.shape
    for c in range(own // 128):
        at = slice(c * 128, (c + 1) * 128)
        turned = (sum_ref[at, :] + base_ref[at, :]).T
        img_ref[:, at] = (
            (turned[:ens] + turned[ens:]) * (row_ref[2:3, at] * 0.25) + row_ref[3:4, at] * v_ref[:, at]
        )


def gram(a, b):
    ahi, alo = two(a)
    bhi, blo = two(b)
    return dot(
        jnp.concatenate([ahi, ahi, alo], axis=1), jnp.concatenate([bhi, blo, bhi], axis=1), NT
    )


def square(n):
    return lax.broadcasted_iota(jnp.int32, (n, n), 0), lax.broadcasted_iota(jnp.int32, (n, n), 1)


def pack_pair(upper, lower):
    n = upper.shape[0]
    row, col = square(n)
    upper, lower = symmetric(upper), symmetric(lower)
    spare = jnp.sum(jnp.where(row == col, lower, 0.0), axis=0, keepdims=True)
    return jnp.where(col >= row, upper, lower), jnp.broadcast_to(spare, (8, n))


def unpack_pair(packed, spare):
    n = packed.shape[0]
    row, col = square(n)
    other = packed.T
    lower = jnp.where(row == col, jnp.broadcast_to(spare, (n, n)), jnp.where(col > row, other, packed))
    return jnp.where(col >= row, packed, other), lower


def start_plan(span_in, item_in, work):
    copies = [
        pltpu.make_async_copy(span_in, work["span"], work["plan_sem"].at[0]),
        pltpu.make_async_copy(item_in, work["item"], work["plan_sem"].at[1]),
    ]
    for copy in copies:
        copy.start()
    return copies


def multiply(copies, work, kept_ref=None):
    turn_vectors(work["v"], work["row"], work["turn"])
    work["sum"][...] = jnp.zeros_like(work["sum"])
    for copy in copies:
        copy.wait()
    if kept_ref is None:
        apply_cov(work, work["s"], KEEP, 0)
    else:
        apply_kept(work, kept_ref, work["ring"])


def lay_own(first_ref, last_ref, work):
    regions = first_ref.shape[1] * 2 // ROWS
    lay_grid([first_ref, last_ref], range(regions), work["row"], work["grid"])
    spread_rows(work["grid"], (work["along_i"], work["across_i"]))
    lay_tables(work["grid"], regions, (work["along"], work["across"]))


def lay_halo(before_ref, after_ref, first_ref, last_ref, work):
    regions = first_ref.shape[1] * 2 // ROWS
    offsets = list(range(-REACH, 0)) + list(range(regions, regions + REACH))
    lay_grid([first_ref, last_ref], range(regions), work["row_i"], work["grid_i"])
    lay_grid([before_ref, after_ref], offsets, work["row"], work["grid"])
    lay_tables(work["grid"], 2 * REACH, (work["along"], work["across"]))


def take_rows(chunks, row_ref):
    width = chunks[0].shape[1]
    for c, ref in enumerate(chunks):
        row_ref[:, c * width : (c + 1) * width] = ref[ref.shape[0] - 8 :, :]


def first_own_kernel(
    names, first_ref, last_ref, sum_out, span_out, item_out, along_out, across_out, along_i_out, across_i_out, s_out, *refs
):
    work = dict(zip(names, refs))
    work.update(along=along_out, across=across_out, along_i=along_i_out, across_i=across_i_out)
    work.update(sum=sum_out, s=s_out)
    ens = work["v"].shape[0]
    lead = first_ref.shape[1]
    lay_own(first_ref, last_ref, work)
    pairs = own_pairs(2 * lead // ROWS)
    plan_windows(pairs, work["row"], work["grid"], work["row"], work["grid"], span_out, item_out)
    copies = start_plan(span_out, item_out, work)
    work["v"][:, :lead] = first_ref[:ens, :]
    work["v"][:, lead:] = last_ref[:ens, :]
    multiply(copies, work)


def first_halo_kernel(
    names,
    before_ref,
    after_ref,
    first_ref,
    last_ref,
    base_ref,
    along_i_ref,
    across_i_ref,
    imga_ref,
    imgb_ref,
    gram_ref,
    span_out,
    item_out,
    along_out,
    across_out,
    s_out,
    *refs,
):
    work = dict(zip(names, refs))
    work.update(along=along_out, across=across_out, along_i=along_i_ref, across_i=across_i_ref, s=s_out)
    ens = work["v"].shape[0]
    lead = first_ref.shape[1]
    lay_halo(before_ref, after_ref, first_ref, last_ref, work)
    pairs = halo_pairs(2 * lead // ROWS)
    plan_windows(pairs, work["row"], work["grid"], work["row_i"], work["grid_i"], span_out, item_out)
    copies = start_plan(span_out, item_out, work)
    work["v"][:, :lead] = before_ref[:ens, :]
    work["v"][:, lead:] = after_ref[:ens, :]
    multiply(copies, work)
    work["v"][:, :lead] = first_ref[:ens, :]
    work["v"][:, lead:] = last_ref[:ens, :]
    img_ref = work["img"]
    finish(work["sum"], base_ref, work["row_i"], work["v"], img_ref)
    imga_ref[...] = img_ref[:, :lead]
    imgb_ref[...] = img_ref[:, lead:]
    r = work["v"][...]
    both = gram(r, jnp.concatenate([r, img_ref[...]], axis=0))
    packed, spare = pack_pair(both[:, :ens], both[:, ens:])
    half = ens // 2
    gram_ref[0:half, :] = jnp.concatenate([packed[:half], packed[half:]], axis=1)
    gram_ref[half : half + 8, :] = jnp.concatenate([spare, spare], axis=1)


def second_own_kernel(
    names,
    span_in,
    item_in,
    gram_ref,
    first_ref,
    last_ref,
    imga_ref,
    imgb_ref,
    along_ref,
    across_ref,
    along_i_ref,
    across_i_ref,
    kept_ref,
    sum_out,
    rest_out,
    step_out,
    inv_out,
    curv_out,
    *refs,
):
    work = dict(zip(names, refs))
    work.update(along=along_ref, across=across_ref, along_i=along_i_ref, across_i=across_i_ref)
    work.update(sum=sum_out, v=rest_out)
    ens = step_out.shape[0]
    lead = first_ref.shape[1]
    copies = start_plan(span_in, item_in, work)
    take_rows([first_ref, last_ref], work["row"])
    solve_first(gram_ref, step_out, inv_out, curv_out)
    step_t = step_out[...].T
    rest_out[:, :lead] = first_ref[:ens, :] - combine(step_t, imga_ref[...])
    rest_out[:, lead:] = last_ref[:ens, :] - combine(step_t, imgb_ref[...])
    multiply(copies, work, kept_ref)


def second_halo_kernel(
    names,
    span_in,
    item_in,
    step_ref,
    before_ref,
    after_ref,
    img_before_ref,
    img_after_ref,
    first_ref,
    last_ref,
    rest_ref,
    imga_ref,
    imgb_ref,
    base_ref,
    along_ref,
    across_ref,
    along_i_ref,
    across_i_ref,
    kept_ref,
    gram_ref,
    *refs,
):
    work = dict(zip(names, refs))
    work.update(along=along_ref, across=across_ref, along_i=along_i_ref, across_i=across_i_ref)
    ens = step_ref.shape[0]
    lead = before_ref.shape[1]
    copies = start_plan(span_in, item_in, work)
    take_rows([first_ref, last_ref], work["row_i"])
    take_rows([before_ref, after_ref], work["row"])
    step_t = step_ref[...].T
    work["v"][:, :lead] = before_ref[:ens, :] - combine(step_t, img_before_ref[...])
    work["v"][:, lead:] = after_ref[:ens, :] - combine(step_t, img_after_ref[...])
    multiply(copies, work, kept_ref)
    img_ref = work["img"]
    finish(work["sum"], base_ref, work["row_i"], rest_ref, img_ref)
    r = rest_ref[...]
    both = gram(r, jnp.concatenate([r, img_ref[...]], axis=0))
    mixed = gram(r, jnp.concatenate([imga_ref[...], imgb_ref[...]], axis=1))
    packed, spare = pack_pair(both[:, :ens], both[:, ens:])
    gram_ref[0:ens, :] = jnp.concatenate([packed, mixed], axis=1)
    gram_ref[ens : ens + 8, :] = jnp.concatenate([spare, spare], axis=1)


def plan_shapes(own):
    tiles = own // TILE
    most = tiles * (ROWS // 128)
    return (8 * (ROWS // 128 + 1), tiles), (3, most // 128 + 1, 128)


def plan_out(own):
    return tuple(jax.ShapeDtypeStruct(shape, jnp.int32) for shape in plan_shapes(own))


def table_shapes(own, halo):
    near = 2 * REACH if halo else own // ROWS
    slots = widest((halo_pairs if halo else own_pairs)(own // ROWS))
    table = jax.ShapeDtypeStruct((128 // STEP * near * (ROWS // 128 + 1), 128), f32)
    kept = jax.ShapeDtypeStruct((KEEP + PAIR, 2 * TILE, slots * 128), bf16)
    return (table, table), (kept,)


def scratch(ens, own, halo, again):
    regions = own // ROWS
    near = 2 * REACH if halo else regions
    slots = widest((halo_pairs if halo else own_pairs)(regions))

    def grid(count):
        return pltpu.VMEM((3, -(-(count * (ROWS // 128 + 1) + 1) // 8) * 8, 128), f32)

    spans, items = plan_shapes(own)
    shapes = {
        "span": pltpu.SMEM(spans, jnp.int32),
        "item": pltpu.SMEM(items, jnp.int32),
        "plan_sem": pltpu.SemaphoreType.DMA((2,)),
        "row": pltpu.VMEM((8, near * ROWS), f32),
        "turn": pltpu.VMEM((near * (ROWS + 128), 2 * ens), bf16),
    }
    if not again:
        shapes["grid"] = grid(near)
    if again:
        shapes["ring"] = pltpu.VMEM((PAIR, 2 * TILE, slots * 128), bf16)
    if halo:
        shapes["row_i"] = pltpu.VMEM((8, own), f32)
        shapes["grid_i"] = grid(regions)
        shapes["img"] = pltpu.VMEM((ens, own), f32)
        shapes["sum"] = pltpu.VMEM((own, 128), f32)
    if halo or not again:
        shapes["v"] = pltpu.VMEM((ens, near * ROWS), f32)
    return tuple(shapes), list(shapes.values())


def operate(kernel, name, kind, args, outs, ens, own):
    names, shapes = scratch(ens, own, *kind)
    return pl.pallas_call(
        functools.partial(kernel, names),
        out_shape=outs,
        in_specs=[vmem] * len(args),
        out_specs=(vmem,) * len(outs),
        scratch_shapes=shapes,
        compiler_params=params(),
        cost_estimate=pl.CostEstimate(flops=10**10, bytes_accessed=4 << 20, transcendentals=0),
        name=name,
    )(*args)


def first_own_call(first, last, ens, own):
    tables, kept = table_shapes(own, False)
    spread = jax.ShapeDtypeStruct((own, 128), f32)
    outs = (spread,) + plan_out(own) + tables + (spread, spread) + kept
    return operate(first_own_kernel, "first_own", (False, False), (first, last), outs, ens, own)


def first_halo_call(chunks, base, spreads, ens, own):
    tables, kept = table_shapes(own, True)
    half = jax.ShapeDtypeStruct((ens, own // 2), f32)
    outs = (half, half, jax.ShapeDtypeStruct((ens // 2 + 8, 2 * ens), f32))
    outs += plan_out(own) + tables + kept
    args = (*chunks, base, *spreads)
    return operate(first_halo_kernel, "first_halo", (True, False), args, outs, ens, own)


def second_own_call(plan, grams, first, last, imga, imgb, laid, ens, own):
    small = jax.ShapeDtypeStruct((ens, ens), f32)
    outs = (jax.ShapeDtypeStruct((own, 2 * ens), f32), jax.ShapeDtypeStruct((ens, own), f32))
    args = (*plan, grams, first, last, imga, imgb, *laid)
    return operate(second_own_kernel, "second_own", (False, True), args, outs + (small,) * 3, ens, own)


def second_halo_call(plan, step, before, after, images, first, last, rest, mine, base, laid, ens, own):
    args = (*plan, step, before, after, *images, first, last, rest, *mine, base, *laid)
    outs = (jax.ShapeDtypeStruct((ens + 8, 2 * ens), f32),)
    return operate(second_halo_kernel, "second_halo", (True, True), args, outs, ens, own)[0]


def flip(me, size):
    return size * (1 - 2 * ((me // size) % 2))


def exchange_steps(total):
    bits = total.bit_length() - 1
    steps = [[1]] if bits % 2 else []
    for k in range(bits % 2, bits, 2):
        steps.append([2**k, 2 ** (k + 1)])
    return steps


def partners_of(steps, n_col, me):
    found = []
    for amounts in steps:
        others = [me + flip(me, size) for size in amounts]
        if len(amounts) == 2:
            others.append(others[0] + flip(me, amounts[1]))
        found.append([(other // n_col, other % n_col) for other in others])
    return found


def sum_all(partners, x_ref, send, recv, sems, work):
    total = x_ref[...]
    slot = 0
    for k, group in enumerate(partners):
        if k:
            send[k] = total
        source = send.at[k] if k else x_ref
        copies = [
            send_to(source, recv.at[slot + p], sems, slot + p, other) for p, other in enumerate(group)
        ]
        for copy in copies:
            copy.start()
        if k < len(work):
            work[k]()
        for copy in copies:
            copy.wait()
        total = total + recv[slot]
        if len(group) == 3:
            total = total + (recv[slot + 1] + recv[slot + 2])
        slot += len(group)
    for piece in work[len(partners) :]:
        piece()
    return total


def local_column(owner, me, total):
    local = owner - me * COLS_DEV
    return jnp.where(local < 0, local + total * COLS_DEV, local)


def add_columns(scaled_ref, owner_ref, me, total, base, target_ref):
    own = owner_ref.shape[1]

    def one(c, carry):
        got = jnp.zeros((scaled_ref.shape[0], 256), f32)
        for g in range(own // ROWS):
            at = slice(g * ROWS, (g + 1) * ROWS)
            slot = lax.broadcasted_iota(jnp.int32, (256, ROWS), 0) + (base + c * 256)
            owner = local_column(owner_ref[:, at], me, total)
            hot = (slot == owner).astype(f32).astype(bf16)
            got = got + dot(scaled_ref[:, at], hot, NT)
        ens = target_ref.shape[0]
        target_ref[:, pl.ds(pl.multiple_of(c * 256, 256), 256)] = got[:ens] + got[ens:]
        return carry

    lax.fori_loop(0, COLS_DEV // 256, one, 0)


def join_first_kernel(
    steps,
    total,
    n_col,
    x_ref,
    imga_ref,
    imgb_ref,
    rank_ref,
    gain_ref,
    owner_ref,
    out_ref,
    back_ref,
    cols_ref,
    edge_ref,
    scaled_ref,
    send,
    recv,
    send_sem,
    recv_sem,
):
    ens, half = imga_ref.shape
    me = lax.axis_index("reg") * n_col + lax.axis_index("col")
    partners = partners_of(steps, n_col, me)
    everyone = [other for group in partners for other in group]
    greet(everyone)
    pl.semaphore_wait(pltpu.get_barrier_semaphore(), len(everyone))

    def unsort():
        for k, img_ref in enumerate((imga_ref, imgb_ref)):

            def one(r, carry, k=k, img_ref=img_ref):
                at = pl.ds(pl.multiple_of(k * half + r * ROWS, ROWS), ROWS)
                rank = rank_ref[0:1, at].astype(jnp.int32)
                mine = img_ref[:, pl.ds(pl.multiple_of(r * ROWS, ROWS), ROWS)]
                lhs = jnp.concatenate(two(mine), axis=0)
                got = jnp.zeros((2 * ens, ROWS), f32)
                for c in range(ROWS // 256):
                    slot = lax.broadcasted_iota(jnp.int32, (256, ROWS), 0) + c * 256
                    place = (slot == rank).astype(f32).astype(bf16)
                    got = got + dot(lhs[:, c * 256 : (c + 1) * 256], place)
                image = got[:ens] + got[ens:]
                back_ref[:, at] = image
                scaled_ref[:, at] = jnp.concatenate(two(image * gain_ref[:, at]), axis=0)
                return carry

            lax.fori_loop(0, half // ROWS, one, 0)

    def outer():
        add_columns(scaled_ref, owner_ref, me, total, COLS_DEV, edge_ref)

    def inner():
        add_columns(scaled_ref, owner_ref, me, total, 0, cols_ref)

    out_ref[...] = sum_all(partners, x_ref, send, recv, (send_sem, recv_sem), [unsort, outer, inner])


def join_second_kernel(
    steps,
    total,
    n_col,
    count_ref,
    x_ref,
    innov_ref,
    gain_ref,
    owner_ref,
    out_ref,
    cols_ref,
    came_ref,
    scaled_ref,
    send,
    recv,
    send_sem,
    recv_sem,
    edge_ref,
    bulk_send_sem,
    bulk_recv_sem,
):
    own = innov_ref.shape[1]
    me, left, right = ring(total, n_col)
    partners = partners_of(steps, n_col, me)
    everyone = [other for group in partners for other in group] + [left, right]
    greet(everyone)
    pl.semaphore_wait(pltpu.get_barrier_semaphore(), len(everyone))
    edge = send_to(edge_ref, came_ref, (bulk_send_sem, bulk_recv_sem), 0, right)

    def scale():
        def one(g, carry):
            at = pl.ds(pl.multiple_of(g * ROWS, ROWS), ROWS)
            factor = gain_ref[:, at] * live_row(count_ref, g)
            scaled_ref[:, at] = jnp.concatenate(two(innov_ref[:, at] * factor), axis=0)
            return carry

        lax.fori_loop(0, own // ROWS, one, 0)

    def outer():
        add_columns(scaled_ref, owner_ref, me, total, COLS_DEV, edge_ref)

    def inner():
        edge.start()
        add_columns(scaled_ref, owner_ref, me, total, 0, cols_ref)

    out_ref[...] = sum_all(partners, x_ref, send, recv, (send_sem, recv_sem), [scale, outer, inner])
    edge.wait()


def join_scratch(steps, shape, ens, own):
    slots = sum(2 ** len(amounts) - 1 for amounts in steps)
    return [
        pltpu.VMEM((2 * ens, own), bf16),
        pltpu.VMEM((len(steps),) + shape, f32),
        pltpu.VMEM((slots,) + shape, f32),
        pltpu.SemaphoreType.DMA((slots,)),
        pltpu.SemaphoreType.DMA((slots,)),
    ]


def join_first(x, imga, imgb, rank, gain, owner):
    ens, half = imga.shape
    total, n_col = sizes()
    steps = exchange_steps(total)
    cols = jax.ShapeDtypeStruct((ens, COLS_DEV), f32)
    return pl.pallas_call(
        functools.partial(join_first_kernel, steps, total, n_col),
        out_shape=(
            jax.ShapeDtypeStruct(x.shape, f32),
            jax.ShapeDtypeStruct((ens, 2 * half), f32),
            cols,
            cols,
        ),
        in_specs=[vmem] * 6,
        out_specs=(vmem,) * 4,
        scratch_shapes=join_scratch(steps, x.shape, ens, 2 * half),
        compiler_params=comm_params(1),
        name="join_first",
    )(x, imga, imgb, rank, gain, owner)


def join_second(count, x, innov, gain, owner):
    ens, own = innov.shape
    total, n_col = sizes()
    steps = exchange_steps(total)
    cols = jax.ShapeDtypeStruct((ens, COLS_DEV), f32)
    return pl.pallas_call(
        functools.partial(join_second_kernel, steps, total, n_col),
        out_shape=(jax.ShapeDtypeStruct(x.shape, f32), cols, cols),
        in_specs=[smem] + [vmem] * 4,
        out_specs=(vmem, vmem, anywhere),
        scratch_shapes=join_scratch(steps, x.shape, ens, own)
        + [
            pltpu.VMEM((ens, COLS_DEV), f32),
            pltpu.SemaphoreType.DMA((1,)),
            pltpu.SemaphoreType.DMA((1,)),
        ],
        compiler_params=comm_params(2),
        name="join_second",
    )(count, x, innov, gain, owner)


def symmetric(matrix):
    return 0.5 * (matrix + matrix.T)


def mm(a, b, dims=NN):
    return lax.dot_general(a, b, dims, precision=highest, preferred_element_type=f32)


def eliminate(chains):
    ens, both = chains[0].shape
    parts = range(ens // 8)
    rows = lax.broadcasted_iota(jnp.int32, (8, both), 0)
    chains = [[m[8 * i : 8 * i + 8] for i in parts] for m in chains]

    def clear(parts_of, col, pivot, at):
        done = [x - c * pivot for x, c in zip(parts_of, col)]
        done[at // 8] = jnp.where(rows == at % 8, pivot, done[at // 8])
        return done

    for k in range(0, ens, PANEL):
        columns = [
            [[jnp.broadcast_to(x[:, k + j : k + j + 1], (8, both)) for x in m] for j in range(PANEL)]
            for m in chains
        ]
        for p in range(PANEL):
            at = k + p
            one = slice(at % 8, at % 8 + 1)
            done = []
            for m, cols in zip(chains, columns):
                col = cols[p]
                scale = 1.0 / col[at // 8][one]
                for j in range(p + 1, PANEL):
                    cols[j] = clear(cols[j], col, cols[j][at // 8][one] * scale, at)
                done.append(clear(m, col, m[at // 8][one] * scale, at))
            chains = done
    return [jnp.concatenate(m, axis=0)[:, ens:] for m in chains]


def solve_first(gram_ref, step_ref, inv_ref, curv_ref):
    ens = step_ref.shape[0]
    half = ens // 2
    packed = jnp.concatenate([gram_ref[0:half, :ens], gram_ref[0:half, ens:]], axis=0)
    norm, curv = unpack_pair(packed, gram_ref[half : half + 1, :ens])
    row, col = square(ens)
    eye = (row == col).astype(f32)
    step, inv = eliminate(
        [jnp.concatenate([curv, norm], axis=1), jnp.concatenate([norm, eye], axis=1)]
    )
    step_ref[...] = step
    inv_ref[...] = inv
    curv_ref[...] = curv


def solve_second(gram_ref, step_ref, inv_ref, curv_ref):
    ens = step_ref.shape[0]
    norm, cross = unpack_pair(gram_ref[0:ens, :ens], gram_ref[ens : ens + 1, :ens])
    mixed = gram_ref[0:ens, ens:]
    conj = mm(inv_ref[...], norm)
    coupled = mm(mixed, conj)
    quad = mm(conj, mm(curv_ref[...], conj), TN)
    curv = symmetric(cross + coupled + coupled.T + quad)
    (step,) = eliminate([jnp.concatenate([curv, norm], axis=1)])
    step0 = step_ref[...]
    keep = step0 + step + mm(conj, step)
    return keep.T, -mm(step0, step).T


def final_kernel(
    count_ref, gram_ref, step_ref, inv_ref, curv_ref, innov_ref, back_ref, rc_ref, rin_ref, ic_ref, iin_ref, w_ref, inc_ref
):
    first, second = solve_second(gram_ref, step_ref, inv_ref, curv_ref)
    for g in range(innov_ref.shape[1] // ROWS):
        at = pl.ds(g * ROWS, ROWS)
        live = live_row(count_ref, g)
        w_ref[:, at] = combine(first, innov_ref[:, at] * live) + combine(second, back_ref[:, at])
    inc_ref[...] = combine(first, rc_ref[...] + rin_ref[...]) + combine(
        second, ic_ref[...] + iin_ref[...]
    )


def final_call(count, solved, innov, back, *cols):
    ens, own = innov.shape
    return pl.pallas_call(
        final_kernel,
        out_shape=(
            jax.ShapeDtypeStruct((ens, own), f32),
            jax.ShapeDtypeStruct((ens, COLS_DEV), f32),
        ),
        in_specs=[smem] + [vmem] * 10,
        out_specs=(vmem, vmem),
        compiler_params=params(),
        name="final",
    )(count, *solved, innov, back, *cols)


def on_device(
    innovation,
    obs_along,
    obs_across,
    obs_scale,
    obs_error,
    obs_gain,
    pair_live,
    obs_count,
    col_owner,
):
    ens, own = innovation.shape
    rows = [x.reshape(1, own) for x in (obs_along, obs_across, obs_scale, obs_error)]
    gain, owner = obs_gain.reshape(1, own), col_owner.reshape(1, own)
    first, last, rank = sort_call(obs_count, pair_live.T, innovation, *rows)
    after, before = shift(first, -1), shift(last, 1)
    base, *rest = first_own_call(first, last, ens, own)
    plan_own, laid_own = rest[:2], rest[2:]
    spreads = laid_own[2:4]
    chunks = [before, after, first, last]
    imga, imgb, grams, *rest = first_halo_call(chunks, base, spreads, ens, own)
    plan_halo, laid_halo = rest[:2], rest[2:4] + spreads + rest[4:]
    grams, back, ic, edge = join_first(grams, imga, imgb, rank, gain, owner)
    senda, sendb, grams = lax.optimization_barrier((imga, imgb, grams))
    img_after, img_before = shift(senda, -1), shift(sendb, 1)
    iin = shift(edge, 1)
    base, rest, step0, inv0, curv0 = second_own_call(plan_own, grams, first, last, imga, imgb, laid_own, ens, own)
    images = [img_before, img_after]
    grams = second_halo_call(
        plan_halo, step0, before, after, images, first, last, rest, [imga, imgb], base, laid_halo, ens, own
    )
    grams, rc, rin = join_second(obs_count, grams, innovation, gain, owner)
    solved = (grams, step0, inv0, curv0)
    return tuple(final_call(obs_count, solved, innovation, back, rc, rin, ic, iin))


def solution(mesh):
    one = P(("reg", "col"))
    in_specs = (P(None, ("reg", "col")), one, one, one, one, one, P(("reg", "col"), None), one, one)
    out_specs = (P(None, ("reg", "col")), P(None, ("reg", "col")))
    return jax.shard_map(
        on_device, mesh=mesh, in_specs=in_specs, out_specs=out_specs, check_vma=False
    )
```

```python
import functools

import jax
import jax.numpy as jnp
from jax import lax
from jax.experimental import pallas as pl
from jax.experimental.pallas import tpu as pltpu
from jax.sharding import PartitionSpec as P

ROWS = 1024
REACH = 2
COLS_DEV = 1024
TILE = 32
STEP = 16
PANEL = 8
EMPTY = ROWS // STEP
DEAD = 1e9
FAR = 1e6
VMEM_LIMIT = 24 * 1024 * 1024
KEEP = 128

highest = lax.Precision.HIGHEST
f32 = jnp.float32
bf16 = jnp.bfloat16
NT = (((1,), (1,)), ((), ()))
NN = (((1,), (0,)), ((), ()))
TN = (((0,), (0,)), ((), ()))
vmem = pl.BlockSpec(memory_space=pltpu.VMEM)
smem = pl.BlockSpec(memory_space=pltpu.SMEM)
anywhere = pl.BlockSpec(memory_space=pl.ANY)


def shift(block, distance):
    axis = ("reg", "col")
    n = lax.axis_size(axis)
    return lax.ppermute(block, axis, [((i - distance) % n, i) for i in range(n)])


def dot(a, b, dims=NN):
    return lax.dot_general(a, b, dims, preferred_element_type=f32)


def two(x):
    hi = x.astype(bf16)
    return hi, (x - hi.astype(f32)).astype(bf16)


def three(x):
    hi = x.astype(bf16)
    rest = x - hi.astype(f32)
    mid = rest.astype(bf16)
    return hi, mid, (rest - mid.astype(f32)).astype(bf16)


def combine(coef_t, blocks):
    chi, clo = two(coef_t)
    bhi, blo = two(blocks)
    return dot(
        jnp.concatenate([chi, chi, clo], axis=1), jnp.concatenate([bhi, blo, bhi], axis=0)
    )


def params():
    return pltpu.CompilerParams(vmem_limit_bytes=VMEM_LIMIT)


def ring(total, n_col):
    me = lax.axis_index("reg") * n_col + lax.axis_index("col")
    left, right = (me + total - 1) % total, (me + 1) % total
    return me, (left // n_col, left % n_col), (right // n_col, right % n_col)


def send_to(src, dst, sems, k, device):
    return pltpu.make_async_remote_copy(
        src_ref=src,
        dst_ref=dst,
        send_sem=sems[0].at[k],
        recv_sem=sems[1].at[k],
        device_id=device,
        device_id_type=pl.DeviceIdType.MESH,
    )


def greet(devices):
    barrier = pltpu.get_barrier_semaphore()
    for device in devices:
        pl.semaphore_signal(barrier, inc=1, device_id=device, device_id_type=pl.DeviceIdType.MESH)


def live_row(count_ref, g):
    slot = lax.broadcasted_iota(jnp.int32, (1, ROWS), 1)
    return (slot < count_ref[g]).astype(f32)


def sort_kernel(
    count_ref,
    pair_ref,
    innov_in,
    along_in,
    across_in,
    scale_in,
    error_in,
    first_ref,
    last_ref,
    ranka_ref,
    rankb_ref,
    innov_ref,
    along_ref,
    across_ref,
    scale_ref,
    error_ref,
    sem,
):
    width = first_ref.shape[1]
    per = width // ROWS
    moves = [
        (across_in, across_ref),
        (along_in, along_ref),
        (scale_in, scale_ref),
        (error_in, error_ref),
        (innov_in.at[:, :width], innov_ref.at[:, :width]),
        (innov_in.at[:, width:], innov_ref.at[:, width:]),
    ]
    fetches = [pltpu.make_async_copy(src, dst, sem.at[k]) for k, (src, dst) in enumerate(moves)]
    for fetch in fetches:
        fetch.start()
    for fetch in fetches[:4]:
        fetch.wait()
    sub = lax.broadcasted_iota(jnp.int32, (128, 128), 0)
    lane = lax.broadcasted_iota(jnp.int32, (128, 128), 1)

    def sort_region(g):
        out_ref, rank_ref = ((first_ref, ranka_ref), (last_ref, rankb_ref))[g // per]
        r = g % per
        cols = pl.ds(g * ROWS, ROWS)
        here = pl.ds(r * ROWS, ROWS)
        live = live_row(count_ref, g)
        across = across_ref[:, cols]
        key = jnp.where(live > 0.5, across, DEAD)
        flags = [jnp.full((1, ROWS), pair_ref[d, g], jnp.int32).astype(f32) for d in range(REACH)]
        meta = [along_ref[:, cols], across, scale_ref[:, cols] * live, error_ref[:, cols]]
        key_col = jnp.broadcast_to(key, (128, ROWS)).T
        ranks = []
        for b in range(ROWS // 128):
            begin, end = b * 128, (b + 1) * 128
            mine = key[:, begin:end]
            other = key_col[begin:end]
            ahead = (other < mine) | ((other == mine) & (sub < lane))
            rank = jnp.sum(jnp.where(ahead, 1.0, 0.0), axis=0, keepdims=True)
            if b:
                ahead = jnp.where(key_col[:begin] <= mine, 1.0, 0.0)
                rank = rank + jnp.sum(ahead, axis=0, keepdims=True)
            if end < ROWS:
                ahead = jnp.where(key_col[end:] < mine, 1.0, 0.0)
                rank = rank + jnp.sum(ahead, axis=0, keepdims=True)
            ranks.append(rank)
        rank = jnp.concatenate(ranks, axis=1)
        rank_ref[:, here] = jnp.broadcast_to(rank, (8, ROWS))
        if r == 0:
            fetches[4 + g // per].wait()
        stack = jnp.concatenate(
            [innov_ref[:, cols] * live] + meta + flags + [key, jnp.zeros((1, ROWS), f32)], axis=0
        )
        lhs = jnp.concatenate(three(stack), axis=0)
        n = stack.shape[0]
        rank_i = rank.astype(jnp.int32)
        for c in range(ROWS // 256):
            slot = lax.broadcasted_iota(jnp.int32, (256, ROWS), 0) + c * 256
            place = (slot == rank_i).astype(f32).astype(bf16)
            got = dot(lhs, place, NT)
            at = pl.ds(r * ROWS + c * 256, 256)
            out_ref[:, at] = got[:n] + got[n : 2 * n] + got[2 * n :]

    for g in range(2 * per):
        sort_region(g)


def sizes():
    n_col = lax.axis_size("col")
    return lax.axis_size("reg") * n_col, n_col


def comm_params(which):
    return pltpu.CompilerParams(
        collective_id=which, has_side_effects=True, vmem_limit_bytes=VMEM_LIMIT
    )


def sort_call(count, pair, innov, *rows):
    ens, n = innov.shape
    half = jax.ShapeDtypeStruct((ens + 8, n // 2), f32)
    rank = jax.ShapeDtypeStruct((8, n // 2), f32)
    return pl.pallas_call(
        sort_kernel,
        out_shape=(half, half, rank, rank),
        in_specs=[smem] * 2 + [pl.BlockSpec(memory_space=pltpu.HBM)] * 5,
        out_specs=(vmem,) * 4,
        scratch_shapes=[pltpu.VMEM((ens, n), f32)]
        + [pltpu.VMEM((1, n), f32)] * 4
        + [pltpu.SemaphoreType.DMA((6,))],
        compiler_params=params(),
        name="sort_slots",
    )(count, pair, *[pltpu.with_memory_space_constraint(x, pltpu.HBM) for x in (innov, *rows)])


def lay_grid(chunks, offsets, row_ref, grid_ref):
    width = chunks[0].shape[1]
    per = width // ROWS
    blocks = ROWS // 128
    grid_ref[...] = jnp.full(grid_ref.shape, FAR, f32)
    for c, ref in enumerate(chunks):
        row_ref[:, c * width : (c + 1) * width] = ref[ref.shape[0] - 8 :, :]
        for r in range(per):
            h = c * per + r
            at = slice(h * ROWS, (h + 1) * ROWS)
            row_ref[0:1, at] = row_ref[0:1, at] + float(offsets[h])
            for q, source in enumerate((0, 1, 6)):
                for b in range(blocks):
                    line = h * (blocks + 1) + b
                    begin = h * ROWS + b * 128
                    grid_ref[q, line : line + 1, :] = row_ref[source : source + 1, begin : begin + 128]


def lay_tables(grid_ref, regions, table_refs):
    count = regions * (ROWS // 128 + 1)
    ways = 128 // STEP
    lane = lax.broadcasted_iota(jnp.int32, (count, 128), 1)
    for q in range(2):
        here = grid_ref[q, :count, :]
        later = grid_ref[q, 1 : count + 1, :]
        table_refs[q][pl.ds(0, count, stride=ways), :] = here
        for k in range(1, ways):
            joined = jnp.where(lane < k * STEP, later, here)
            table_refs[q][pl.ds(k, count, stride=ways), :] = pltpu.roll(joined, 128 - k * STEP, 1)


def spread_rows(grid_ref, spread_refs):
    blocks = ROWS // 128
    regions = spread_refs[0].shape[0] // ROWS
    count = regions * (blocks + 1)
    for q in range(2):
        turned = jnp.concatenate(
            [grid_ref[q, :count, :], jnp.zeros((128 - count, 128), f32)], axis=0
        ).T
        for g in range(regions):
            for b in range(blocks):
                line = g * (blocks + 1) + b
                begin = g * ROWS + b * 128
                spread_refs[q][begin : begin + 128, :] = jnp.broadcast_to(
                    turned[:, line : line + 1], (128, 128)
                )


def own_pairs(regions):
    near = range(-REACH, REACH + 1)
    return [[(g + d, d) for d in near if 0 <= g + d < regions] for g in range(regions)]


def halo_pairs(regions):
    found = []
    for g in range(regions):
        mine = [(g + d + REACH, d) for d in range(-REACH, 0) if g + d < 0]
        mine += [(g + d - regions + REACH, d) for d in range(1, REACH + 1) if g + d >= regions]
        found.append(mine)
    return found


def widest(pairs):
    return max(len(mine) for mine in pairs)


def plan_windows(pairs, row_ref, grid_ref, row_i_ref, grid_i_ref, span_ref, item_ref):
    blocks = ROWS // 128
    regions = len(pairs)
    per = ROWS // TILE
    tiles = regions * per
    ways = 128 // STEP
    slots = widest(pairs)

    def keys_of(ref, count):
        return [ref[2, h * (blocks + 1) : h * (blocks + 1) + blocks, :] for h in range(count)]

    mine = jnp.concatenate(keys_of(grid_i_ref, regions), axis=0)
    top = jnp.where(mine < 0.5 * DEAD, mine, -DEAD)
    size = 1
    while size < TILE:
        top = jnp.maximum(top, pltpu.roll(top, 128 - size, 1))
        size *= 2
    parts = 128 // TILE
    lines = regions * blocks
    tile = lax.broadcasted_iota(jnp.int32, (lines, tiles), 1)
    line = lax.broadcasted_iota(jnp.int32, (lines, tiles), 0)
    first = jnp.zeros((1, tiles), f32)
    last = jnp.zeros((1, tiles), f32)
    for p in range(parts):
        here = tile == line * parts + p
        lane = slice(p * TILE, p * TILE + 1)
        first = first + jnp.sum(
            jnp.where(here, jnp.broadcast_to(mine[:, lane], (lines, tiles)), 0.0), axis=0, keepdims=True
        )
        last = last + jnp.sum(
            jnp.where(here, jnp.broadcast_to(top[:, lane], (lines, tiles)), 0.0), axis=0, keepdims=True
        )
    under, over = first - 1.001, last + 1.001
    begins, ends = [], []
    for key in keys_of(grid_ref, row_ref.shape[1] // ROWS):
        begin = jnp.zeros((blocks, tiles), f32)
        end = jnp.zeros((blocks, tiles), f32)
        for k in range(ways):
            low = jnp.broadcast_to(key[:, k * STEP : k * STEP + 1], (blocks, tiles))
            high = jnp.broadcast_to(key[:, (k + 1) * STEP - 1 : (k + 1) * STEP], (blocks, tiles))
            begin = begin + jnp.where(high < under, 1.0, 0.0)
            end = end + jnp.where(low <= over, 1.0, 0.0)
        begins.append(jnp.sum(begin, axis=0, keepdims=True))
        ends.append(jnp.sum(end, axis=0, keepdims=True))
    group = lax.broadcasted_iota(jnp.int32, (1, tiles), 1) // per
    alive = first < 0.5 * DEAD
    starts, stops = [], []
    needs = jnp.zeros((1, tiles), f32)
    for slot in range(slots):
        start = jnp.zeros((1, tiles), f32)
        stop = jnp.zeros((1, tiles), f32)
        for g, mine in enumerate(pairs):
            if slot >= len(mine):
                continue
            j, d = mine[slot]
            base = float(j * (ROWS + 128) // STEP)
            begin, end = begins[j] + base, ends[j] + base
            if d:
                source = 3 + abs(d)
                owner, holder = (g, row_i_ref) if d > 0 else (j, row_ref)
                flag = holder[source : source + 1, owner * ROWS : owner * ROWS + 128]
                end = jnp.where(flag[:, :tiles] > 0.5, end, begin)
            start = jnp.where(group == g, begin, start)
            stop = jnp.where(group == g, end, stop)
        stop = jnp.where(alive, jnp.maximum(stop, start), start)
        needs = jnp.maximum(needs, jnp.floor((stop - start + (ways - 1.0)) * (1.0 / ways)))
        starts.append(start)
        stops.append(stop)
    blank = jnp.full((8 - slots, tiles), float(EMPTY), f32)
    for m in range(blocks + 1):
        lines_m = [
            jnp.where(start + float(ways * m) < stop, start + float(ways * m), float(EMPTY))
            for start, stop in zip(starts, stops)
        ]
        span_ref[8 * m : 8 * m + 8, :] = jnp.concatenate(lines_m + [blank], axis=0).astype(jnp.int32)
    row = lax.broadcasted_iota(jnp.int32, (tiles, tiles), 0)
    col = lax.broadcasted_iota(jnp.int32, (tiles, tiles), 1)
    many = jnp.broadcast_to(needs, (tiles, tiles)).astype(bf16)
    done = dot((col <= row).astype(f32).astype(bf16), many, NT)
    each = dot((col == row).astype(f32).astype(bf16), many, NT)
    total = jnp.max(done, axis=0, keepdims=True)
    for k in range(item_ref.shape[1]):
        slot = lax.broadcasted_iota(jnp.int32, (1, tiles), 1).astype(f32) + float(k * tiles)
        past = done <= slot
        at = jnp.sum(jnp.where(past, 1.0, 0.0), axis=0, keepdims=True)
        began = jnp.sum(jnp.where(past, each, 0.0), axis=0, keepdims=True)
        spare = slot >= total
        item_ref[0, k : k + 1, :] = jnp.where(spare, 0.0, at).astype(jnp.int32)
        item_ref[1, k : k + 1, :] = jnp.where(spare, float(blocks), slot - began).astype(jnp.int32)
        item_ref[2, k : k + 1, :] = total.astype(jnp.int32)


def turn_vectors(v_ref, row_ref, turn_ref):
    ens, wide = v_ref.shape
    padded = ROWS + 128
    row = lax.broadcasted_iota(jnp.int32, (256, 256), 0)
    eye = (row == lax.broadcasted_iota(jnp.int32, (256, 256), 1)).astype(f32).astype(bf16)
    for h in range(wide // ROWS):
        for b in range(ROWS // 256):
            at = slice(h * ROWS + b * 256, h * ROWS + (b + 1) * 256)
            stack = jnp.concatenate(two(v_ref[:, at] * row_ref[2:3, at]), axis=0)
            begin = h * padded + b * 256
            turn_ref[begin : begin + 256, :] = dot(eye, stack, NT).astype(bf16)
        turn_ref[h * padded + ROWS : (h + 1) * padded, :] = jnp.zeros((128, 2 * ens), bf16)


def windows(work, n, slots):
    line, lane = lax.shift_right_logical(n, jnp.int32(7)), lax.bitwise_and(n, jnp.int32(127))
    tile = work["item"][0, line, lane]
    level = work["item"][1, line, lane] * 8
    return [tile] + [work["span"][level + slot, tile] for slot in range(slots)]


def gather(work, cov, where_to):
    tile, *found = where_to
    turn_ref = work["turn"]
    rhs = jnp.concatenate(
        [turn_ref[pl.ds(pl.multiple_of(w * STEP, STEP), 128), :] for w in found], axis=0
    )
    got = dot(cov, rhs)
    at = pl.ds(pl.multiple_of(tile * TILE, TILE), TILE)
    work["sum"][at, :] += got[:TILE] + got[TILE:]


def unroll_of(slots):
    return 8 if slots <= REACH else 4


def count_trips(work, unroll):
    return lax.shift_right_logical(
        work["item"][2, 0, 0] + (unroll - 1), jnp.int32(unroll.bit_length() - 1)
    )


def apply_cov(work, s_ref, keep, begin):
    slots = s_ref.shape[2] // 128
    unroll = unroll_of(slots)
    s_ref[keep : keep + unroll] = jnp.zeros((unroll,) + s_ref.shape[1:], bf16)

    def place(k):
        return jnp.where(k < keep // unroll, k * unroll, keep)

    def step(k, carry):
        before = jnp.where(k == begin, keep, place(k - 1))
        for p in range(unroll):
            gather(work, s_ref[before + p], carry[p])
        now = [windows(work, k * unroll + p, slots) for p in range(unroll)]
        after = place(k)
        for p in range(unroll):
            tile, *found = now[p]
            at = pl.ds(pl.multiple_of(tile * TILE, TILE), TILE)
            a_i = work["along_i"][at, :]
            b_i = work["across_i"][at, :]
            for d, w in enumerate(found):
                da = work["along"][pl.ds(w, 1), :] - a_i
                db = work["across"][pl.ds(w, 1), :] - b_i
                r2 = da * da + db * db
                r = r2 * lax.rsqrt(jnp.maximum(r2, 1e-30))
                u = jnp.maximum(1.0 - r, 0.0)
                u2 = u * u
                hi, lo = two((u2 * u2) * (r + 0.25))
                s_ref[after + p, 0:TILE, d * 128 : (d + 1) * 128] = hi
                s_ref[after + p, TILE : 2 * TILE, d * 128 : (d + 1) * 128] = lo
        return now

    trips = count_trips(work, unroll)
    end = jnp.where(trips > begin, trips + 1, begin)
    lax.fori_loop(begin, end, step, [windows(work, p, slots) for p in range(unroll)])


def apply_kept(work, kept_ref, ring_ref):
    slots = kept_ref.shape[2] // 128
    unroll = unroll_of(slots)
    most = KEEP // unroll

    def step(k, carry):
        for p in range(unroll):
            gather(work, kept_ref[k * unroll + p], windows(work, k * unroll + p, slots))
        return carry

    lax.fori_loop(0, jnp.minimum(count_trips(work, unroll), most), step, 0)
    apply_cov(work, ring_ref, 0, most)


def finish(sum_ref, base_ref, row_ref, v_ref, img_ref):
    ens, own = img_ref.shape
    for c in range(own // 128):
        at = slice(c * 128, (c + 1) * 128)
        turned = (sum_ref[at, :] + base_ref[at, :]).T
        img_ref[:, at] = (
            (turned[:ens] + turned[ens:]) * (row_ref[2:3, at] * 0.25) + row_ref[3:4, at] * v_ref[:, at]
        )


def gram(a, b):
    ahi, alo = two(a)
    bhi, blo = two(b)
    return dot(
        jnp.concatenate([ahi, ahi, alo], axis=1), jnp.concatenate([bhi, blo, bhi], axis=1), NT
    )


def square(n):
    return lax.broadcasted_iota(jnp.int32, (n, n), 0), lax.broadcasted_iota(jnp.int32, (n, n), 1)


def pack_pair(upper, lower):
    n = upper.shape[0]
    row, col = square(n)
    upper, lower = symmetric(upper), symmetric(lower)
    spare = jnp.sum(jnp.where(row == col, lower, 0.0), axis=0, keepdims=True)
    return jnp.where(col >= row, upper, lower), jnp.broadcast_to(spare, (8, n))


def unpack_pair(packed, spare):
    n = packed.shape[0]
    row, col = square(n)
    other = packed.T
    lower = jnp.where(row == col, jnp.broadcast_to(spare, (n, n)), jnp.where(col > row, other, packed))
    return jnp.where(col >= row, packed, other), lower


def start_plan(span_in, item_in, work):
    copies = [
        pltpu.make_async_copy(span_in, work["span"], work["plan_sem"].at[0]),
        pltpu.make_async_copy(item_in, work["item"], work["plan_sem"].at[1]),
    ]
    for copy in copies:
        copy.start()
    return copies


def multiply(copies, work, kept_ref=None):
    turn_vectors(work["v"], work["row"], work["turn"])
    work["sum"][...] = jnp.zeros_like(work["sum"])
    for copy in copies:
        copy.wait()
    if kept_ref is None:
        apply_cov(work, work["s"], KEEP, 0)
    else:
        apply_kept(work, kept_ref, work["ring"])


def lay_own(first_ref, last_ref, work):
    regions = first_ref.shape[1] * 2 // ROWS
    lay_grid([first_ref, last_ref], range(regions), work["row"], work["grid"])
    spread_rows(work["grid"], (work["along_i"], work["across_i"]))
    lay_tables(work["grid"], regions, (work["along"], work["across"]))


def lay_halo(before_ref, after_ref, first_ref, last_ref, work):
    regions = first_ref.shape[1] * 2 // ROWS
    offsets = list(range(-REACH, 0)) + list(range(regions, regions + REACH))
    lay_grid([first_ref, last_ref], range(regions), work["row_i"], work["grid_i"])
    lay_grid([before_ref, after_ref], offsets, work["row"], work["grid"])
    lay_tables(work["grid"], 2 * REACH, (work["along"], work["across"]))


def take_rows(chunks, row_ref):
    width = chunks[0].shape[1]
    for c, ref in enumerate(chunks):
        row_ref[:, c * width : (c + 1) * width] = ref[ref.shape[0] - 8 :, :]


def first_own_kernel(
    names, first_ref, last_ref, sum_out, span_out, item_out, along_out, across_out, along_i_out, across_i_out, s_out, *refs
):
    work = dict(zip(names, refs))
    work.update(along=along_out, across=across_out, along_i=along_i_out, across_i=across_i_out)
    work.update(sum=sum_out, s=s_out)
    ens = work["v"].shape[0]
    lead = first_ref.shape[1]
    lay_own(first_ref, last_ref, work)
    pairs = own_pairs(2 * lead // ROWS)
    plan_windows(pairs, work["row"], work["grid"], work["row"], work["grid"], span_out, item_out)
    copies = start_plan(span_out, item_out, work)
    work["v"][:, :lead] = first_ref[:ens, :]
    work["v"][:, lead:] = last_ref[:ens, :]
    multiply(copies, work)


def first_halo_kernel(
    names,
    before_ref,
    after_ref,
    first_ref,
    last_ref,
    base_ref,
    along_i_ref,
    across_i_ref,
    imga_ref,
    imgb_ref,
    gram_ref,
    span_out,
    item_out,
    along_out,
    across_out,
    s_out,
    *refs,
):
    work = dict(zip(names, refs))
    work.update(along=along_out, across=across_out, along_i=along_i_ref, across_i=across_i_ref, s=s_out)
    ens = work["v"].shape[0]
    lead = first_ref.shape[1]
    lay_halo(before_ref, after_ref, first_ref, last_ref, work)
    pairs = halo_pairs(2 * lead // ROWS)
    plan_windows(pairs, work["row"], work["grid"], work["row_i"], work["grid_i"], span_out, item_out)
    copies = start_plan(span_out, item_out, work)
    work["v"][:, :lead] = before_ref[:ens, :]
    work["v"][:, lead:] = after_ref[:ens, :]
    multiply(copies, work)
    work["v"][:, :lead] = first_ref[:ens, :]
    work["v"][:, lead:] = last_ref[:ens, :]
    img_ref = work["img"]
    finish(work["sum"], base_ref, work["row_i"], work["v"], img_ref)
    imga_ref[...] = img_ref[:, :lead]
    imgb_ref[...] = img_ref[:, lead:]
    r = work["v"][...]
    both = gram(r, jnp.concatenate([r, img_ref[...]], axis=0))
    packed, spare = pack_pair(both[:, :ens], both[:, ens:])
    half = ens // 2
    gram_ref[0:half, :] = jnp.concatenate([packed[:half], packed[half:]], axis=1)
    gram_ref[half : half + 8, :] = jnp.concatenate([spare, spare], axis=1)


def second_own_kernel(
    names,
    span_in,
    item_in,
    gram_ref,
    first_ref,
    last_ref,
    imga_ref,
    imgb_ref,
    along_ref,
    across_ref,
    along_i_ref,
    across_i_ref,
    kept_ref,
    sum_out,
    rest_out,
    step_out,
    inv_out,
    curv_out,
    *refs,
):
    work = dict(zip(names, refs))
    work.update(along=along_ref, across=across_ref, along_i=along_i_ref, across_i=across_i_ref)
    work.update(sum=sum_out, v=rest_out)
    ens = step_out.shape[0]
    lead = first_ref.shape[1]
    copies = start_plan(span_in, item_in, work)
    take_rows([first_ref, last_ref], work["row"])
    solve_first(gram_ref, step_out, inv_out, curv_out)
    step_t = step_out[...].T
    rest_out[:, :lead] = first_ref[:ens, :] - combine(step_t, imga_ref[...])
    rest_out[:, lead:] = last_ref[:ens, :] - combine(step_t, imgb_ref[...])
    multiply(copies, work, kept_ref)


def second_halo_kernel(
    names,
    span_in,
    item_in,
    step_ref,
    before_ref,
    after_ref,
    img_before_ref,
    img_after_ref,
    first_ref,
    last_ref,
    rest_ref,
    imga_ref,
    imgb_ref,
    base_ref,
    along_ref,
    across_ref,
    along_i_ref,
    across_i_ref,
    kept_ref,
    gram_ref,
    *refs,
):
    work = dict(zip(names, refs))
    work.update(along=along_ref, across=across_ref, along_i=along_i_ref, across_i=across_i_ref)
    ens = step_ref.shape[0]
    lead = before_ref.shape[1]
    copies = start_plan(span_in, item_in, work)
    take_rows([first_ref, last_ref], work["row_i"])
    take_rows([before_ref, after_ref], work["row"])
    step_t = step_ref[...].T
    work["v"][:, :lead] = before_ref[:ens, :] - combine(step_t, img_before_ref[...])
    work["v"][:, lead:] = after_ref[:ens, :] - combine(step_t, img_after_ref[...])
    multiply(copies, work, kept_ref)
    img_ref = work["img"]
    finish(work["sum"], base_ref, work["row_i"], rest_ref, img_ref)
    r = rest_ref[...]
    both = gram(r, jnp.concatenate([r, img_ref[...]], axis=0))
    mixed = gram(r, jnp.concatenate([imga_ref[...], imgb_ref[...]], axis=1))
    packed, spare = pack_pair(both[:, :ens], both[:, ens:])
    gram_ref[0:ens, :] = jnp.concatenate([packed, mixed], axis=1)
    gram_ref[ens : ens + 8, :] = jnp.concatenate([spare, spare], axis=1)


def plan_shapes(own):
    tiles = own // TILE
    most = tiles * (ROWS // 128)
    return (8 * (ROWS // 128 + 1), tiles), (3, most // 128 + 1, 128)


def plan_out(own):
    return tuple(jax.ShapeDtypeStruct(shape, jnp.int32) for shape in plan_shapes(own))


def table_shapes(own, halo):
    near = 2 * REACH if halo else own // ROWS
    slots = widest((halo_pairs if halo else own_pairs)(own // ROWS))
    table = jax.ShapeDtypeStruct((128 // STEP * near * (ROWS // 128 + 1), 128), f32)
    kept = jax.ShapeDtypeStruct((KEEP + unroll_of(slots), 2 * TILE, slots * 128), bf16)
    return (table, table), (kept,)


def scratch(ens, own, halo, again):
    regions = own // ROWS
    near = 2 * REACH if halo else regions
    slots = widest((halo_pairs if halo else own_pairs)(regions))

    def grid(count):
        return pltpu.VMEM((3, -(-(count * (ROWS // 128 + 1) + 1) // 8) * 8, 128), f32)

    spans, items = plan_shapes(own)
    shapes = {
        "span": pltpu.SMEM(spans, jnp.int32),
        "item": pltpu.SMEM(items, jnp.int32),
        "plan_sem": pltpu.SemaphoreType.DMA((2,)),
        "row": pltpu.VMEM((8, near * ROWS), f32),
        "turn": pltpu.VMEM((near * (ROWS + 128), 2 * ens), bf16),
    }
    if not again:
        shapes["grid"] = grid(near)
    if again:
        shapes["ring"] = pltpu.VMEM((unroll_of(slots), 2 * TILE, slots * 128), bf16)
    if halo:
        shapes["row_i"] = pltpu.VMEM((8, own), f32)
        shapes["grid_i"] = grid(regions)
        shapes["img"] = pltpu.VMEM((ens, own), f32)
        shapes["sum"] = pltpu.VMEM((own, 128), f32)
    if halo or not again:
        shapes["v"] = pltpu.VMEM((ens, near * ROWS), f32)
    return tuple(shapes), list(shapes.values())


def operate(kernel, name, kind, args, outs, ens, own):
    names, shapes = scratch(ens, own, *kind)
    return pl.pallas_call(
        functools.partial(kernel, names),
        out_shape=outs,
        in_specs=[vmem] * len(args),
        out_specs=(vmem,) * len(outs),
        scratch_shapes=shapes,
        compiler_params=params(),
        cost_estimate=pl.CostEstimate(flops=10**10, bytes_accessed=4 << 20, transcendentals=0),
        name=name,
    )(*args)


def first_own_call(first, last, ens, own):
    tables, kept = table_shapes(own, False)
    spread = jax.ShapeDtypeStruct((own, 128), f32)
    outs = (spread,) + plan_out(own) + tables + (spread, spread) + kept
    return operate(first_own_kernel, "first_own", (False, False), (first, last), outs, ens, own)


def first_halo_call(chunks, base, spreads, ens, own):
    tables, kept = table_shapes(own, True)
    half = jax.ShapeDtypeStruct((ens, own // 2), f32)
    outs = (half, half, jax.ShapeDtypeStruct((ens // 2 + 8, 2 * ens), f32))
    outs += plan_out(own) + tables + kept
    args = (*chunks, base, *spreads)
    return operate(first_halo_kernel, "first_halo", (True, False), args, outs, ens, own)


def second_own_call(plan, grams, first, last, imga, imgb, laid, ens, own):
    small = jax.ShapeDtypeStruct((ens, ens), f32)
    outs = (jax.ShapeDtypeStruct((own, 2 * ens), f32), jax.ShapeDtypeStruct((ens, own), f32))
    args = (*plan, grams, first, last, imga, imgb, *laid)
    return operate(second_own_kernel, "second_own", (False, True), args, outs + (small,) * 3, ens, own)


def second_halo_call(plan, step, before, after, images, first, last, rest, mine, base, laid, ens, own):
    args = (*plan, step, before, after, *images, first, last, rest, *mine, base, *laid)
    outs = (jax.ShapeDtypeStruct((ens + 8, 2 * ens), f32),)
    return operate(second_halo_kernel, "second_halo", (True, True), args, outs, ens, own)[0]


def flip(me, size):
    return size * (1 - 2 * ((me // size) % 2))


def exchange_steps(total):
    bits = total.bit_length() - 1
    steps = [[1]] if bits % 2 else []
    for k in range(bits % 2, bits, 2):
        steps.append([2**k, 2 ** (k + 1)])
    return steps


def partners_of(steps, n_col, me):
    found = []
    for amounts in steps:
        others = [me + flip(me, size) for size in amounts]
        if len(amounts) == 2:
            others.append(others[0] + flip(me, amounts[1]))
        found.append([(other // n_col, other % n_col) for other in others])
    return found


def sum_all(partners, x_ref, send, recv, sems, work):
    total = x_ref[...]
    slot = 0
    for k, group in enumerate(partners):
        if k:
            send[k] = total
        source = send.at[k] if k else x_ref
        copies = [
            send_to(source, recv.at[slot + p], sems, slot + p, other) for p, other in enumerate(group)
        ]
        for copy in copies:
            copy.start()
        if k < len(work):
            work[k]()
        for copy in copies:
            copy.wait()
        total = total + recv[slot]
        if len(group) == 3:
            total = total + (recv[slot + 1] + recv[slot + 2])
        slot += len(group)
    for piece in work[len(partners) :]:
        piece()
    return total


def local_column(owner, me, total):
    local = owner - me * COLS_DEV
    return jnp.where(local < 0, local + total * COLS_DEV, local)


def add_columns(scaled_ref, owner_ref, me, total, base, target_ref):
    own = owner_ref.shape[1]

    def one(c, carry):
        got = jnp.zeros((scaled_ref.shape[0], 256), f32)
        for g in range(own // ROWS):
            at = slice(g * ROWS, (g + 1) * ROWS)
            slot = lax.broadcasted_iota(jnp.int32, (256, ROWS), 0) + (base + c * 256)
            owner = local_column(owner_ref[:, at], me, total)
            hot = (slot == owner).astype(f32).astype(bf16)
            got = got + dot(scaled_ref[:, at], hot, NT)
        ens = target_ref.shape[0]
        target_ref[:, pl.ds(pl.multiple_of(c * 256, 256), 256)] = got[:ens] + got[ens:]
        return carry

    lax.fori_loop(0, COLS_DEV // 256, one, 0)


def join_first_kernel(
    steps,
    total,
    n_col,
    x_ref,
    imga_ref,
    imgb_ref,
    ranka_ref,
    rankb_ref,
    gain_ref,
    owner_ref,
    out_ref,
    back_ref,
    scaled_ref,
    edge_ref,
    send,
    recv,
    send_sem,
    recv_sem,
):
    ens, half = imga_ref.shape
    me = lax.axis_index("reg") * n_col + lax.axis_index("col")
    partners = partners_of(steps, n_col, me)
    everyone = [other for group in partners for other in group]
    greet(everyone)
    pl.semaphore_wait(pltpu.get_barrier_semaphore(), len(everyone))

    def unsort():
        for k, (img_ref, rank_ref) in enumerate(((imga_ref, ranka_ref), (imgb_ref, rankb_ref))):

            def one(r, carry, k=k, img_ref=img_ref, rank_ref=rank_ref):
                at = pl.ds(pl.multiple_of(k * half + r * ROWS, ROWS), ROWS)
                here = pl.ds(pl.multiple_of(r * ROWS, ROWS), ROWS)
                rank = rank_ref[0:1, here].astype(jnp.int32)
                lhs = jnp.concatenate(two(img_ref[:, here]), axis=0)
                got = jnp.zeros((2 * ens, ROWS), f32)
                for c in range(ROWS // 256):
                    slot = lax.broadcasted_iota(jnp.int32, (256, ROWS), 0) + c * 256
                    place = (slot == rank).astype(f32).astype(bf16)
                    got = got + dot(lhs[:, c * 256 : (c + 1) * 256], place)
                image = got[:ens] + got[ens:]
                back_ref[:, at] = image
                scaled_ref[:, at] = jnp.concatenate(two(image * gain_ref[:, at]), axis=0)
                return carry

            lax.fori_loop(0, half // ROWS, one, 0)

    def outer():
        add_columns(scaled_ref, owner_ref, me, total, COLS_DEV, edge_ref)

    out_ref[...] = sum_all(partners, x_ref, send, recv, (send_sem, recv_sem), [unsort, outer])


def inner_columns_kernel(total, n_col, scaled_ref, owner_ref, cols_ref):
    me = lax.axis_index("reg") * n_col + lax.axis_index("col")
    add_columns(scaled_ref, owner_ref, me, total, 0, cols_ref)


def join_second_kernel(
    steps,
    total,
    n_col,
    count_ref,
    x_ref,
    innov_ref,
    gain_ref,
    owner_ref,
    out_ref,
    cols_ref,
    came_ref,
    scaled_ref,
    send,
    recv,
    send_sem,
    recv_sem,
    edge_ref,
    bulk_send_sem,
    bulk_recv_sem,
):
    own = innov_ref.shape[1]
    me, left, right = ring(total, n_col)
    partners = partners_of(steps, n_col, me)
    everyone = [other for group in partners for other in group] + [left, right]
    greet(everyone)
    pl.semaphore_wait(pltpu.get_barrier_semaphore(), len(everyone))
    edge = send_to(edge_ref, came_ref, (bulk_send_sem, bulk_recv_sem), 0, right)

    def scale():
        def one(g, carry):
            at = pl.ds(pl.multiple_of(g * ROWS, ROWS), ROWS)
            factor = gain_ref[:, at] * live_row(count_ref, g)
            scaled_ref[:, at] = jnp.concatenate(two(innov_ref[:, at] * factor), axis=0)
            return carry

        lax.fori_loop(0, own // ROWS, one, 0)

    def outer():
        add_columns(scaled_ref, owner_ref, me, total, COLS_DEV, edge_ref)

    def inner():
        edge.start()
        add_columns(scaled_ref, owner_ref, me, total, 0, cols_ref)

    out_ref[...] = sum_all(partners, x_ref, send, recv, (send_sem, recv_sem), [scale, outer, inner])
    edge.wait()


def join_scratch(steps, shape):
    slots = sum(2 ** len(amounts) - 1 for amounts in steps)
    return [
        pltpu.VMEM((len(steps),) + shape, f32),
        pltpu.VMEM((slots,) + shape, f32),
        pltpu.SemaphoreType.DMA((slots,)),
        pltpu.SemaphoreType.DMA((slots,)),
    ]


def inner_columns(scaled, owner):
    return pl.pallas_call(
        functools.partial(inner_columns_kernel, *sizes()),
        out_shape=jax.ShapeDtypeStruct((scaled.shape[0] // 2, COLS_DEV), f32),
        in_specs=[vmem] * 2,
        out_specs=vmem,
        compiler_params=params(),
        cost_estimate=pl.CostEstimate(flops=4 * 10**9, bytes_accessed=1 << 20, transcendentals=0),
        name="inner_columns",
    )(scaled, owner)


def join_first(x, imga, imgb, ranka, rankb, gain, owner):
    ens, half = imga.shape
    total, n_col = sizes()
    steps = exchange_steps(total)
    cols = jax.ShapeDtypeStruct((ens, COLS_DEV), f32)
    return pl.pallas_call(
        functools.partial(join_first_kernel, steps, total, n_col),
        out_shape=(
            jax.ShapeDtypeStruct(x.shape, f32),
            jax.ShapeDtypeStruct((ens, 2 * half), f32),
            jax.ShapeDtypeStruct((2 * ens, 2 * half), bf16),
            cols,
        ),
        in_specs=[vmem] * 7,
        out_specs=(vmem,) * 4,
        scratch_shapes=join_scratch(steps, x.shape),
        compiler_params=comm_params(1),
        name="join_first",
    )(x, imga, imgb, ranka, rankb, gain, owner)


def join_second(count, x, innov, gain, owner):
    ens, own = innov.shape
    total, n_col = sizes()
    steps = exchange_steps(total)
    cols = jax.ShapeDtypeStruct((ens, COLS_DEV), f32)
    return pl.pallas_call(
        functools.partial(join_second_kernel, steps, total, n_col),
        out_shape=(jax.ShapeDtypeStruct(x.shape, f32), cols, cols),
        in_specs=[smem] + [vmem] * 4,
        out_specs=(vmem, vmem, anywhere),
        scratch_shapes=[pltpu.VMEM((2 * ens, own), bf16)]
        + join_scratch(steps, x.shape)
        + [
            pltpu.VMEM((ens, COLS_DEV), f32),
            pltpu.SemaphoreType.DMA((1,)),
            pltpu.SemaphoreType.DMA((1,)),
        ],
        compiler_params=comm_params(2),
        name="join_second",
    )(count, x, innov, gain, owner)


def symmetric(matrix):
    return 0.5 * (matrix + matrix.T)


def mm(a, b, dims=NN):
    return lax.dot_general(a, b, dims, precision=highest, preferred_element_type=f32)


def eliminate(chains):
    ens, both = chains[0].shape
    parts = range(ens // 8)
    rows = lax.broadcasted_iota(jnp.int32, (8, both), 0)
    chains = [[m[8 * i : 8 * i + 8] for i in parts] for m in chains]

    def clear(parts_of, col, pivot, at):
        done = [x - c * pivot for x, c in zip(parts_of, col)]
        done[at // 8] = jnp.where(rows == at % 8, pivot, done[at // 8])
        return done

    for k in range(0, ens, PANEL):
        columns = [
            [[jnp.broadcast_to(x[:, k + j : k + j + 1], (8, both)) for x in m] for j in range(PANEL)]
            for m in chains
        ]
        for p in range(PANEL):
            at = k + p
            one = slice(at % 8, at % 8 + 1)
            done = []
            for m, cols in zip(chains, columns):
                col = cols[p]
                scale = 1.0 / col[at // 8][one]
                for j in range(p + 1, PANEL):
                    cols[j] = clear(cols[j], col, cols[j][at // 8][one] * scale, at)
                done.append(clear(m, col, m[at // 8][one] * scale, at))
            chains = done
    return [jnp.concatenate(m, axis=0)[:, ens:] for m in chains]


def solve_first(gram_ref, step_ref, inv_ref, curv_ref):
    ens = step_ref.shape[0]
    half = ens // 2
    packed = jnp.concatenate([gram_ref[0:half, :ens], gram_ref[0:half, ens:]], axis=0)
    norm, curv = unpack_pair(packed, gram_ref[half : half + 1, :ens])
    row, col = square(ens)
    eye = (row == col).astype(f32)
    step, inv = eliminate(
        [jnp.concatenate([curv, norm], axis=1), jnp.concatenate([norm, eye], axis=1)]
    )
    step_ref[...] = step
    inv_ref[...] = inv
    curv_ref[...] = curv


def solve_second(gram_ref, step_ref, inv_ref, curv_ref):
    ens = step_ref.shape[0]
    norm, cross = unpack_pair(gram_ref[0:ens, :ens], gram_ref[ens : ens + 1, :ens])
    mixed = gram_ref[0:ens, ens:]
    conj = mm(inv_ref[...], norm)
    coupled = mm(mixed, conj)
    quad = mm(conj, mm(curv_ref[...], conj), TN)
    curv = symmetric(cross + coupled + coupled.T + quad)
    (step,) = eliminate([jnp.concatenate([curv, norm], axis=1)])
    step0 = step_ref[...]
    keep = step0 + step + mm(conj, step)
    return keep.T, -mm(step0, step).T


def final_kernel(
    count_ref, gram_ref, step_ref, inv_ref, curv_ref, innov_ref, back_ref, rc_ref, rin_ref, ic_ref, iin_ref, w_ref, inc_ref
):
    first, second = solve_second(gram_ref, step_ref, inv_ref, curv_ref)
    for g in range(innov_ref.shape[1] // ROWS):
        at = pl.ds(g * ROWS, ROWS)
        live = live_row(count_ref, g)
        w_ref[:, at] = combine(first, innov_ref[:, at] * live) + combine(second, back_ref[:, at])
    inc_ref[...] = combine(first, rc_ref[...] + rin_ref[...]) + combine(
        second, ic_ref[...] + iin_ref[...]
    )


def final_call(count, solved, innov, back, *cols):
    ens, own = innov.shape
    return pl.pallas_call(
        final_kernel,
        out_shape=(
            jax.ShapeDtypeStruct((ens, own), f32),
            jax.ShapeDtypeStruct((ens, COLS_DEV), f32),
        ),
        in_specs=[smem] + [vmem] * 10,
        out_specs=(vmem, vmem),
        compiler_params=params(),
        name="final",
    )(count, *solved, innov, back, *cols)


def on_device(
    innovation,
    obs_along,
    obs_across,
    obs_scale,
    obs_error,
    obs_gain,
    pair_live,
    obs_count,
    col_owner,
):
    ens, own = innovation.shape
    rows = [x.reshape(1, own) for x in (obs_along, obs_across, obs_scale, obs_error)]
    gain, owner = obs_gain.reshape(1, own), col_owner.reshape(1, own)
    first, last, rank_a, rank_b = sort_call(obs_count, pair_live.T, innovation, *rows)
    after, before = shift(first, -1), shift(last, 1)
    base, *rest = first_own_call(first, last, ens, own)
    plan_own, laid_own = rest[:2], rest[2:]
    spreads = laid_own[2:4]
    chunks = [before, after, first, last]
    imga, imgb, grams, *rest = first_halo_call(chunks, base, spreads, ens, own)
    plan_halo, laid_halo = rest[:2], rest[2:4] + spreads + rest[4:]
    grams, back, scaled, edge = join_first(grams, imga, imgb, rank_a, rank_b, gain, owner)
    senda, sendb, grams = lax.optimization_barrier((imga, imgb, grams))
    img_after, img_before = shift(senda, -1), shift(sendb, 1)
    iin = shift(edge, 1)
    ic = inner_columns(scaled, owner)
    base, rest, step0, inv0, curv0 = second_own_call(plan_own, grams, first, last, imga, imgb, laid_own, ens, own)
    images = [img_before, img_after]
    grams = second_halo_call(
        plan_halo, step0, before, after, images, first, last, rest, [imga, imgb], base, laid_halo, ens, own
    )
    grams, rc, rin = join_second(obs_count, grams, innovation, gain, owner)
    solved = (grams, step0, inv0, curv0)
    return tuple(final_call(obs_count, solved, innovation, back, rc, rin, ic, iin))


def solution(mesh):
    one = P(("reg", "col"))
    in_specs = (P(None, ("reg", "col")), one, one, one, one, one, P(("reg", "col"), None), one, one)
    out_specs = (P(None, ("reg", "col")), P(None, ("reg", "col")))
    return jax.shard_map(
        on_device, mesh=mesh, in_specs=in_specs, out_specs=out_specs, check_vma=False
    )
```

```python
import functools

import jax
import jax.numpy as jnp
from jax import lax
from jax.experimental import pallas as pl
from jax.experimental.pallas import tpu as pltpu
from jax.sharding import PartitionSpec as P

ROWS = 1024
REACH = 2
COLS_DEV = 1024
TILE = 32
STEP = 16
PANEL = 8
EMPTY = ROWS // STEP
DEAD = 1e9
FAR = 1e6
VMEM_LIMIT = 24 * 1024 * 1024
KEEP = 128

highest = lax.Precision.HIGHEST
f32 = jnp.float32
bf16 = jnp.bfloat16
NT = (((1,), (1,)), ((), ()))
NN = (((1,), (0,)), ((), ()))
TN = (((0,), (0,)), ((), ()))
vmem = pl.BlockSpec(memory_space=pltpu.VMEM)
smem = pl.BlockSpec(memory_space=pltpu.SMEM)
anywhere = pl.BlockSpec(memory_space=pl.ANY)


def shift(block, distance):
    axis = ("reg", "col")
    n = lax.axis_size(axis)
    return lax.ppermute(block, axis, [((i - distance) % n, i) for i in range(n)])


def dot(a, b, dims=NN):
    return lax.dot_general(a, b, dims, preferred_element_type=f32)


def two(x):
    hi = x.astype(bf16)
    return hi, (x - hi.astype(f32)).astype(bf16)


def three(x):
    hi = x.astype(bf16)
    rest = x - hi.astype(f32)
    mid = rest.astype(bf16)
    return hi, mid, (rest - mid.astype(f32)).astype(bf16)


def combine(coef_t, blocks):
    chi, clo = two(coef_t)
    bhi, blo = two(blocks)
    return dot(
        jnp.concatenate([chi, chi, clo], axis=1), jnp.concatenate([bhi, blo, bhi], axis=0)
    )


def params():
    return pltpu.CompilerParams(vmem_limit_bytes=VMEM_LIMIT)


def ring(total, n_col):
    me = lax.axis_index("reg") * n_col + lax.axis_index("col")
    left, right = (me + total - 1) % total, (me + 1) % total
    return me, (left // n_col, left % n_col), (right // n_col, right % n_col)


def send_to(src, dst, sems, k, device):
    return pltpu.make_async_remote_copy(
        src_ref=src,
        dst_ref=dst,
        send_sem=sems[0].at[k],
        recv_sem=sems[1].at[k],
        device_id=device,
        device_id_type=pl.DeviceIdType.MESH,
    )


def greet(devices):
    barrier = pltpu.get_barrier_semaphore()
    for device in devices:
        pl.semaphore_signal(barrier, inc=1, device_id=device, device_id_type=pl.DeviceIdType.MESH)


def live_row(count_ref, g):
    slot = lax.broadcasted_iota(jnp.int32, (1, ROWS), 1)
    return (slot < count_ref[g]).astype(f32)


def sort_kernel(
    count_ref,
    pair_ref,
    innov_in,
    along_in,
    across_in,
    scale_in,
    error_in,
    first_ref,
    last_ref,
    ranka_ref,
    rankb_ref,
    innov_ref,
    along_ref,
    across_ref,
    scale_ref,
    error_ref,
    sem,
):
    width = first_ref.shape[1]
    per = width // ROWS
    moves = [
        (across_in, across_ref),
        (along_in, along_ref),
        (scale_in, scale_ref),
        (error_in, error_ref),
        (innov_in.at[:, :width], innov_ref.at[:, :width]),
        (innov_in.at[:, width:], innov_ref.at[:, width:]),
    ]
    fetches = [pltpu.make_async_copy(src, dst, sem.at[k]) for k, (src, dst) in enumerate(moves)]
    for fetch in fetches:
        fetch.start()
    for fetch in fetches[:4]:
        fetch.wait()
    sub = lax.broadcasted_iota(jnp.int32, (128, 128), 0)
    lane = lax.broadcasted_iota(jnp.int32, (128, 128), 1)

    def sort_region(g):
        out_ref, rank_ref = ((first_ref, ranka_ref), (last_ref, rankb_ref))[g // per]
        r = g % per
        cols = pl.ds(g * ROWS, ROWS)
        here = pl.ds(r * ROWS, ROWS)
        live = live_row(count_ref, g)
        across = across_ref[:, cols]
        key = jnp.where(live > 0.5, across, DEAD)
        flags = [jnp.full((1, ROWS), pair_ref[d, g], jnp.int32).astype(f32) for d in range(REACH)]
        meta = [along_ref[:, cols], across, scale_ref[:, cols] * live, error_ref[:, cols]]
        key_col = jnp.broadcast_to(key, (128, ROWS)).T
        ranks = []
        for b in range(ROWS // 128):
            begin, end = b * 128, (b + 1) * 128
            mine = key[:, begin:end]
            other = key_col[begin:end]
            ahead = (other < mine) | ((other == mine) & (sub < lane))
            rank = jnp.sum(jnp.where(ahead, 1.0, 0.0), axis=0, keepdims=True)
            if b:
                ahead = jnp.where(key_col[:begin] <= mine, 1.0, 0.0)
                rank = rank + jnp.sum(ahead, axis=0, keepdims=True)
            if end < ROWS:
                ahead = jnp.where(key_col[end:] < mine, 1.0, 0.0)
                rank = rank + jnp.sum(ahead, axis=0, keepdims=True)
            ranks.append(rank)
        rank = jnp.concatenate(ranks, axis=1)
        rank_ref[:, here] = jnp.broadcast_to(rank, (8, ROWS))
        if r == 0:
            fetches[4 + g // per].wait()
        stack = jnp.concatenate(
            [innov_ref[:, cols] * live] + meta + flags + [key, jnp.zeros((1, ROWS), f32)], axis=0
        )
        lhs = jnp.concatenate(three(stack), axis=0)
        n = stack.shape[0]
        for c in range(ROWS // 256):
            got = dot(lhs, one_hot(rank - float(c * 256)), NT)
            at = pl.ds(r * ROWS + c * 256, 256)
            out_ref[:, at] = got[:n] + got[n : 2 * n] + got[2 * n :]

    for g in range(2 * per):
        sort_region(g)


def sizes():
    n_col = lax.axis_size("col")
    return lax.axis_size("reg") * n_col, n_col


def comm_params(which):
    return pltpu.CompilerParams(
        collective_id=which, has_side_effects=True, vmem_limit_bytes=VMEM_LIMIT
    )


def sort_call(count, pair, innov, *rows):
    ens, n = innov.shape
    half = jax.ShapeDtypeStruct((ens + 8, n // 2), f32)
    rank = jax.ShapeDtypeStruct((8, n // 2), f32)
    return pl.pallas_call(
        sort_kernel,
        out_shape=(half, half, rank, rank),
        in_specs=[smem] * 2 + [pl.BlockSpec(memory_space=pltpu.HBM)] * 5,
        out_specs=(vmem,) * 4,
        scratch_shapes=[pltpu.VMEM((ens, n), f32)]
        + [pltpu.VMEM((1, n), f32)] * 4
        + [pltpu.SemaphoreType.DMA((6,))],
        compiler_params=params(),
        name="sort_slots",
    )(*[pltpu.with_memory_space_constraint(x, pltpu.HBM) for x in (count, pair, innov, *rows)])


def lay_grid(chunks, offsets, row_ref, grid_ref):
    width = chunks[0].shape[1]
    per = width // ROWS
    blocks = ROWS // 128
    grid_ref[...] = jnp.full(grid_ref.shape, FAR, f32)
    for c, ref in enumerate(chunks):
        row_ref[:, c * width : (c + 1) * width] = ref[ref.shape[0] - 8 :, :]
        for r in range(per):
            h = c * per + r
            at = slice(h * ROWS, (h + 1) * ROWS)
            row_ref[0:1, at] = row_ref[0:1, at] + float(offsets[h])
            for q, source in enumerate((0, 1, 6)):
                for b in range(blocks):
                    line = h * (blocks + 1) + b
                    begin = h * ROWS + b * 128
                    grid_ref[q, line : line + 1, :] = row_ref[source : source + 1, begin : begin + 128]


def lay_tables(grid_ref, regions, table_refs):
    count = regions * (ROWS // 128 + 1)
    ways = 128 // STEP
    lane = lax.broadcasted_iota(jnp.int32, (count, 128), 1)
    for q in range(2):
        here = grid_ref[q, :count, :]
        later = grid_ref[q, 1 : count + 1, :]
        table_refs[q][pl.ds(0, count, stride=ways), :] = here
        for k in range(1, ways):
            joined = jnp.where(lane < k * STEP, later, here)
            table_refs[q][pl.ds(k, count, stride=ways), :] = pltpu.roll(joined, 128 - k * STEP, 1)


def spread_rows(grid_ref, spread_refs):
    blocks = ROWS // 128
    regions = spread_refs[0].shape[0] // ROWS
    count = regions * (blocks + 1)
    for q in range(2):
        turned = jnp.concatenate(
            [grid_ref[q, :count, :], jnp.zeros((128 - count, 128), f32)], axis=0
        ).T
        for g in range(regions):
            for b in range(blocks):
                line = g * (blocks + 1) + b
                begin = g * ROWS + b * 128
                spread_refs[q][begin : begin + 128, :] = jnp.broadcast_to(
                    turned[:, line : line + 1], (128, 128)
                )


def own_pairs(regions):
    near = range(-REACH, REACH + 1)
    return [[(g + d, d) for d in near if 0 <= g + d < regions] for g in range(regions)]


def halo_pairs(regions):
    found = []
    for g in range(regions):
        mine = [(g + d + REACH, d) for d in range(-REACH, 0) if g + d < 0]
        mine += [(g + d - regions + REACH, d) for d in range(1, REACH + 1) if g + d >= regions]
        found.append(mine)
    return found


def widest(pairs):
    return max(len(mine) for mine in pairs)


def plan_windows(pairs, row_ref, grid_ref, row_i_ref, grid_i_ref, span_ref, item_ref):
    blocks = ROWS // 128
    regions = len(pairs)
    per = ROWS // TILE
    tiles = regions * per
    ways = 128 // STEP
    slots = widest(pairs)

    def keys_of(ref, count):
        return [ref[2, h * (blocks + 1) : h * (blocks + 1) + blocks, :] for h in range(count)]

    mine = jnp.concatenate(keys_of(grid_i_ref, regions), axis=0)
    top = jnp.where(mine < 0.5 * DEAD, mine, -DEAD)
    size = 1
    while size < TILE:
        top = jnp.maximum(top, pltpu.roll(top, 128 - size, 1))
        size *= 2
    parts = 128 // TILE
    lines = regions * blocks
    tile = lax.broadcasted_iota(jnp.int32, (lines, tiles), 1)
    line = lax.broadcasted_iota(jnp.int32, (lines, tiles), 0)
    first = jnp.zeros((1, tiles), f32)
    last = jnp.zeros((1, tiles), f32)
    for p in range(parts):
        here = tile == line * parts + p
        lane = slice(p * TILE, p * TILE + 1)
        first = first + jnp.sum(
            jnp.where(here, jnp.broadcast_to(mine[:, lane], (lines, tiles)), 0.0), axis=0, keepdims=True
        )
        last = last + jnp.sum(
            jnp.where(here, jnp.broadcast_to(top[:, lane], (lines, tiles)), 0.0), axis=0, keepdims=True
        )
    under, over = first - 1.001, last + 1.001
    begins, ends = [], []
    for key in keys_of(grid_ref, row_ref.shape[1] // ROWS):
        begin = jnp.zeros((blocks, tiles), f32)
        end = jnp.zeros((blocks, tiles), f32)
        for k in range(ways):
            low = jnp.broadcast_to(key[:, k * STEP : k * STEP + 1], (blocks, tiles))
            high = jnp.broadcast_to(key[:, (k + 1) * STEP - 1 : (k + 1) * STEP], (blocks, tiles))
            begin = begin + jnp.where(high < under, 1.0, 0.0)
            end = end + jnp.where(low <= over, 1.0, 0.0)
        begins.append(jnp.sum(begin, axis=0, keepdims=True))
        ends.append(jnp.sum(end, axis=0, keepdims=True))
    group = lax.broadcasted_iota(jnp.int32, (1, tiles), 1) // per
    alive = first < 0.5 * DEAD
    starts, stops = [], []
    needs = jnp.zeros((1, tiles), f32)
    for slot in range(slots):
        start = jnp.zeros((1, tiles), f32)
        stop = jnp.zeros((1, tiles), f32)
        for g, mine in enumerate(pairs):
            if slot >= len(mine):
                continue
            j, d = mine[slot]
            base = float(j * (ROWS + 128) // STEP)
            begin, end = begins[j] + base, ends[j] + base
            if d:
                source = 3 + abs(d)
                owner, holder = (g, row_i_ref) if d > 0 else (j, row_ref)
                flag = holder[source : source + 1, owner * ROWS : owner * ROWS + 128]
                end = jnp.where(flag[:, :tiles] > 0.5, end, begin)
            start = jnp.where(group == g, begin, start)
            stop = jnp.where(group == g, end, stop)
        stop = jnp.where(alive, jnp.maximum(stop, start), start)
        needs = jnp.maximum(needs, jnp.floor((stop - start + (ways - 1.0)) * (1.0 / ways)))
        starts.append(start)
        stops.append(stop)
    blank = jnp.full((8 - slots, tiles), float(EMPTY), f32)
    for m in range(blocks + 1):
        lines_m = [
            jnp.where(start + float(ways * m) < stop, start + float(ways * m), float(EMPTY))
            for start, stop in zip(starts, stops)
        ]
        span_ref[8 * m : 8 * m + 8, :] = jnp.concatenate(lines_m + [blank], axis=0).astype(jnp.int32)
    row = lax.broadcasted_iota(jnp.int32, (tiles, tiles), 0)
    col = lax.broadcasted_iota(jnp.int32, (tiles, tiles), 1)
    many = jnp.broadcast_to(needs, (tiles, tiles)).astype(bf16)
    done = dot((col <= row).astype(f32).astype(bf16), many, NT)
    each = dot((col == row).astype(f32).astype(bf16), many, NT)
    total = jnp.max(done, axis=0, keepdims=True)
    for k in range(item_ref.shape[1]):
        slot = lax.broadcasted_iota(jnp.int32, (1, tiles), 1).astype(f32) + float(k * tiles)
        past = done <= slot
        at = jnp.sum(jnp.where(past, 1.0, 0.0), axis=0, keepdims=True)
        began = jnp.sum(jnp.where(past, each, 0.0), axis=0, keepdims=True)
        spare = slot >= total
        item_ref[0, k : k + 1, :] = jnp.where(spare, 0.0, at).astype(jnp.int32)
        item_ref[1, k : k + 1, :] = jnp.where(spare, float(blocks), slot - began).astype(jnp.int32)
        item_ref[2, k : k + 1, :] = total.astype(jnp.int32)


def turn_vectors(v_ref, row_ref, turn_ref):
    ens, wide = v_ref.shape
    padded = ROWS + 128
    row = lax.broadcasted_iota(jnp.int32, (256, 256), 0)
    eye = (row == lax.broadcasted_iota(jnp.int32, (256, 256), 1)).astype(f32).astype(bf16)
    for h in range(wide // ROWS):
        for b in range(ROWS // 256):
            at = slice(h * ROWS + b * 256, h * ROWS + (b + 1) * 256)
            stack = jnp.concatenate(two(v_ref[:, at] * row_ref[2:3, at]), axis=0)
            begin = h * padded + b * 256
            turn_ref[begin : begin + 256, :] = dot(eye, stack, NT).astype(bf16)
        turn_ref[h * padded + ROWS : (h + 1) * padded, :] = jnp.zeros((128, 2 * ens), bf16)


def windows(work, n, slots):
    line, lane = lax.shift_right_logical(n, jnp.int32(7)), lax.bitwise_and(n, jnp.int32(127))
    tile = work["item"][0, line, lane]
    level = work["item"][1, line, lane] * 8
    return [tile] + [work["span"][level + slot, tile] for slot in range(slots)]


def gather(work, cov, where_to):
    tile, *found = where_to
    turn_ref = work["turn"]
    rhs = jnp.concatenate(
        [turn_ref[pl.ds(pl.multiple_of(w * STEP, STEP), 128), :] for w in found], axis=0
    )
    got = dot(cov, rhs)
    at = pl.ds(pl.multiple_of(tile * TILE, TILE), TILE)
    work["sum"][at, :] += got[:TILE] + got[TILE:]


def unroll_of(slots):
    return 8 if slots <= REACH else 4


def count_trips(work, unroll):
    return lax.shift_right_logical(
        work["item"][2, 0, 0] + (unroll - 1), jnp.int32(unroll.bit_length() - 1)
    )


def apply_cov(work, s_ref, keep, begin):
    slots = s_ref.shape[2] // 128
    unroll = unroll_of(slots)
    s_ref[keep : keep + unroll] = jnp.zeros((unroll,) + s_ref.shape[1:], bf16)

    def place(k):
        return jnp.where(k < keep // unroll, k * unroll, keep)

    def step(k, carry):
        before = jnp.where(k == begin, keep, place(k - 1))
        for p in range(unroll):
            gather(work, s_ref[before + p], carry[p])
        now = [windows(work, k * unroll + p, slots) for p in range(unroll)]
        after = place(k)
        for p in range(unroll):
            tile, *found = now[p]
            at = pl.ds(pl.multiple_of(tile * TILE, TILE), TILE)
            a_i = work["along_i"][at, :]
            b_i = work["across_i"][at, :]
            for d, w in enumerate(found):
                da = work["along"][pl.ds(w, 1), :] - a_i
                db = work["across"][pl.ds(w, 1), :] - b_i
                r2 = da * da + db * db
                r = r2 * lax.rsqrt(jnp.maximum(r2, 1e-30))
                u = jnp.maximum(1.0 - r, 0.0)
                u2 = u * u
                hi, lo = two((u2 * u2) * (r + 0.25))
                s_ref[after + p, 0:TILE, d * 128 : (d + 1) * 128] = hi
                s_ref[after + p, TILE : 2 * TILE, d * 128 : (d + 1) * 128] = lo
        return now

    trips = count_trips(work, unroll)
    end = jnp.where(trips > begin, trips + 1, begin)
    lax.fori_loop(begin, end, step, [windows(work, p, slots) for p in range(unroll)])


def apply_kept(work, kept_ref, ring_ref):
    slots = kept_ref.shape[2] // 128
    unroll = unroll_of(slots)
    most = KEEP // unroll

    def step(k, carry):
        for p in range(unroll):
            gather(work, kept_ref[k * unroll + p], windows(work, k * unroll + p, slots))
        return carry

    lax.fori_loop(0, jnp.minimum(count_trips(work, unroll), most), step, 0)
    apply_cov(work, ring_ref, 0, most)


def finish(sum_ref, base_ref, row_ref, v_ref, img_ref):
    ens, own = img_ref.shape
    for c in range(own // 128):
        at = slice(c * 128, (c + 1) * 128)
        turned = (sum_ref[at, :] + base_ref[at, :]).T
        img_ref[:, at] = (
            (turned[:ens] + turned[ens:]) * (row_ref[2:3, at] * 0.25) + row_ref[3:4, at] * v_ref[:, at]
        )


def one_hot(row):
    slot = lax.broadcasted_iota(jnp.int32, (256, row.shape[1]), 0).astype(f32).astype(bf16)
    same = slot == jnp.broadcast_to(row, (256, row.shape[1])).astype(bf16)
    return jnp.where(same, jnp.ones((), bf16), jnp.zeros((), bf16))


def gram(a, b):
    ahi, alo = two(a)
    bhi, blo = two(b)
    return dot(
        jnp.concatenate([ahi, ahi, alo], axis=1), jnp.concatenate([bhi, blo, bhi], axis=1), NT
    )


def square(n):
    return lax.broadcasted_iota(jnp.int32, (n, n), 0), lax.broadcasted_iota(jnp.int32, (n, n), 1)


def pack_pair(upper, lower):
    n = upper.shape[0]
    row, col = square(n)
    upper, lower = symmetric(upper), symmetric(lower)
    spare = jnp.sum(jnp.where(row == col, lower, 0.0), axis=0, keepdims=True)
    return jnp.where(col >= row, upper, lower), jnp.broadcast_to(spare, (8, n))


def unpack_pair(packed, spare):
    n = packed.shape[0]
    row, col = square(n)
    other = packed.T
    lower = jnp.where(row == col, jnp.broadcast_to(spare, (n, n)), jnp.where(col > row, other, packed))
    return jnp.where(col >= row, packed, other), lower


def start_plan(span_in, item_in, work):
    copies = [
        pltpu.make_async_copy(span_in, work["span"], work["plan_sem"].at[0]),
        pltpu.make_async_copy(item_in, work["item"], work["plan_sem"].at[1]),
    ]
    for copy in copies:
        copy.start()
    return copies


def multiply(copies, work, kept_ref=None):
    turn_vectors(work["v"], work["row"], work["turn"])
    work["sum"][...] = jnp.zeros_like(work["sum"])
    for copy in copies:
        copy.wait()
    if kept_ref is None:
        apply_cov(work, work["s"], KEEP, 0)
    else:
        apply_kept(work, kept_ref, work["ring"])


def lay_own(first_ref, last_ref, work):
    regions = first_ref.shape[1] * 2 // ROWS
    lay_grid([first_ref, last_ref], range(regions), work["row"], work["grid"])
    spread_rows(work["grid"], (work["along_i"], work["across_i"]))
    lay_tables(work["grid"], regions, (work["along"], work["across"]))


def lay_halo(before_ref, after_ref, first_ref, last_ref, work):
    regions = first_ref.shape[1] * 2 // ROWS
    offsets = list(range(-REACH, 0)) + list(range(regions, regions + REACH))
    lay_grid([first_ref, last_ref], range(regions), work["row_i"], work["grid_i"])
    lay_grid([before_ref, after_ref], offsets, work["row"], work["grid"])
    lay_tables(work["grid"], 2 * REACH, (work["along"], work["across"]))


def take_rows(chunks, row_ref):
    width = chunks[0].shape[1]
    for c, ref in enumerate(chunks):
        row_ref[:, c * width : (c + 1) * width] = ref[ref.shape[0] - 8 :, :]


def first_own_kernel(
    names, first_ref, last_ref, sum_out, span_out, item_out, along_out, across_out, along_i_out, across_i_out, s_out, *refs
):
    work = dict(zip(names, refs))
    work.update(along=along_out, across=across_out, along_i=along_i_out, across_i=across_i_out)
    work.update(sum=sum_out, s=s_out)
    ens = work["v"].shape[0]
    lead = first_ref.shape[1]
    lay_own(first_ref, last_ref, work)
    pairs = own_pairs(2 * lead // ROWS)
    plan_windows(pairs, work["row"], work["grid"], work["row"], work["grid"], span_out, item_out)
    copies = start_plan(span_out, item_out, work)
    work["v"][:, :lead] = first_ref[:ens, :]
    work["v"][:, lead:] = last_ref[:ens, :]
    multiply(copies, work)


def first_halo_kernel(
    names,
    before_ref,
    after_ref,
    first_ref,
    last_ref,
    base_ref,
    along_i_ref,
    across_i_ref,
    imga_ref,
    imgb_ref,
    gram_ref,
    span_out,
    item_out,
    along_out,
    across_out,
    s_out,
    *refs,
):
    work = dict(zip(names, refs))
    work.update(along=along_out, across=across_out, along_i=along_i_ref, across_i=across_i_ref, s=s_out)
    ens = work["v"].shape[0]
    lead = first_ref.shape[1]
    lay_halo(before_ref, after_ref, first_ref, last_ref, work)
    pairs = halo_pairs(2 * lead // ROWS)
    plan_windows(pairs, work["row"], work["grid"], work["row_i"], work["grid_i"], span_out, item_out)
    copies = start_plan(span_out, item_out, work)
    work["v"][:, :lead] = before_ref[:ens, :]
    work["v"][:, lead:] = after_ref[:ens, :]
    multiply(copies, work)
    work["v"][:, :lead] = first_ref[:ens, :]
    work["v"][:, lead:] = last_ref[:ens, :]
    img_ref = work["img"]
    finish(work["sum"], base_ref, work["row_i"], work["v"], img_ref)
    imga_ref[...] = img_ref[:, :lead]
    imgb_ref[...] = img_ref[:, lead:]
    r = work["v"][...]
    both = gram(r, jnp.concatenate([r, img_ref[...]], axis=0))
    packed, spare = pack_pair(both[:, :ens], both[:, ens:])
    half = ens // 2
    gram_ref[0:half, :] = jnp.concatenate([packed[:half], packed[half:]], axis=1)
    gram_ref[half : half + 8, :] = jnp.concatenate([spare, spare], axis=1)


def second_own_kernel(
    names,
    span_in,
    item_in,
    gram_ref,
    first_ref,
    last_ref,
    imga_ref,
    imgb_ref,
    along_ref,
    across_ref,
    along_i_ref,
    across_i_ref,
    kept_ref,
    sum_out,
    rest_out,
    step_out,
    inv_out,
    curv_out,
    *refs,
):
    work = dict(zip(names, refs))
    work.update(along=along_ref, across=across_ref, along_i=along_i_ref, across_i=across_i_ref)
    work.update(sum=sum_out, v=rest_out)
    ens = step_out.shape[0]
    lead = first_ref.shape[1]
    copies = start_plan(span_in, item_in, work)
    take_rows([first_ref, last_ref], work["row"])
    solve_first(gram_ref, step_out, inv_out, curv_out)
    step_t = step_out[...].T
    rest_out[:, :lead] = first_ref[:ens, :] - combine(step_t, imga_ref[...])
    rest_out[:, lead:] = last_ref[:ens, :] - combine(step_t, imgb_ref[...])
    multiply(copies, work, kept_ref)


def second_halo_kernel(
    names,
    span_in,
    item_in,
    step_ref,
    before_ref,
    after_ref,
    img_before_ref,
    img_after_ref,
    first_ref,
    last_ref,
    rest_ref,
    imga_ref,
    imgb_ref,
    base_ref,
    along_ref,
    across_ref,
    along_i_ref,
    across_i_ref,
    kept_ref,
    gram_ref,
    *refs,
):
    work = dict(zip(names, refs))
    work.update(along=along_ref, across=across_ref, along_i=along_i_ref, across_i=across_i_ref)
    ens = step_ref.shape[0]
    lead = before_ref.shape[1]
    copies = start_plan(span_in, item_in, work)
    take_rows([first_ref, last_ref], work["row_i"])
    take_rows([before_ref, after_ref], work["row"])
    step_t = step_ref[...].T
    work["v"][:, :lead] = before_ref[:ens, :] - combine(step_t, img_before_ref[...])
    work["v"][:, lead:] = after_ref[:ens, :] - combine(step_t, img_after_ref[...])
    multiply(copies, work, kept_ref)
    img_ref = work["img"]
    finish(work["sum"], base_ref, work["row_i"], rest_ref, img_ref)
    r = rest_ref[...]
    both = gram(r, jnp.concatenate([r, img_ref[...]], axis=0))
    mixed = gram(r, jnp.concatenate([imga_ref[...], imgb_ref[...]], axis=1))
    packed, spare = pack_pair(both[:, :ens], both[:, ens:])
    gram_ref[0:ens, :] = jnp.concatenate([packed, mixed], axis=1)
    gram_ref[ens : ens + 8, :] = jnp.concatenate([spare, spare], axis=1)


def plan_shapes(own):
    tiles = own // TILE
    most = tiles * (ROWS // 128)
    return (8 * (ROWS // 128 + 1), tiles), (3, most // 128 + 1, 128)


def plan_out(own):
    return tuple(jax.ShapeDtypeStruct(shape, jnp.int32) for shape in plan_shapes(own))


def table_shapes(own, halo):
    near = 2 * REACH if halo else own // ROWS
    slots = widest((halo_pairs if halo else own_pairs)(own // ROWS))
    table = jax.ShapeDtypeStruct((128 // STEP * near * (ROWS // 128 + 1), 128), f32)
    kept = jax.ShapeDtypeStruct((KEEP + unroll_of(slots), 2 * TILE, slots * 128), bf16)
    return (table, table), (kept,)


def scratch(ens, own, halo, again):
    regions = own // ROWS
    near = 2 * REACH if halo else regions
    slots = widest((halo_pairs if halo else own_pairs)(regions))

    def grid(count):
        return pltpu.VMEM((3, -(-(count * (ROWS // 128 + 1) + 1) // 8) * 8, 128), f32)

    spans, items = plan_shapes(own)
    shapes = {
        "span": pltpu.SMEM(spans, jnp.int32),
        "item": pltpu.SMEM(items, jnp.int32),
        "plan_sem": pltpu.SemaphoreType.DMA((2,)),
        "row": pltpu.VMEM((8, near * ROWS), f32),
        "turn": pltpu.VMEM((near * (ROWS + 128), 2 * ens), bf16),
    }
    if not again:
        shapes["grid"] = grid(near)
    if again:
        shapes["ring"] = pltpu.VMEM((unroll_of(slots), 2 * TILE, slots * 128), bf16)
    if halo:
        shapes["row_i"] = pltpu.VMEM((8, own), f32)
        shapes["grid_i"] = grid(regions)
        shapes["img"] = pltpu.VMEM((ens, own), f32)
        shapes["sum"] = pltpu.VMEM((own, 128), f32)
    if halo or not again:
        shapes["v"] = pltpu.VMEM((ens, near * ROWS), f32)
    return tuple(shapes), list(shapes.values())


def operate(kernel, name, kind, args, outs, ens, own):
    names, shapes = scratch(ens, own, *kind)
    return pl.pallas_call(
        functools.partial(kernel, names),
        out_shape=outs,
        in_specs=[vmem] * len(args),
        out_specs=(vmem,) * len(outs),
        scratch_shapes=shapes,
        compiler_params=params(),
        cost_estimate=pl.CostEstimate(flops=10**10, bytes_accessed=4 << 20, transcendentals=0),
        name=name,
    )(*args)


def first_own_call(first, last, ens, own):
    tables, kept = table_shapes(own, False)
    spread = jax.ShapeDtypeStruct((own, 128), f32)
    outs = (spread,) + plan_out(own) + tables + (spread, spread) + kept
    return operate(first_own_kernel, "first_own", (False, False), (first, last), outs, ens, own)


def first_halo_call(chunks, base, spreads, ens, own):
    tables, kept = table_shapes(own, True)
    half = jax.ShapeDtypeStruct((ens, own // 2), f32)
    outs = (half, half, jax.ShapeDtypeStruct((ens // 2 + 8, 2 * ens), f32))
    outs += plan_out(own) + tables + kept
    args = (*chunks, base, *spreads)
    return operate(first_halo_kernel, "first_halo", (True, False), args, outs, ens, own)


def second_own_call(plan, grams, first, last, imga, imgb, laid, ens, own):
    small = jax.ShapeDtypeStruct((ens, ens), f32)
    outs = (jax.ShapeDtypeStruct((own, 2 * ens), f32), jax.ShapeDtypeStruct((ens, own), f32))
    args = (*plan, grams, first, last, imga, imgb, *laid)
    return operate(second_own_kernel, "second_own", (False, True), args, outs + (small,) * 3, ens, own)


def second_halo_call(plan, step, before, after, images, first, last, rest, mine, base, laid, ens, own):
    args = (*plan, step, before, after, *images, first, last, rest, *mine, base, *laid)
    outs = (jax.ShapeDtypeStruct((ens + 8, 2 * ens), f32),)
    return operate(second_halo_kernel, "second_halo", (True, True), args, outs, ens, own)[0]


def flip(me, size):
    return size * (1 - 2 * ((me // size) % 2))


def exchange_steps(total):
    bits = total.bit_length() - 1
    steps = [[1]] if bits % 2 else []
    for k in range(bits % 2, bits, 2):
        steps.append([2**k, 2 ** (k + 1)])
    return steps


def partners_of(steps, n_col, me):
    found = []
    for amounts in steps:
        others = [me + flip(me, size) for size in amounts]
        if len(amounts) == 2:
            others.append(others[0] + flip(me, amounts[1]))
        found.append([(other // n_col, other % n_col) for other in others])
    return found


def sum_all(partners, x_ref, send, recv, sems, work):
    total = x_ref[...]
    slot = 0
    for k, group in enumerate(partners):
        if k:
            send[k] = total
        source = send.at[k] if k else x_ref
        copies = [
            send_to(source, recv.at[slot + p], sems, slot + p, other) for p, other in enumerate(group)
        ]
        for copy in copies:
            copy.start()
        if k < len(work):
            work[k]()
        for copy in copies:
            copy.wait()
        total = total + recv[slot]
        if len(group) == 3:
            total = total + (recv[slot + 1] + recv[slot + 2])
        slot += len(group)
    for piece in work[len(partners) :]:
        piece()
    return total


def local_column(owner, me, total):
    local = owner - me * COLS_DEV
    return jnp.where(local < 0, local + total * COLS_DEV, local)


def add_columns(scaled_ref, owner_ref, me, total, base, target_ref):
    own = owner_ref.shape[1]

    def one(c, carry):
        got = jnp.zeros((scaled_ref.shape[0], 256), f32)
        for g in range(own // ROWS):
            at = slice(g * ROWS, (g + 1) * ROWS)
            owner = local_column(owner_ref[:, at], me, total)
            hot = one_hot((owner - (base + c * 256)).astype(f32))
            got = got + dot(scaled_ref[:, at], hot, NT)
        ens = target_ref.shape[0]
        target_ref[:, pl.ds(pl.multiple_of(c * 256, 256), 256)] = got[:ens] + got[ens:]
        return carry

    lax.fori_loop(0, COLS_DEV // 256, one, 0)


def join_first_kernel(
    steps,
    total,
    n_col,
    x_ref,
    imga_ref,
    imgb_ref,
    ranka_ref,
    rankb_ref,
    gain_ref,
    owner_ref,
    out_ref,
    back_ref,
    scaled_ref,
    edge_ref,
    send,
    recv,
    send_sem,
    recv_sem,
):
    ens, half = imga_ref.shape
    me = lax.axis_index("reg") * n_col + lax.axis_index("col")
    partners = partners_of(steps, n_col, me)
    everyone = [other for group in partners for other in group]
    greet(everyone)
    pl.semaphore_wait(pltpu.get_barrier_semaphore(), len(everyone))

    def unsort():
        for k, (img_ref, rank_ref) in enumerate(((imga_ref, ranka_ref), (imgb_ref, rankb_ref))):

            def one(r, carry, k=k, img_ref=img_ref, rank_ref=rank_ref):
                at = pl.ds(pl.multiple_of(k * half + r * ROWS, ROWS), ROWS)
                here = pl.ds(pl.multiple_of(r * ROWS, ROWS), ROWS)
                rank = rank_ref[0:1, here]
                lhs = jnp.concatenate(two(img_ref[:, here]), axis=0)
                got = jnp.zeros((2 * ens, ROWS), f32)
                for c in range(ROWS // 256):
                    place = one_hot(rank - float(c * 256))
                    got = got + dot(lhs[:, c * 256 : (c + 1) * 256], place)
                image = got[:ens] + got[ens:]
                back_ref[:, at] = image
                scaled_ref[:, at] = jnp.concatenate(two(image * gain_ref[:, at]), axis=0)
                return carry

            lax.fori_loop(0, half // ROWS, one, 0)

    def outer():
        add_columns(scaled_ref, owner_ref, me, total, COLS_DEV, edge_ref)

    out_ref[...] = sum_all(partners, x_ref, send, recv, (send_sem, recv_sem), [unsort, outer])


def inner_columns_kernel(total, n_col, scaled_ref, owner_ref, cols_ref):
    me = lax.axis_index("reg") * n_col + lax.axis_index("col")
    add_columns(scaled_ref, owner_ref, me, total, 0, cols_ref)


def join_second_kernel(
    steps,
    total,
    n_col,
    count_ref,
    x_ref,
    innov_ref,
    gain_ref,
    owner_ref,
    out_ref,
    cols_ref,
    came_ref,
    scaled_ref,
    send,
    recv,
    send_sem,
    recv_sem,
    edge_ref,
    bulk_send_sem,
    bulk_recv_sem,
):
    own = innov_ref.shape[1]
    me, left, right = ring(total, n_col)
    partners = partners_of(steps, n_col, me)
    everyone = [other for group in partners for other in group] + [left, right]
    greet(everyone)
    pl.semaphore_wait(pltpu.get_barrier_semaphore(), len(everyone))
    edge = send_to(edge_ref, came_ref, (bulk_send_sem, bulk_recv_sem), 0, right)

    def scale():
        def one(g, carry):
            at = pl.ds(pl.multiple_of(g * ROWS, ROWS), ROWS)
            factor = gain_ref[:, at] * live_row(count_ref, g)
            scaled_ref[:, at] = jnp.concatenate(two(innov_ref[:, at] * factor), axis=0)
            return carry

        lax.fori_loop(0, own // ROWS, one, 0)

    def outer():
        add_columns(scaled_ref, owner_ref, me, total, COLS_DEV, edge_ref)

    def inner():
        edge.start()
        add_columns(scaled_ref, owner_ref, me, total, 0, cols_ref)

    out_ref[...] = sum_all(partners, x_ref, send, recv, (send_sem, recv_sem), [scale, outer, inner])
    edge.wait()


def join_scratch(steps, shape):
    slots = sum(2 ** len(amounts) - 1 for amounts in steps)
    return [
        pltpu.VMEM((len(steps),) + shape, f32),
        pltpu.VMEM((slots,) + shape, f32),
        pltpu.SemaphoreType.DMA((slots,)),
        pltpu.SemaphoreType.DMA((slots,)),
    ]


def inner_columns(scaled, owner):
    return pl.pallas_call(
        functools.partial(inner_columns_kernel, *sizes()),
        out_shape=jax.ShapeDtypeStruct((scaled.shape[0] // 2, COLS_DEV), f32),
        in_specs=[vmem] * 2,
        out_specs=vmem,
        compiler_params=params(),
        cost_estimate=pl.CostEstimate(flops=4 * 10**9, bytes_accessed=1 << 20, transcendentals=0),
        name="inner_columns",
    )(scaled, owner)


def join_first(x, imga, imgb, ranka, rankb, gain, owner):
    ens, half = imga.shape
    total, n_col = sizes()
    steps = exchange_steps(total)
    cols = jax.ShapeDtypeStruct((ens, COLS_DEV), f32)
    return pl.pallas_call(
        functools.partial(join_first_kernel, steps, total, n_col),
        out_shape=(
            jax.ShapeDtypeStruct(x.shape, f32),
            jax.ShapeDtypeStruct((ens, 2 * half), f32),
            jax.ShapeDtypeStruct((2 * ens, 2 * half), bf16),
            cols,
        ),
        in_specs=[vmem] * 7,
        out_specs=(vmem,) * 4,
        scratch_shapes=join_scratch(steps, x.shape),
        compiler_params=comm_params(1),
        name="join_first",
    )(x, imga, imgb, ranka, rankb, gain, owner)


def join_second(count, x, innov, gain, owner):
    ens, own = innov.shape
    total, n_col = sizes()
    steps = exchange_steps(total)
    cols = jax.ShapeDtypeStruct((ens, COLS_DEV), f32)
    return pl.pallas_call(
        functools.partial(join_second_kernel, steps, total, n_col),
        out_shape=(jax.ShapeDtypeStruct(x.shape, f32), cols, cols),
        in_specs=[smem] + [vmem] * 4,
        out_specs=(vmem, vmem, anywhere),
        scratch_shapes=[pltpu.VMEM((2 * ens, own), bf16)]
        + join_scratch(steps, x.shape)
        + [
            pltpu.VMEM((ens, COLS_DEV), f32),
            pltpu.SemaphoreType.DMA((1,)),
            pltpu.SemaphoreType.DMA((1,)),
        ],
        compiler_params=comm_params(2),
        name="join_second",
    )(count, x, innov, gain, owner)


def symmetric(matrix):
    return 0.5 * (matrix + matrix.T)


def mm(a, b, dims=NN):
    return lax.dot_general(a, b, dims, precision=highest, preferred_element_type=f32)


def eliminate(chains):
    ens, both = chains[0].shape
    parts = range(ens // 8)
    rows = lax.broadcasted_iota(jnp.int32, (8, both), 0)
    chains = [[m[8 * i : 8 * i + 8] for i in parts] for m in chains]

    def clear(parts_of, col, pivot, at):
        done = [x - c * pivot for x, c in zip(parts_of, col)]
        done[at // 8] = jnp.where(rows == at % 8, pivot, done[at // 8])
        return done

    for k in range(0, ens, PANEL):
        columns = [
            [[jnp.broadcast_to(x[:, k + j : k + j + 1], (8, both)) for x in m] for j in range(PANEL)]
            for m in chains
        ]
        for p in range(PANEL):
            at = k + p
            one = slice(at % 8, at % 8 + 1)
            done = []
            for m, cols in zip(chains, columns):
                col = cols[p]
                scale = 1.0 / col[at // 8][one]
                for j in range(p + 1, PANEL):
                    cols[j] = clear(cols[j], col, cols[j][at // 8][one] * scale, at)
                done.append(clear(m, col, m[at // 8][one] * scale, at))
            chains = done
    return [jnp.concatenate(m, axis=0)[:, ens:] for m in chains]


def solve_first(gram_ref, step_ref, inv_ref, curv_ref):
    ens = step_ref.shape[0]
    half = ens // 2
    packed = jnp.concatenate([gram_ref[0:half, :ens], gram_ref[0:half, ens:]], axis=0)
    norm, curv = unpack_pair(packed, gram_ref[half : half + 1, :ens])
    row, col = square(ens)
    eye = (row == col).astype(f32)
    step, inv = eliminate(
        [jnp.concatenate([curv, norm], axis=1), jnp.concatenate([norm, eye], axis=1)]
    )
    step_ref[...] = step
    inv_ref[...] = inv
    curv_ref[...] = curv


def solve_second(gram_ref, step_ref, inv_ref, curv_ref):
    ens = step_ref.shape[0]
    norm, cross = unpack_pair(gram_ref[0:ens, :ens], gram_ref[ens : ens + 1, :ens])
    mixed = gram_ref[0:ens, ens:]
    conj = mm(inv_ref[...], norm)
    coupled = mm(mixed, conj)
    quad = mm(conj, mm(curv_ref[...], conj), TN)
    curv = symmetric(cross + coupled + coupled.T + quad)
    (step,) = eliminate([jnp.concatenate([curv, norm], axis=1)])
    step0 = step_ref[...]
    keep = step0 + step + mm(conj, step)
    return keep.T, -mm(step0, step).T


def final_kernel(
    count_ref, gram_ref, step_ref, inv_ref, curv_ref, innov_ref, back_ref, rc_ref, rin_ref, ic_ref, iin_ref, w_ref, inc_ref
):
    first, second = solve_second(gram_ref, step_ref, inv_ref, curv_ref)
    for g in range(innov_ref.shape[1] // ROWS):
        at = pl.ds(g * ROWS, ROWS)
        live = live_row(count_ref, g)
        w_ref[:, at] = combine(first, innov_ref[:, at] * live) + combine(second, back_ref[:, at])
    inc_ref[...] = combine(first, rc_ref[...] + rin_ref[...]) + combine(
        second, ic_ref[...] + iin_ref[...]
    )


def final_call(count, solved, innov, back, *cols):
    ens, own = innov.shape
    return pl.pallas_call(
        final_kernel,
        out_shape=(
            jax.ShapeDtypeStruct((ens, own), f32),
            jax.ShapeDtypeStruct((ens, COLS_DEV), f32),
        ),
        in_specs=[smem] + [vmem] * 10,
        out_specs=(vmem, vmem),
        compiler_params=params(),
        name="final",
    )(count, *solved, innov, back, *cols)


def on_device(
    innovation,
    obs_along,
    obs_across,
    obs_scale,
    obs_error,
    obs_gain,
    pair_live,
    obs_count,
    col_owner,
):
    ens, own = innovation.shape
    rows = [x.reshape(1, own) for x in (obs_along, obs_across, obs_scale, obs_error)]
    gain, owner = obs_gain.reshape(1, own), col_owner.reshape(1, own)
    first, last, rank_a, rank_b = sort_call(obs_count, pair_live.T, innovation, *rows)
    after, before = shift(first, -1), shift(last, 1)
    base, *rest = first_own_call(first, last, ens, own)
    plan_own, laid_own = rest[:2], rest[2:]
    spreads = laid_own[2:4]
    chunks = [before, after, first, last]
    imga, imgb, grams, *rest = first_halo_call(chunks, base, spreads, ens, own)
    plan_halo, laid_halo = rest[:2], rest[2:4] + spreads + rest[4:]
    grams, back, scaled, edge = join_first(grams, imga, imgb, rank_a, rank_b, gain, owner)
    senda, sendb, grams = lax.optimization_barrier((imga, imgb, grams))
    img_after, img_before = shift(senda, -1), shift(sendb, 1)
    iin = shift(edge, 1)
    ic = inner_columns(scaled, owner)
    base, rest, step0, inv0, curv0 = second_own_call(plan_own, grams, first, last, imga, imgb, laid_own, ens, own)
    images = [img_before, img_after]
    grams = second_halo_call(
        plan_halo, step0, before, after, images, first, last, rest, [imga, imgb], base, laid_halo, ens, own
    )
    grams, rc, rin = join_second(obs_count, grams, innovation, gain, owner)
    solved = (grams, step0, inv0, curv0)
    return tuple(final_call(obs_count, solved, innovation, back, rc, rin, ic, iin))


def solution(mesh):
    one = P(("reg", "col"))
    in_specs = (P(None, ("reg", "col")), one, one, one, one, one, P(("reg", "col"), None), one, one)
    out_specs = (P(None, ("reg", "col")), P(None, ("reg", "col")))
    return jax.shard_map(
        on_device, mesh=mesh, in_specs=in_specs, out_specs=out_specs, check_vma=False
    )
```
